32 devices in a mesh: wide: 8 (over y, x, core), narrow: 4 (over z).
Axes of the slice: x: 2, y: 2, z: 4, core: 2. Of those that a mesh axis runs over, the one named last changes fastest.
Arguments:
- patches: bfloat16 [768, 50, 1024], P(('wide', 'narrow')), may hold values from -6 to 6
- keep_order: int32 [768, 50], P(('wide', 'narrow')), may hold values from 0 to 49, each once within a row
- keep_count: int32 [768], P(('wide', 'narrow')), may hold values from 25 to 50, as said below
- ln1_gain: bfloat16 [1024], P(('wide', 'narrow')), may hold values from 0.5 to 1.5
- ln1_bias: bfloat16 [1024], P(('wide', 'narrow')), may hold values from -1.796875 to 1.796875
- w_qkv: bfloat16 [1024, 3072], P(('wide', 'narrow')), may hold values from -0.1875 to 0.1875
- bias_q: bfloat16 [1024], P(('wide', 'narrow')), may hold values from -1.796875 to 1.796875
- bias_v: bfloat16 [1024], P(('wide', 'narrow')), may hold values from -1.796875 to 1.796875
- w_out: bfloat16 [1024, 1024], P(('wide', 'narrow')), may hold values from -0.5 to 0.5
- bias_out: bfloat16 [1024], P(('wide', 'narrow')), may hold values from -1.796875 to 1.796875
- ln2_gain: bfloat16 [1024], P(('wide', 'narrow')), may hold values from 0.5 to 1.5
- ln2_bias: bfloat16 [1024], P(('wide', 'narrow')), may hold values from -1.796875 to 1.796875
- w_up: bfloat16 [1024, 4096], P(('wide', 'narrow')), may hold values from -0.1875 to 0.1875
- bias_up: bfloat16 [4096], P(('wide', 'narrow')), may hold values from -1.796875 to 1.796875
- w_down: bfloat16 [4096, 1024], P(('wide', 'narrow')), may hold values from -0.125 to 0.125
- bias_down: bfloat16 [1024], P(('wide', 'narrow')), may hold values from -1.796875 to 1.796875
- cotangent: bfloat16 [768, 50, 1024], P(('wide', 'narrow')), may hold values from -6 to 6
Outputs:
- block_out: bfloat16 [768, 50, 1024], P(('wide', 'narrow'))
- grad_patches: bfloat16 [768, 50, 1024], P(('wide', 'narrow'))
- grad_ln1_gain: float32 [1024], P(('wide', 'narrow'))
- grad_ln1_bias: float32 [1024], P(('wide', 'narrow'))
- grad_w_qkv: float32 [1024, 3072], P(('wide', 'narrow'))
- grad_bias_q: float32 [1024], P(('wide', 'narrow'))
- grad_bias_v: float32 [1024], P(('wide', 'narrow'))
- grad_w_out: float32 [1024, 1024], P(('wide', 'narrow'))
- grad_bias_out: float32 [1024], P(('wide', 'narrow'))
- grad_ln2_gain: float32 [1024], P(('wide', 'narrow'))
- grad_ln2_bias: float32 [1024], P(('wide', 'narrow'))
- grad_w_up: float32 [1024, 4096], P(('wide', 'narrow'))
- grad_bias_up: float32 [4096], P(('wide', 'narrow'))
- grad_w_down: float32 [4096, 1024], P(('wide', 'narrow'))
- grad_bias_down: float32 [1024], P(('wide', 'narrow'))
The draws below stay inside these ranges and needn't reach their ends.
Inputs may be any that keep to these rules, and one draw needn't show every extreme that they name: `keep_order`: each row lists every slot of its image once; the first keep_count of them are the kept slots. `keep_count`: in every draw some image keeps all 50 slots and some image keeps 50 // 2.
All inputs are finite; a program needn't handle non-finite values.
Results may differ from the reference program's by a relative error of at most 0.012.
Values may be sent and summed in bfloat16 or wider, within the bound.
No kernel may reach another device: no remote copies, remote signals or barrier semaphores. Data moves between devices by JAX's collectives and lax.ppermute only.
A program may use at most 256 MiB of HBM per device.

```python
import jax
import jax.numpy as jnp
from jax import lax

D = 1024
HEADS = 16
HEAD_DIM = 64
FF = 4096
SLOTS = 50
IMG_DEV = 24
IMAGES = 768


def draw_keep_count(key, part):
    key_base, key_low, key_high = jax.random.split(key, 3)
    counts_drawn = jax.random.randint(key_base, (IMAGES,), SLOTS * 3 // 5, SLOTS + 1)
    low_place = jax.random.randint(key_low, (), 0, IMAGES)
    high_place = (low_place + 1 + jax.random.randint(key_high, (), 0, IMAGES - 1)) % IMAGES
    places = jnp.arange(IMAGES)
    counts_drawn = jnp.where(places == low_place, SLOTS // 2, counts_drawn)
    counts_drawn = jnp.where(places == high_place, SLOTS, counts_drawn)
    return counts_drawn.astype(jnp.int32)


def block_levels(rng, dims, pieces, smallest, high):
    factor_of, own = 1.0, jax.random.fold_in(rng, 6)
    for axis_at, shards_of in pieces:
        steps = jnp.exp(jax.random.uniform(jax.random.fold_in(own, axis_at), (shards_of,), jnp.float32, smallest / len(pieces), high / len(pieces)))
        factor_of = factor_of * jnp.repeat(steps, dims[axis_at] // shards_of).reshape([-1 if axis == axis_at else 1 for axis in range(len(dims))])
    return factor_of


def gaussian(rng, shape, scale, bound, shards=(), dtype=jnp.bfloat16):
    result = scale * jax.random.normal(rng, shape, jnp.float32)
    if shards:
        result = result * block_levels(rng, shape, shards, -0.22, 0.18)
    return jnp.clip(result, -bound, bound).astype(dtype)


def setup_inputs(seed: int = 0) -> dict:
    splits = jax.random.split(jax.random.key(seed), 18)
    patches = gaussian(splits[0], (IMAGES, SLOTS, D), 1.0, 6.0, ((0, 32),))
    keep_order = jax.vmap(lambda own: jax.random.permutation(own, SLOTS))(jax.random.split(splits[1], IMAGES)).reshape((IMAGES, SLOTS)).astype(jnp.int32)
    keep_count = draw_keep_count(jax.random.fold_in(splits[17], 71), 0)
    ln1_gain = jnp.clip(1.0 + 0.1 * jax.random.normal(splits[3], (D,), jnp.float32), 0.5, 1.5).astype(jnp.bfloat16)
    ln1_bias = gaussian(splits[4], (D,), 0.3, 1.796875, ((0, 32),))
    w_qkv = gaussian(splits[5], (D, 3 * D), D ** -0.5, 0.1875, ((0, 32),))
    bias_q = gaussian(splits[6], (D,), 0.3, 1.796875, ((0, 32),))
    bias_v = gaussian(splits[7], (D,), 0.3, 1.796875, ((0, 32),))
    w_out = gaussian(splits[8], (D, D), (D // 8) ** -0.5, 0.5, ((0, 32),))
    bias_out = gaussian(splits[9], (D,), 0.3, 1.796875, ((0, 32),))
    ln2_gain = jnp.clip(1.0 + 0.1 * jax.random.normal(splits[10], (D,), jnp.float32), 0.5, 1.5).astype(jnp.bfloat16)
    ln2_bias = gaussian(splits[11], (D,), 0.3, 1.796875, ((0, 32),))
    w_up = gaussian(splits[12], (D, FF), D ** -0.5, 0.1875, ((0, 32),))
    bias_up = gaussian(splits[13], (FF,), 0.3, 1.796875, ((0, 32),))
    w_down = gaussian(splits[14], (FF, D), (FF // 2) ** -0.5, 0.125, ((0, 32),))
    bias_down = gaussian(splits[15], (D,), 0.3, 1.796875, ((0, 32),))
    cotangent = gaussian(splits[16], (IMAGES, SLOTS, D), 1.0, 6.0, ((0, 32),))
    return dict(patches=patches, keep_order=keep_order, keep_count=keep_count, ln1_gain=ln1_gain, ln1_bias=ln1_bias, w_qkv=w_qkv, bias_q=bias_q, bias_v=bias_v, w_out=w_out, bias_out=bias_out, ln2_gain=ln2_gain, ln2_bias=ln2_bias, w_up=w_up, bias_up=bias_up, w_down=w_down, bias_down=bias_down, cotangent=cotangent)


@jax.custom_vjp
def low(v):
    return lax.optimization_barrier(v.astype(jnp.bfloat16)).astype(jnp.float32)

@jax.custom_vjp
def low_back(v):
    return v

def low_keep(v):
    return (low(v), None)

def low_pass(kept, grad):
    return (grad,)

def back_keep(v):
    return (v, None)

def back_low(kept, grad):
    return (low(grad),)
low.defvjp(low_keep, low_pass)
low_back.defvjp(back_keep, back_low)

def both_ways(values_in):
    return low(low_back(values_in))

def layer_norm(row_data, gain_vec, offset):
    center = row_data - lax.optimization_barrier(jnp.mean(row_data, axis=-1, keepdims=True))
    spread = lax.optimization_barrier(jnp.mean(center * center, axis=-1, keepdims=True))
    return center * lax.rsqrt(spread + 1e-06) * gain_vec + offset

def matmul(left_side, right_side):
    return jnp.dot(left_side, right_side, precision=lax.Precision.HIGHEST)

def kept_slots(keep_order, keep_count):
    slot_ids = lax.iota(jnp.int32, keep_order.shape[-1])
    listed = keep_order[:, :, None] == slot_ids[None, None, :]
    within = slot_ids[None, :] < keep_count[:, None]
    return jnp.any(jnp.logical_and(listed, within[:, :, None]), axis=1)

def forward(params, row_block, keep_mask):
    ln1_gain, ln1_bias, w_qkv, bias_q, bias_v, w_out, bias_out, ln2_gain, ln2_bias, w_up, bias_up, w_down, bias_down = params
    image_count = row_block.shape[0]
    row_count = image_count * SLOTS
    head_shape = (image_count, SLOTS, HEADS, HEAD_DIM)
    flat_rows = row_block.reshape(row_count, D)
    normed_one = low(layer_norm(flat_rows, ln1_gain, ln1_bias))
    projected = matmul(normed_one, w_qkv)
    queries = both_ways(projected[:, :D] + bias_q).reshape(head_shape)
    key_rows = both_ways(projected[:, D:2 * D]).reshape(head_shape)
    value_rows = both_ways(projected[:, 2 * D:] + bias_v).reshape(head_shape)
    scores = low_back(jnp.einsum('bqhe,bkhe->bhqk', queries, key_rows, precision=lax.Precision.HIGHEST) * HEAD_DIM ** (-0.5))
    masked = jnp.where(keep_mask[:, None, None, :], scores, -jnp.inf)
    row_peak = lax.optimization_barrier(jnp.max(masked, axis=-1, keepdims=True))
    exp_terms = jnp.exp(masked - row_peak)
    attn_prob = low(exp_terms / lax.optimization_barrier(jnp.sum(exp_terms, axis=-1, keepdims=True)))
    attn_mixed = both_ways(jnp.einsum('bhqk,bkhe->bqhe', attn_prob, value_rows, precision=lax.Precision.HIGHEST).reshape(row_count, D))
    residual = flat_rows + low_back(matmul(attn_mixed, w_out) + bias_out)
    normed_two = low(layer_norm(residual, ln2_gain, ln2_bias))
    hidden = low_back(matmul(normed_two, w_up) + bias_up)
    activated = low(jax.nn.gelu(hidden, approximate=False))
    summed_out = residual + low_back(matmul(activated, w_down) + bias_down)
    return jnp.where(keep_mask.reshape(row_count, 1), summed_out, 0.0)

def reference(patches, keep_order, keep_count, ln1_gain, ln1_bias, w_qkv, bias_q, bias_v, w_out, bias_out, ln2_gain, ln2_bias, w_up, bias_up, w_down, bias_down, cotangent):
    keep_mask = kept_slots(keep_order, keep_count)
    params = tuple((weight_arr.astype(jnp.float32) for weight_arr in (ln1_gain, ln1_bias, w_qkv, bias_q, bias_v, w_out, bias_out, ln2_gain, ln2_bias, w_up, bias_up, w_down, bias_down)))
    block_total = IMAGES // IMG_DEV
    stacked = (patches.astype(jnp.float32).reshape(block_total, IMG_DEV, SLOTS, D), keep_mask.reshape(block_total, IMG_DEV, SLOTS), cotangent.astype(jnp.float32).reshape(block_total, IMG_DEV * SLOTS, D))

    def block_step(running_sums, block_in):
        row_block, keep_block, cot_block = block_in

        def local_forward(param_set, row_set):
            return forward(param_set, row_set, keep_block)
        out_block, pull_back = jax.vjp(local_forward, params, row_block)
        grad_params, grad_rows = pull_back(cot_block)
        running_sums = jax.tree.map(lambda running, addend: running + addend, running_sums, grad_params)
        return (running_sums, (out_block.astype(jnp.bfloat16), grad_rows.astype(jnp.bfloat16)))
    start_sums = tuple((jnp.zeros_like(weight_arr) for weight_arr in params))
    sums, (out_blocks, grad_blocks) = lax.scan(block_step, start_sums, stacked)
    block_out = out_blocks.reshape(IMAGES, SLOTS, D)
    grad_patches = grad_blocks.reshape(IMAGES, SLOTS, D)
    return (block_out, grad_patches, sums[0], sums[1], sums[2], sums[3], sums[4], sums[5], sums[6], sums[7], sums[8], sums[9], sums[10], sums[11], sums[12])
```

```python
import functools

import jax
import jax.numpy as jnp
import numpy as np
from jax import lax
from jax.experimental import pallas as pl
from jax.experimental.pallas import tpu as pltpu
from jax.sharding import PartitionSpec as P

HEADS = 16
EPS = 1e-06
AXES = ("wide", "narrow")
BF = jnp.bfloat16
F32 = jnp.float32
NEG = -1e30
VMEM_LIMIT = 62 << 20
IMG_BLOCK = 8


class Layout:
    def __init__(self, mesh):
        self.wide = mesh.shape["wide"]
        self.narrow = mesh.shape["narrow"]
        self.count = self.wide * self.narrow
        self.chip_bits = (self.wide // 2).bit_length() - 1
        self.line_bits = self.narrow.bit_length() - 1

    def bit_of(self, core, level):
        return level if core == 0 else self.chip_bits - 1 - level

    def flip(self, core, piece):
        total = 0
        for level in range(self.chip_bits):
            if piece >> level & 1:
                total ^= 1 << self.bit_of(core, level)
        return total

    def swap_line(self, bit):
        return [(d, d ^ (1 << bit)) for d in range(self.count)]

    def swap_core(self):
        return [(d, d ^ self.narrow) for d in range(self.count)]

    def swap_chip(self, level):
        pairs = []
        for d in range(self.count):
            place, line = divmod(d, self.narrow)
            chip, core = divmod(place, 2)
            other = chip ^ (1 << self.bit_of(core, level))
            pairs.append((d, (other * 2 + core) * self.narrow + line))
        return pairs

    def swap_chip_bit(self, bit):
        return [(d, d ^ (2 * self.narrow << bit)) for d in range(self.count)]

    def table(self):
        place = lax.axis_index("wide")
        chip, core = place // 2, place % 2
        half = 1 << self.chip_bits
        even = np.array([self.flip(0, q) for q in range(half)], np.int32)
        odd = np.array([self.flip(1, q) for q in range(half)], np.int32)
        mine = jnp.where(core == 0, even, odd)
        other = jnp.where(core == 0, odd, even)
        return jnp.concatenate(
            [(chip ^ mine) * 2 + core, (chip ^ other) * 2 + (1 - core)]
        ).astype(jnp.int32)


def move(x, pairs):
    return lax.ppermute(x, AXES, pairs)


def in_order(bit, mine, theirs):
    return jnp.where(
        bit == 0, jnp.concatenate([mine, theirs], 0), jnp.concatenate([theirs, mine], 0)
    )


def gather_line(lay, shard):
    line = lax.axis_index("narrow")
    for b in range(lay.line_bits):
        shard = in_order((line >> b) & 1, shard, move(shard, lay.swap_line(b)))
    return shard


def gather_pieces(lay, shard):
    pieces = [gather_line(lay, shard)]
    for level in range(lay.chip_bits):
        pieces = pieces + [move(p, lay.swap_chip(level)) for p in pieces]
    return pieces + [move(p, lay.swap_core()) for p in pieces]


def gather_small(lay, shard):
    whole = gather_line(lay, shard)
    place = lax.axis_index("wide")
    whole = in_order(place & 1, whole, move(whole, lay.swap_core()))
    for b in range(lay.chip_bits):
        whole = in_order((place >> (b + 1)) & 1, whole, move(whole, lay.swap_chip_bit(b)))
    return whole


def plus(a, b, dtype=BF):
    return (a.astype(F32) + b.astype(F32)).astype(dtype)


def halve(x, bit, pairs, dtype):
    size = x.shape[0] // 2
    give = lax.dynamic_slice_in_dim(x, (1 - bit) * size, size, 0)
    keep = lax.dynamic_slice_in_dim(x, bit * size, size, 0)
    return plus(keep, move(give, pairs), dtype)


def scatter_line(lay, x, dtype):
    line = lax.axis_index("narrow")
    for b in reversed(range(lay.line_bits)):
        x = halve(x, (line >> b) & 1, lay.swap_line(b), F32 if b == 0 else dtype)
    return x


def scatter_pieces(lay, give, keep):
    x = plus(keep, move(give, lay.swap_core()))
    for level in reversed(range(lay.chip_bits)):
        size = x.shape[0] // 2
        x = plus(x[:size], move(x[size:], lay.swap_chip(level)))
    return scatter_line(lay, x, BF)


def scatter_small(lay, x):
    place = lax.axis_index("wide")
    for b in reversed(range(lay.chip_bits)):
        x = halve(x, (place >> (b + 1)) & 1, lay.swap_chip_bit(b), F32)
    x = halve(x, place & 1, lay.swap_core(), F32)
    return scatter_line(lay, x, F32)


def dot_nn(a, b):
    return jnp.dot(a, b, preferred_element_type=F32)


def dot_nt(a, b):
    return lax.dot_general(a, b, (((1,), (1,)), ((), ())), preferred_element_type=F32)


def dot_tn(a, b):
    return lax.dot_general(a, b, (((0,), (0,)), ((), ())), preferred_element_type=F32)


def normalize(r):
    center = r - jnp.mean(r, axis=-1, keepdims=True)
    spread = jnp.mean(center * center, axis=-1, keepdims=True)
    rinv = lax.rsqrt(spread + EPS)
    return center * rinv, rinv


def norm_back(up, gain, n, rinv):
    u = up * gain
    return rinv * (
        u - jnp.mean(u, axis=-1, keepdims=True) - n * jnp.mean(u * n, axis=-1, keepdims=True)
    )


def col_sum(x):
    return jnp.sum(x, axis=0, keepdims=True)


def call(body, outs, grid, in_specs, out_specs, scratch, flops, nbytes, name, trans=0):
    return pl.pallas_call(
        body,
        out_shape=outs,
        grid_spec=pltpu.PrefetchScalarGridSpec(
            num_scalar_prefetch=1,
            grid=grid,
            in_specs=in_specs,
            out_specs=out_specs,
            scratch_shapes=scratch,
        ),
        compiler_params=pltpu.CompilerParams(vmem_limit_bytes=VMEM_LIMIT),
        cost_estimate=pl.CostEstimate(flops=flops, bytes_accessed=nbytes, transcendentals=trans),
        name=name,
    )


def full(shape):
    zeros = (0,) * len(shape)
    return pl.BlockSpec(shape, lambda *_: zeros)


def anywhere(count):
    return [pl.BlockSpec(memory_space=pl.ANY)] * count


def sds(shape, dtype):
    return jax.ShapeDtypeStruct(shape, dtype)


def fill_tile(tab, pieces, tile):
    size = pieces[0].shape[0]
    for p, piece in enumerate(pieces):
        tile[pl.ds(pl.multiple_of(tab[p] * size, size), size), :] = piece[...]


def load_copies(tab, pieces, store, sem):
    size = pieces[0].shape[0]
    return [
        pltpu.make_async_copy(
            piece,
            store.at[pl.ds(pl.multiple_of(tab[p] * size, size), size)],
            sem.at[p],
        )
        for p, piece in enumerate(pieces)
    ]


def row_chunk(rows):
    for size in (240, 200, 160, 80, 48, 16):
        if rows % size == 0:
            return size
    return rows


def qkv_product(tab, x, gain, bias, bias_qkv, pieces):
    rows, width = x.shape
    cols = pieces[0].shape[1]
    tn = 512
    count = len(pieces)
    chunk = row_chunk(rows)

    def body(tab_ref, x_ref, g_ref, b_ref, c_ref, *rest):
        piece_refs, (n_ref, o_ref, tile) = rest[:count], rest[count:]

        @pl.when(pl.program_id(0) == 0)
        def _():
            @pl.loop(0, rows // chunk)
            def _(i):
                at = pl.ds(pl.multiple_of(i * chunk, chunk), chunk)
                n, _unused = normalize(x_ref[at, :].astype(F32))
                n_ref[at, :] = (n * g_ref[...] + b_ref[...]).astype(BF)

        fill_tile(tab_ref, piece_refs, tile)
        o_ref[...] = (dot_nn(n_ref[...], tile[...]) + c_ref[...]).astype(BF)

    size = pieces[0].shape[0]
    return call(
        body,
        (sds((rows, width), BF), sds((rows, cols), BF)),
        (cols // tn,),
        [full((rows, width)), full((1, width)), full((1, width))]
        + [pl.BlockSpec((1, tn), lambda j, t: (0, j))]
        + [pl.BlockSpec((size, tn), lambda j, t: (0, j))] * count,
        (full((rows, width)), pl.BlockSpec((rows, tn), lambda j, t: (0, j))),
        [pltpu.VMEM((width, tn), BF)],
        2 * rows * width * cols,
        2 * (2 * rows * width + rows * cols + width * cols),
        "qkv_product",
    )(tab, x, gain, bias, bias_qkv, *pieces)


def two_heads(x, lane):
    return jnp.concatenate([jnp.where(lane < 64, x, 0.0), jnp.where(lane < 64, 0.0, x)], 0).astype(
        BF
    )


def half_max(s, low):
    a = jnp.max(jnp.where(low, s, NEG), axis=-1, keepdims=True)
    b = jnp.max(jnp.where(low, NEG, s), axis=-1, keepdims=True)
    return jnp.where(low, a, b)


def half_sum(s, low):
    a = jnp.sum(jnp.where(low, s, 0.0), axis=-1, keepdims=True)
    b = jnp.sum(jnp.where(low, 0.0, s), axis=-1, keepdims=True)
    return jnp.where(low, a, b)


def softmax_pair(q, kk, key_bias, low, scale):
    s = dot_nt(q, kk) * scale + key_bias
    e = jnp.exp(s - half_max(s, low))
    return e / half_sum(e, low)


def attention(tab, qkv, key_bias, slots):
    rows, three = qkv.shape
    width = three // 3
    pairs = width // 128
    blk = IMG_BLOCK * slots
    pad = -(-slots // 8) * 8
    scale = float(64**-0.5)

    def body(tab_ref, q_ref, k_ref, v_ref, kb_ref, o_ref, qf, kf, vf, of):
        qf[0:blk, :] = q_ref[...].astype(F32)
        kf[0:blk, :] = k_ref[...].astype(F32)
        vf[0:blk, :] = v_ref[...].astype(F32)
        kf[blk : blk + 16, :] = jnp.zeros((16, 128), F32)
        vf[blk : blk + 16, :] = jnp.zeros((16, 128), F32)
        qf[blk : blk + 16, :] = jnp.zeros((16, 128), F32)
        lane = lax.broadcasted_iota(jnp.int32, (64, 128), 1)
        low = lax.broadcasted_iota(jnp.int32, (pad, 128), 1) < 64
        for b in range(IMG_BLOCK):
            at = slots * b
            kk = two_heads(kf[at : at + 64, :], lane)
            vv = two_heads(vf[at : at + 64, :], lane)
            q = qf[at : at + pad, :].astype(BF)
            p = softmax_pair(q, kk, kb_ref[b], low, scale)
            of[at : at + pad, :] = dot_nn(p.astype(BF), vv)
        o_ref[...] = of[0:blk, :].astype(BF)

    return call(
        body,
        sds((rows, width), BF),
        (pairs, rows // blk),
        [
            pl.BlockSpec((blk, 128), lambda h, i, t: (i, h)),
            pl.BlockSpec((blk, 128), lambda h, i, t: (i, h + pairs)),
            pl.BlockSpec((blk, 128), lambda h, i, t: (i, h + 2 * pairs)),
            pl.BlockSpec((IMG_BLOCK, 1, 128), lambda h, i, t: (i, 0, 0)),
        ],
        pl.BlockSpec((blk, 128), lambda h, i, t: (i, h)),
        [pltpu.VMEM((blk + 16, 128), F32)] * 4,
        8 * rows * 128 * width * 2,
        2 * 4 * rows * width,
        "attention",
    )(tab, qkv, qkv, qkv, key_bias)


def attention_back(tab, qkv, key_bias, grad_mixed, slots):
    rows, three = qkv.shape
    width = three // 3
    pairs = width // 128
    blk = IMG_BLOCK * slots
    pad = -(-slots // 8) * 8
    scale = float(64**-0.5)

    def body(tab_ref, q_ref, k_ref, v_ref, kb_ref, g_ref, o_ref, s_ref, qf, kf, vf, gf, *outs):
        dqf, dkf, dvf = outs
        for ref, src in ((qf, q_ref), (kf, k_ref), (vf, v_ref), (gf, g_ref)):
            ref[0:blk, :] = src[...].astype(F32)
            ref[blk : blk + 16, :] = jnp.zeros((16, 128), F32)
        lane = lax.broadcasted_iota(jnp.int32, (64, 128), 1)
        low = lax.broadcasted_iota(jnp.int32, (pad, 128), 1) < 64
        real = lax.broadcasted_iota(jnp.int32, (pad, 128), 0) < slots
        for b in range(IMG_BLOCK):
            at = slots * b
            kk = two_heads(kf[at : at + 64, :], lane)
            vv = two_heads(vf[at : at + 64, :], lane)
            q = jnp.where(real, qf[at : at + pad, :], 0.0).astype(BF)
            g = jnp.where(real, gf[at : at + pad, :], 0.0).astype(BF)
            p = softmax_pair(q, kk, kb_ref[b], low, scale)
            dp = dot_nt(g, vv)
            ds = (p * (dp - half_sum(p * dp, low))).astype(BF)
            dqf[at : at + pad, :] = dot_nn(ds, kk) * scale
            dk = dot_tn(ds, q) * scale
            dv = dot_tn(p.astype(BF), g)
            dkf[at : at + pad, :] = jnp.where(low, dk[0:pad], dk[64 : 64 + pad])
            dvf[at : at + pad, :] = jnp.where(low, dv[0:pad], dv[64 : 64 + pad])
        @pl.when(pl.program_id(1) == 0)
        def _():
            s_ref[...] = jnp.zeros_like(s_ref)

        for at, ref in enumerate((dqf, dkf, dvf)):
            rounded = ref[0:blk, :].astype(BF)
            o_ref[at] = rounded
            s_ref[at : at + 1, :] += col_sum(rounded.astype(F32))

    spec = pl.BlockSpec((blk, 128), lambda h, i, t: (i, h))
    return call(
        body,
        (sds((3, rows, width), BF), sds((8, width), F32)),
        (pairs, rows // blk),
        [
            spec,
            pl.BlockSpec((blk, 128), lambda h, i, t: (i, h + pairs)),
            pl.BlockSpec((blk, 128), lambda h, i, t: (i, h + 2 * pairs)),
            pl.BlockSpec((IMG_BLOCK, 1, 128), lambda h, i, t: (i, 0, 0)),
            spec,
        ],
        (
            pl.BlockSpec((3, blk, 128), lambda h, i, t: (0, i, h)),
            pl.BlockSpec((8, 128), lambda h, i, t: (0, h)),
        ),
        [pltpu.VMEM((blk + 16, 128), F32)] * 7,
        20 * rows * 128 * width * 2,
        2 * 7 * rows * width,
        "attention_back",
    )(tab, qkv, qkv, qkv, key_bias, grad_mixed)


def out_product(tab, mixed, x, bias_out, gain, bias, pieces, slots):
    rows, width = mixed.shape
    blk = IMG_BLOCK * slots
    count = len(pieces)

    def body(tab_ref, m_ref, x_ref, c_ref, g_ref, b_ref, *rest):
        piece_refs, (r_ref, n_ref, store, sem) = rest[:count], rest[count:]

        @pl.when(pl.program_id(0) == 0)
        def _():
            copies = load_copies(tab_ref, piece_refs, store, sem)
            for c in copies:
                c.start()
            for c in copies:
                c.wait()

        r = x_ref[...].astype(F32) + dot_nn(m_ref[...], store[...]) + c_ref[...]
        r_ref[...] = r
        n, _unused = normalize(r)
        n_ref[...] = (n * g_ref[...] + b_ref[...]).astype(BF)

    spec = pl.BlockSpec((blk, width), lambda i, t: (i, 0))
    return call(
        body,
        (sds((rows, width), F32), sds((rows, width), BF)),
        (rows // blk,),
        [spec, spec] + [full((1, width))] * 3 + anywhere(count),
        (spec, spec),
        [pltpu.VMEM((width, width), BF), pltpu.SemaphoreType.DMA((count,))],
        2 * rows * width * width,
        10 * rows * width + 2 * width * width,
        "out_product",
    )(tab, mixed, x, bias_out, gain, bias, *pieces)


def up_product(tab, n2, bias_up, pieces):
    rows, width = n2.shape
    hid = pieces[0].shape[1]
    count = len(pieces)
    tn = hid // count
    size = pieces[0].shape[0]

    def body(tab_ref, n_ref, c_ref, *rest):
        piece_refs, (a_ref, d_ref, tile) = rest[:count], rest[count:]
        fill_tile(tab_ref, piece_refs, tile)
        u = dot_nn(n_ref[...], tile[...]) + c_ref[...]
        phi = 0.5 + 0.5 * lax.erf(u * np.float32(0.5**0.5))
        a_ref[...] = (u * phi).astype(BF)
        slope = phi + u * jnp.exp(-0.5 * u * u) * np.float32((2 * np.pi) ** -0.5)
        d_ref[...] = slope.astype(BF)

    spec = pl.BlockSpec((rows, tn), lambda p, t: (0, p))
    return call(
        body,
        (sds((rows, hid), BF), sds((rows, hid), BF)),
        (count,),
        [full((rows, width)), pl.BlockSpec((1, tn), lambda p, t: (0, t[p]))]
        + [pl.BlockSpec((size, tn), lambda p, t: (0, t[p]))] * count,
        (spec, spec),
        [pltpu.VMEM((width, tn), BF)],
        2 * rows * width * hid + 30 * rows * hid,
        2 * (rows * width + 2 * rows * hid + width * hid),
        "up_product",
        2 * rows * hid,
    )(tab, n2, bias_up, *pieces)


def down_product(tab, act, residual, bias_down, keep, pieces, images, slots):
    rows, hid = act.shape
    size, width = pieces[0].shape
    blk = IMG_BLOCK * slots
    count = len(pieces)

    def body(tab_ref, a_ref, r_ref, c_ref, k_ref, *rest):
        piece_refs, (o_ref, store, sem) = rest[:count], rest[count:]

        @pl.when(pl.program_id(0) == 0)
        def _():
            copies = [
                pltpu.make_async_copy(ref, store.at[pl.ds(p * size, size)], sem.at[p])
                for p, ref in enumerate(piece_refs)
            ]
            for c in copies:
                c.start()
            for c in copies:
                c.wait()

        y = r_ref[...] + dot_nn(a_ref[...], store[...]) + c_ref[...]
        y = jnp.where(k_ref[...] > 0.0, y, 0.0)
        for b in range(IMG_BLOCK):
            o_ref[b] = y[slots * b : slots * (b + 1)].astype(BF)

    return call(
        body,
        sds((images, slots, width), BF),
        (rows // blk,),
        [
            pl.BlockSpec((blk, hid), lambda i, t: (i, 0)),
            pl.BlockSpec((blk, width), lambda i, t: (i, 0)),
            full((1, width)),
            pl.BlockSpec((blk, 1), lambda i, t: (i, 0)),
        ]
        + anywhere(count),
        pl.BlockSpec((IMG_BLOCK, slots, width), lambda i, t: (i, 0, 0)),
        [pltpu.VMEM((hid, width), BF), pltpu.SemaphoreType.DMA((count,))],
        2 * rows * width * hid,
        2 * (rows * hid + 3 * rows * width + width * hid),
        "down_product",
    )(tab, act, residual, bias_down, keep, *pieces)


def hidden_back(tab, top, slope, pieces):
    rows, width = top.shape
    hid = slope.shape[1]
    count = len(pieces)
    tn = hid // count

    def body(tab_ref, t_ref, d_ref, *rest):
        piece_refs, (o_ref, s_ref, store, sem) = rest[:count], rest[count:]
        p = pl.program_id(0)
        copies = [
            pltpu.make_async_copy(ref, store.at[at], sem.at[at])
            for at, ref in enumerate(piece_refs)
        ]

        @pl.when(p == 0)
        def _():
            for c in copies:
                c.start()

        pltpu.make_async_copy(store.at[p], store.at[p], sem.at[p]).wait()
        g = (dot_nt(t_ref[...], store[p]) * d_ref[...].astype(F32)).astype(BF)
        o_ref[...] = g
        s_ref[...] = col_sum(g.astype(F32))

    spec = pl.BlockSpec((rows, tn), lambda p, t: (0, p))
    return call(
        body,
        (sds((rows, hid), BF), sds((1, hid), F32)),
        (count,),
        [full((rows, width)), spec] + anywhere(count),
        (spec, pl.BlockSpec((1, tn), lambda p, t: (0, t[p]))),
        [pltpu.VMEM((count, tn, width), BF), pltpu.SemaphoreType.DMA((count,))],
        2 * rows * width * hid,
        2 * (rows * width + 2 * rows * hid + width * hid),
        "hidden_back",
    )(tab, top, slope, *pieces)


def up_back(tab, grad_hidden, residual, top, gain, pieces, out_pieces):
    rows, hid = grad_hidden.shape
    width = residual.shape[1]
    count = len(pieces)
    tn = hid // count
    size = pieces[0].shape[0]
    chunk = row_chunk(rows)

    def body(tab_ref, h_ref, r_ref, t_ref, g_ref, *rest):
        piece_refs, out_refs = rest[:count], rest[count : 2 * count]
        gr_ref, gb_ref, gm_ref, s_ref, tile, acc, store, sem = rest[2 * count :]
        p = pl.program_id(0)
        copies = load_copies(tab_ref, out_refs, store, sem)

        @pl.when(p == 0)
        def _():
            for c in copies:
                c.start()

        fill_tile(tab_ref, piece_refs, tile)
        part = dot_nt(h_ref[...], tile[...])

        @pl.when(p == 0)
        def _():
            acc[...] = part

        @pl.when(p > 0)
        def _():
            acc[...] += part

        @pl.when(p == count - 1)
        def _():
            for c in copies:
                c.wait()
            s_ref[...] = jnp.zeros_like(s_ref)

            @pl.loop(0, rows // chunk)
            def _(i):
                at = pl.ds(pl.multiple_of(i * chunk, chunk), chunk)
                n, rinv = normalize(r_ref[at, :])
                up = acc[at, :]
                grad = t_ref[at, :].astype(F32) + norm_back(up, g_ref[...], n, rinv)
                branch = grad.astype(BF)
                gr_ref[at, :] = grad
                gb_ref[at, :] = branch
                gm_ref[at, :] = dot_nt(branch, store[...]).astype(BF)
                s_ref[0:1, :] += col_sum(up * n)
                s_ref[1:2, :] += col_sum(up)
                s_ref[2:3, :] += col_sum(branch.astype(F32))
                s_ref[3:4, :] += col_sum(t_ref[at, :].astype(F32))

    whole = full((rows, width))
    return call(
        body,
        (
            sds((rows, width), F32),
            sds((rows, width), BF),
            sds((rows, width), BF),
            sds((8, width), F32),
        ),
        (count,),
        [pl.BlockSpec((rows, tn), lambda p, t: (0, p)), whole, whole, full((1, width))]
        + [pl.BlockSpec((size, tn), lambda p, t: (0, t[p]))] * count
        + anywhere(count),
        (whole, whole, whole, full((8, width))),
        [
            pltpu.VMEM((width, tn), BF),
            pltpu.VMEM((rows, width), F32),
            pltpu.VMEM((width, width), BF),
            pltpu.SemaphoreType.DMA((count,)),
        ],
        2 * rows * width * (hid + width),
        2 * (rows * hid + 8 * rows * width + width * hid),
        "up_back",
    )(tab, grad_hidden, residual, top, gain, *pieces, *out_pieces)


def qkv_back(tab, grads, x, grad_residual, gain, pieces, images, slots):
    _three, rows, width = grads.shape
    blk = IMG_BLOCK * slots
    count = len(pieces)

    def body(tab_ref, d_ref, x_ref, r_ref, g_ref, *rest):
        piece_refs, (o_ref, s_ref, store, sem) = rest[:count], rest[count:]

        @pl.when(pl.program_id(0) == 0)
        def _():
            copies = load_copies(tab_ref, piece_refs, store, sem)
            for c in copies:
                c.start()
            s_ref[...] = jnp.zeros_like(s_ref)
            for c in copies:
                c.wait()

        up = dot_nt(d_ref[0], store[:, 0:width])
        up += dot_nt(d_ref[1], store[:, width : 2 * width])
        up += dot_nt(d_ref[2], store[:, 2 * width :])
        n, rinv = normalize(x_ref[...].astype(F32))
        y = r_ref[...] + norm_back(up, g_ref[...], n, rinv)
        s_ref[0:1, :] += col_sum(up * n)
        s_ref[1:2, :] += col_sum(up)
        for b in range(IMG_BLOCK):
            o_ref[b] = y[slots * b : slots * (b + 1)].astype(BF)

    spec = pl.BlockSpec((blk, width), lambda i, t: (i, 0))
    return call(
        body,
        (sds((images, slots, width), BF), sds((8, width), F32)),
        (rows // blk,),
        [pl.BlockSpec((3, blk, width), lambda i, t: (0, i, 0)), spec, spec, full((1, width))]
        + anywhere(count),
        (pl.BlockSpec((IMG_BLOCK, slots, width), lambda i, t: (i, 0, 0)), full((8, width))),
        [pltpu.VMEM((width, 3 * width), BF), pltpu.SemaphoreType.DMA((count,))],
        6 * rows * width * width,
        2 * (3 * rows * width + 4 * rows * width + 3 * width * width),
        "qkv_back",
    )(tab, grads, x, grad_residual, gain, *pieces)


def weight_grad(order, x, g, pieces_of, name, places=None):
    parts, rows, width = g.shape
    count = order.shape[0]
    size = x.shape[1] // pieces_of

    def body(tab_ref, *rest):
        x_refs, (g_ref, o_ref, xs) = rest[:count], rest[count:]

        @pl.when(pl.program_id(0) == 0)
        def _():
            for p in range(count):
                xs[:, size * p : size * (p + 1)] = x_refs[p][...]

        o_ref[...] = dot_tn(xs[...], g_ref[0]).astype(BF)

    tn = width if places is None else width // places.shape[0]
    per = width // tn
    if places is None:
        table = order
        put = pl.BlockSpec((count * size, tn), lambda j, t: (0, j))
    else:
        table = jnp.concatenate([order, places])
        put = pl.BlockSpec((count * size, tn), lambda j, t: (0, t[count + j]))

    def column(p):
        return lambda j, t: (0, t[p])

    return call(
        body,
        sds((count * size, parts * width), BF),
        (parts * per,),
        [pl.BlockSpec((rows, size), column(p)) for p in range(count)]
        + [pl.BlockSpec((1, rows, tn), lambda j, t: (j // per, 0, j % per))],
        put,
        [pltpu.VMEM((rows, count * size), BF)],
        2 * rows * count * size * parts * width,
        2 * (rows * count * size + parts * rows * width + count * size * parts * width),
        name,
    )(table, *([x] * count), g)


def down_grad(order, act, top, pieces_of, name):
    rows, hid = act.shape
    width = top.shape[1]
    count = order.shape[0]
    size = hid // pieces_of

    def body(tab_ref, a_ref, t_ref, o_ref):
        o_ref[...] = dot_tn(a_ref[...], t_ref[...]).astype(BF)

    return call(
        body,
        sds((count * size, width), BF),
        (count,),
        [pl.BlockSpec((rows, size), lambda p, t: (0, t[p])), full((rows, width))],
        pl.BlockSpec((size, width), lambda p, t: (p, 0)),
        [],
        2 * rows * count * size * width,
        2 * (rows * count * size + rows * width + count * size * width),
        name,
    )(order, act, top)


def kept_slots(keep_order, keep_count):
    slot_ids = lax.iota(jnp.int32, keep_order.shape[-1])
    listed = keep_order[:, :, None] == slot_ids[None, None, :]
    within = slot_ids[None, :] < keep_count[:, None]
    return jnp.any(jnp.logical_and(listed, within[:, :, None]), axis=1)


def local(lay, *args):
    (
        patches,
        keep_order,
        keep_count,
        ln1_gain,
        ln1_bias,
        w_qkv,
        bias_q,
        bias_v,
        w_out,
        bias_out,
        ln2_gain,
        ln2_bias,
        w_up,
        bias_up,
        w_down,
        bias_down,
        cotangent,
    ) = args
    images, slots, width = patches.shape
    rows = images * slots
    ndev = lay.count
    own = width // ndev
    own_up = bias_up.shape[0]
    hid = own_up * ndev

    tab = lay.table()
    groups = lay.wide
    half = groups // 2

    small = jnp.concatenate(
        [ln1_gain, ln1_bias, bias_q, bias_v, bias_out, ln2_gain, ln2_bias, bias_down, bias_up]
    )[None, :]
    vec = gather_small(lay, small).astype(F32)
    eight = vec[:, : 8 * own].reshape(ndev, 8, own).transpose(1, 0, 2).reshape(8, 1, width)
    gain_one, offset_one, vec_q, vec_v, vec_out, gain_two, offset_two, vec_down = eight
    vec_up = vec[:, 8 * own :].reshape(1, hid)

    qkv_pieces = gather_pieces(lay, w_qkv)
    out_pieces = gather_pieces(lay, w_out)
    up_pieces = gather_pieces(lay, w_up)
    down_pieces = gather_pieces(lay, w_down)

    keep_mask = kept_slots(keep_order, keep_count)
    keep_rows = keep_mask.reshape(rows, 1)
    keep_f = keep_rows.astype(F32)
    pad_keys = jnp.pad(jnp.where(keep_mask, 0.0, NEG), ((0, 0), (0, 64 - slots)), constant_values=NEG)
    key_bias = jnp.concatenate([pad_keys, pad_keys], 1).reshape(images, 1, 128)
    x = patches.reshape(rows, width)
    top = jnp.where(keep_rows, cotangent.reshape(rows, width), jnp.zeros((), BF))

    vec_qkv = jnp.concatenate([vec_q, jnp.zeros_like(vec_q), vec_v], axis=1)
    normed_one, qkv = qkv_product(tab, x, gain_one, offset_one, vec_qkv, qkv_pieces)
    mixed = attention(tab, qkv, key_bias, slots)
    residual, normed_two = out_product(
        tab, mixed, x, vec_out, gain_two, offset_two, out_pieces, slots
    )
    act, slope = up_product(tab, normed_two, vec_up, up_pieces)
    block_out = down_product(
        tab, act, residual, vec_down, keep_f, down_pieces, images, slots
    )

    straight = jnp.arange(groups, dtype=jnp.int32)
    give_down = down_grad(straight[half:], act, top, groups, "down_grad_give")
    keep_down = down_grad(straight[:half], act, top, groups, "down_grad_keep")
    grad_w_down = scatter_pieces(lay, give_down, keep_down)

    grad_hidden, sum_up = hidden_back(tab, top, slope, down_pieces)

    size = width // groups
    if size % 128 == 0:
        order = tab

        def placed(a):
            return a
    else:
        order = straight

        def placed(a):
            return a.reshape(rows, groups, size)[:, tab].reshape(rows, width)

    def pair(a, g, name, places=None):
        a = placed(a)
        if size % 128 == 0:
            return (
                weight_grad(order[half:], a, g, groups, name + "_give", places),
                weight_grad(order[:half], a, g, groups, name + "_keep", places),
            )
        two = straight[:2]
        return (
            weight_grad(two[1:], a, g, 2, name + "_give", places),
            weight_grad(two[:1], a, g, 2, name + "_keep", places),
        )

    grad_w_up = scatter_pieces(lay, *pair(normed_two, grad_hidden[None], "up_grad", tab))
    grad_residual, branch, grad_mixed, sums_two = up_back(
        tab, grad_hidden, residual, top, gain_two, up_pieces, out_pieces
    )
    grad_w_out = scatter_pieces(lay, *pair(mixed, branch[None], "out_grad"))
    grads, sums_att = attention_back(tab, qkv, key_bias, grad_mixed, slots)
    grad_w_qkv = scatter_pieces(lay, *pair(normed_one, grads, "qkv_grad"))
    grad_patches, sums_one = qkv_back(
        tab, grads, x, grad_residual, gain_one, qkv_pieces, images, slots
    )

    eight_sums = jnp.stack(
        [
            sums_one[0],
            sums_one[1],
            sums_att[0],
            sums_att[2],
            sums_two[2],
            sums_two[0],
            sums_two[1],
            sums_two[3],
        ]
    )
    packed = jnp.concatenate(
        [
            eight_sums.reshape(8, ndev, own).transpose(1, 0, 2).reshape(ndev, 8 * own),
            sum_up.reshape(ndev, own_up),
        ],
        axis=1,
    )
    mine = scatter_small(lay, packed)[0]
    vecs = [mine[own * i : own * (i + 1)] for i in range(8)]
    return (
        block_out,
        grad_patches,
        vecs[0],
        vecs[1],
        grad_w_qkv,
        vecs[2],
        vecs[3],
        grad_w_out,
        vecs[4],
        vecs[5],
        vecs[6],
        grad_w_up,
        mine[8 * own :],
        grad_w_down,
        vecs[7],
    )


def solution(mesh):
    both = P(AXES)
    mat = P(AXES, None)
    cube = P(AXES, None, None)
    in_specs = (
        cube, mat, both, both, both, mat, both, both, mat, both, both, both, mat, both, mat, both,
        cube,
    )
    out_specs = (
        cube, cube, both, both, mat, both, both, mat, both, both, both, mat, both, mat, both,
    )
    return jax.shard_map(
        functools.partial(local, Layout(mesh)),
        mesh=mesh,
        in_specs=in_specs,
        out_specs=out_specs,
        check_vma=False,
    )
```

```python
import functools

import jax
import jax.numpy as jnp
import numpy as np
from jax import lax
from jax.experimental import pallas as pl
from jax.experimental.pallas import tpu as pltpu
from jax.sharding import PartitionSpec as P

HEADS = 16
EPS = 1e-06
AXES = ("wide", "narrow")
BF = jnp.bfloat16
F32 = jnp.float32
NEG = -1e30
VMEM_LIMIT = 62 << 20
IMG_BLOCK = 8


class Layout:
    def __init__(self, mesh):
        self.wide = mesh.shape["wide"]
        self.narrow = mesh.shape["narrow"]
        self.count = self.wide * self.narrow
        self.chip_bits = (self.wide // 2).bit_length() - 1
        self.line_bits = self.narrow.bit_length() - 1

    def bit_of(self, core, level):
        return level if core == 0 else self.chip_bits - 1 - level

    def flip(self, core, piece):
        total = 0
        for level in range(self.chip_bits):
            if piece >> level & 1:
                total ^= 1 << self.bit_of(core, level)
        return total

    def swap_line(self, bit):
        return [(d, d ^ (1 << bit)) for d in range(self.count)]

    def swap_core(self):
        return [(d, d ^ self.narrow) for d in range(self.count)]

    def swap_chip(self, level):
        pairs = []
        for d in range(self.count):
            place, line = divmod(d, self.narrow)
            chip, core = divmod(place, 2)
            other = chip ^ (1 << self.bit_of(core, level))
            pairs.append((d, (other * 2 + core) * self.narrow + line))
        return pairs

    def swap_chip_bit(self, bit):
        return [(d, d ^ (2 * self.narrow << bit)) for d in range(self.count)]

    def table(self):
        place = lax.axis_index("wide")
        chip, core = place // 2, place % 2
        half = 1 << self.chip_bits
        even = np.array([self.flip(0, q) for q in range(half)], np.int32)
        odd = np.array([self.flip(1, q) for q in range(half)], np.int32)
        mine = jnp.where(core == 0, even, odd)
        other = jnp.where(core == 0, odd, even)
        return jnp.concatenate(
            [(chip ^ mine) * 2 + core, (chip ^ other) * 2 + (1 - core)]
        ).astype(jnp.int32)


def move(x, pairs):
    return lax.ppermute(x, AXES, pairs)


def in_order(bit, mine, theirs):
    return jnp.where(
        bit == 0, jnp.concatenate([mine, theirs], 0), jnp.concatenate([theirs, mine], 0)
    )


def plus(a, b, dtype=BF):
    return (a.astype(F32) + b.astype(F32)).astype(dtype)


def gather_steps(lay, x):
    line = lax.axis_index("narrow")
    for b in range(lay.line_bits):
        (got,) = yield [(x, lay.swap_line(b))]
        x = in_order((line >> b) & 1, x, got)
    parts = [x]
    for level in range(lay.chip_bits):
        x = parts[0] if len(parts) == 1 else jnp.concatenate(parts, 0)
        (got,) = yield [(x, lay.swap_chip(level))]
        parts = [x, got]
    more = yield [(p, lay.swap_core()) for p in parts]
    return parts + list(more)


def gather_small_steps(lay, x):
    line, place = lax.axis_index("narrow"), lax.axis_index("wide")
    for b in range(lay.line_bits):
        (got,) = yield [(x, lay.swap_line(b))]
        x = in_order((line >> b) & 1, x, got)
    (got,) = yield [(x, lay.swap_core())]
    x = in_order(place & 1, x, got)
    for b in range(lay.chip_bits):
        (got,) = yield [(x, lay.swap_chip_bit(b))]
        x = in_order((place >> (b + 1)) & 1, x, got)
    return x


def halving(x, bit, pairs, dtype):
    size = x.shape[0] // 2
    give = lax.dynamic_slice_in_dim(x, (1 - bit) * size, size, 0)
    (got,) = yield [(give, pairs)]
    keep = lax.dynamic_slice_in_dim(x, bit * size, size, 0)
    return plus(keep, got, dtype)


def scatter_line_steps(lay, x, dtype):
    line = lax.axis_index("narrow")
    for b in reversed(range(lay.line_bits)):
        x = yield from halving(x, (line >> b) & 1, lay.swap_line(b), F32 if b == 0 else dtype)
    return x


def scatter_steps(lay, give, keep):
    (got,) = yield [(give, lay.swap_core())]
    x = plus(keep[0], got)
    for level in reversed(range(lay.chip_bits)):
        size = x.shape[0] // 2
        (got,) = yield [(x[size:], lay.swap_chip(level))]
        x = plus(x[:size], got)
    return (yield from scatter_line_steps(lay, x, BF))


def scatter_small_steps(lay, x):
    place = lax.axis_index("wide")
    for b in reversed(range(lay.chip_bits)):
        x = yield from halving(x, (place >> (b + 1)) & 1, lay.swap_chip_bit(b), F32)
    x = yield from halving(x, place & 1, lay.swap_core(), F32)
    return (yield from scatter_line_steps(lay, x, F32))


class Chain:
    def __init__(self, steps):
        self.steps = steps
        self.want = next(steps)
        self.flying = None
        self.result = None

    def take(self, got):
        self.flying = None
        try:
            self.want = self.steps.send(got)
        except StopIteration as end:
            self.want, self.result = None, end.value


class Clock:
    def __init__(self, tab):
        self.tab = tab
        self.chains = []

    def begin(self, *chains):
        for c in chains:
            if c.want is None or c.flying is not None:
                continue
            operands, self.tab = lax.optimization_barrier(([w[0] for w in c.want], self.tab))
            c.flying = [move(x, w[1]) for x, w in zip(operands, c.want)]

    def tick(self, compute=None, start=(), finish=None):
        self.begin(*start)
        out = compute(self.tab) if compute is not None else ()
        done = [c for c in (start if finish is None else finish) if c.flying is not None]
        self.tab, got, out = lax.optimization_barrier((self.tab, [c.flying for c in done], out))
        for c, g in zip(done, got):
            c.take(g)
        return out

    def drain(self, *chains):
        while any(c.want is not None for c in chains):
            self.tick(None, chains)


def dot_nn(a, b):
    return jnp.dot(a, b, preferred_element_type=F32)


def dot_nt(a, b):
    return lax.dot_general(a, b, (((1,), (1,)), ((), ())), preferred_element_type=F32)


def dot_tn(a, b):
    return lax.dot_general(a, b, (((0,), (0,)), ((), ())), preferred_element_type=F32)


def normalize(r):
    center = r - jnp.mean(r, axis=-1, keepdims=True)
    spread = jnp.mean(center * center, axis=-1, keepdims=True)
    rinv = lax.rsqrt(spread + EPS)
    return center * rinv, rinv


def norm_back(up, gain, n, rinv):
    u = up * gain
    return rinv * (
        u - jnp.mean(u, axis=-1, keepdims=True) - n * jnp.mean(u * n, axis=-1, keepdims=True)
    )


def col_sum(x):
    return jnp.sum(x, axis=0, keepdims=True)


def call(body, outs, grid, in_specs, out_specs, scratch, flops, nbytes, name, trans=0, aliases={}):
    return pl.pallas_call(
        body,
        out_shape=outs,
        grid_spec=pltpu.PrefetchScalarGridSpec(
            num_scalar_prefetch=1,
            grid=grid,
            in_specs=in_specs,
            out_specs=out_specs,
            scratch_shapes=scratch,
        ),
        compiler_params=pltpu.CompilerParams(vmem_limit_bytes=VMEM_LIMIT),
        cost_estimate=pl.CostEstimate(flops=flops, bytes_accessed=nbytes, transcendentals=trans),
        name=name,
        input_output_aliases=aliases,
    )


def full(shape):
    zeros = (0,) * len(shape)
    return pl.BlockSpec(shape, lambda *_: zeros)


def anywhere(count):
    return [pl.BlockSpec(memory_space=pl.ANY)] * count


def sds(shape, dtype):
    return jax.ShapeDtypeStruct(shape, dtype)


def fill_tile(tab, pieces, tile, size):
    per = pieces[0].shape[0] // size
    for a, piece in enumerate(pieces):
        for i in range(per):
            at = pl.multiple_of(tab[a * per + i] * size, size)
            tile[pl.ds(at, size), :] = piece[i * size : (i + 1) * size, :]


def load_copies(tab, pieces, store, sem, size):
    per = pieces[0].shape[0] // size
    copies = []
    for a, piece in enumerate(pieces):
        for i in range(per):
            at = pl.multiple_of(tab[a * per + i] * size, size)
            copies.append(
                pltpu.make_async_copy(
                    piece.at[pl.ds(i * size, size)],
                    store.at[pl.ds(at, size)],
                    sem.at[a * per + i],
                )
            )
    return copies


def row_chunk(rows):
    for size in (240, 200, 160, 80, 48, 16):
        if rows % size == 0:
            return size
    return rows


def qkv_product(tab, x, gain, bias, bias_qkv, pieces):
    rows, width = x.shape
    cols = pieces[0].shape[1]
    tn = 512
    count = len(pieces)
    chunk = row_chunk(rows)

    def body(tab_ref, x_ref, g_ref, b_ref, c_ref, *rest):
        piece_refs, (n_ref, o_ref, tile) = rest[:count], rest[count:]

        @pl.when(pl.program_id(0) == 0)
        def _():
            @pl.loop(0, rows // chunk)
            def _(i):
                at = pl.ds(pl.multiple_of(i * chunk, chunk), chunk)
                n, _unused = normalize(x_ref[at, :].astype(F32))
                n_ref[at, :] = (n * g_ref[...] + b_ref[...]).astype(BF)

        fill_tile(tab_ref, piece_refs, tile, width // tab.shape[0])
        o_ref[...] = (dot_nn(n_ref[...], tile[...]) + c_ref[...]).astype(BF)

    size = pieces[0].shape[0]
    return call(
        body,
        (sds((rows, width), BF), sds((rows, cols), BF)),
        (cols // tn,),
        [full((rows, width)), full((1, width)), full((1, width))]
        + [pl.BlockSpec((1, tn), lambda j, t: (0, j))]
        + [pl.BlockSpec((size, tn), lambda j, t: (0, j))] * count,
        (full((rows, width)), pl.BlockSpec((rows, tn), lambda j, t: (0, j))),
        [pltpu.VMEM((width, tn), BF)],
        2 * rows * width * cols,
        2 * (2 * rows * width + rows * cols + width * cols),
        "qkv_product",
    )(tab, x, gain, bias, bias_qkv, *pieces)


def two_heads(x, lane):
    return jnp.concatenate([jnp.where(lane < 64, x, 0.0), jnp.where(lane < 64, 0.0, x)], 0).astype(
        BF
    )


def half_max(s, low):
    a = jnp.max(jnp.where(low, s, NEG), axis=-1, keepdims=True)
    b = jnp.max(jnp.where(low, NEG, s), axis=-1, keepdims=True)
    return jnp.where(low, a, b)


def half_sum(s, ones):
    high = s.astype(BF)
    rest = (s - high.astype(F32)).astype(BF)
    return dot_nn(high, ones) + dot_nn(rest, ones)


def softmax_pair(s, low, ones):
    e = jnp.exp(s - half_max(s, low))
    return e / half_sum(e, ones)


def head_ones():
    row = lax.broadcasted_iota(jnp.int32, (128, 128), 0) < 64
    col = lax.broadcasted_iota(jnp.int32, (128, 128), 1) < 64
    return jnp.where(row == col, 1.0, 0.0).astype(BF)


def attention(tab, qkv, key_bias, slots):
    rows, three = qkv.shape
    width = three // 3
    pairs = width // 128
    blk = IMG_BLOCK * slots
    pad = -(-slots // 8) * 8
    scale = float(64**-0.5)

    def body(tab_ref, q_ref, k_ref, v_ref, kb_ref, o_ref, qf, kf, vf, of, sf):
        for ref, src in ((qf, q_ref), (kf, k_ref), (vf, v_ref)):
            ref[0:blk, :] = src[...].astype(F32)
            ref[blk : blk + 16, :] = jnp.zeros((16, 128), F32)
        lane = lax.broadcasted_iota(jnp.int32, (64, 128), 1)
        low = lax.broadcasted_iota(jnp.int32, (pad, 128), 1) < 64
        ones = head_ones()
        for b in range(IMG_BLOCK):
            at = slots * b
            kk = two_heads(kf[at : at + 64, :], lane)
            q = qf[at : at + pad, :].astype(BF)
            sf[pad * b : pad * (b + 1), :] = dot_nt(q, kk) * scale + kb_ref[b]
        low = lax.broadcasted_iota(jnp.int32, (pad * IMG_BLOCK, 128), 1) < 64
        p = softmax_pair(sf[...], low, ones)
        outs = []
        for b in range(IMG_BLOCK):
            at = slots * b
            vv = two_heads(vf[at : at + 64, :], lane)
            outs.append(dot_nn(p[pad * b : pad * (b + 1)].astype(BF), vv))
        for b in range(IMG_BLOCK):
            at = slots * b
            of[at : at + pad, :] = outs[b]
        o_ref[...] = of[0:blk, :].astype(BF)

    return call(
        body,
        sds((rows, width), BF),
        (pairs, rows // blk),
        [
            pl.BlockSpec((blk, 128), lambda h, i, t: (i, h)),
            pl.BlockSpec((blk, 128), lambda h, i, t: (i, h + pairs)),
            pl.BlockSpec((blk, 128), lambda h, i, t: (i, h + 2 * pairs)),
            pl.BlockSpec((IMG_BLOCK, 1, 128), lambda h, i, t: (i, 0, 0)),
        ],
        pl.BlockSpec((blk, 128), lambda h, i, t: (i, h)),
        [pltpu.VMEM((blk + 16, 128), F32)] * 4 + [pltpu.VMEM((pad * IMG_BLOCK, 128), F32)],
        8 * rows * 128 * width * 2,
        2 * 4 * rows * width,
        "attention",
    )(tab, qkv, qkv, qkv, key_bias)


def attention_back(tab, qkv, key_bias, grad_mixed, slots):
    rows, three = qkv.shape
    width = three // 3
    pairs = width // 128
    blk = IMG_BLOCK * slots
    pad = -(-slots // 8) * 8
    tall = pad * IMG_BLOCK
    scale = float(64**-0.5)

    def body(tab_ref, q_ref, k_ref, v_ref, kb_ref, g_ref, o_ref, s_ref, qf, kf, vf, gf, *outs):
        dqf, dkf, dvf, sf, pf = outs
        for ref, src in ((qf, q_ref), (kf, k_ref), (vf, v_ref), (gf, g_ref)):
            ref[0:blk, :] = src[...].astype(F32)
            ref[blk : blk + 16, :] = jnp.zeros((16, 128), F32)
        lane = lax.broadcasted_iota(jnp.int32, (64, 128), 1)
        low = lax.broadcasted_iota(jnp.int32, (pad, 128), 1) < 64
        real = lax.broadcasted_iota(jnp.int32, (pad, 128), 0) < slots
        ones = head_ones()
        kks, qs, gs = [], [], []
        for b in range(IMG_BLOCK):
            at = slots * b
            kks.append(two_heads(kf[at : at + 64, :], lane))
            vv = two_heads(vf[at : at + 64, :], lane)
            qs.append(jnp.where(real, qf[at : at + pad, :], 0.0).astype(BF))
            gs.append(jnp.where(real, gf[at : at + pad, :], 0.0).astype(BF))
            sf[pad * b : pad * (b + 1), :] = dot_nt(qs[b], kks[b]) * scale + kb_ref[b]
            pf[pad * b : pad * (b + 1), :] = dot_nt(gs[b], vv)
        p = softmax_pair(sf[...], lax.broadcasted_iota(jnp.int32, (tall, 128), 1) < 64, ones)
        dp = pf[...]
        ds = p * (dp - half_sum(p * dp, ones))
        res = []
        for b in range(IMG_BLOCK):
            d = ds[pad * b : pad * (b + 1)].astype(BF)
            w = p[pad * b : pad * (b + 1)].astype(BF)
            res.append((dot_nn(d, kks[b]), dot_tn(d, qs[b]), dot_tn(w, gs[b])))
        for b in range(IMG_BLOCK):
            at = slots * b
            dq, dk, dv = res[b]
            dqf[at : at + pad, :] = dq * scale
            dkf[at : at + pad, :] = jnp.where(low, dk[0:pad], dk[64 : 64 + pad]) * scale
            dvf[at : at + pad, :] = jnp.where(low, dv[0:pad], dv[64 : 64 + pad])

        @pl.when(pl.program_id(1) == 0)
        def _():
            s_ref[...] = jnp.zeros_like(s_ref)

        for at, ref in enumerate((dqf, dkf, dvf)):
            rounded = ref[0:blk, :].astype(BF)
            o_ref[at] = rounded
            if at != 1:
                s_ref[at : at + 1, :] += col_sum(rounded.astype(F32))

    spec = pl.BlockSpec((blk, 128), lambda h, i, t: (i, h))
    return call(
        body,
        (sds((3, rows, width), BF), sds((8, width), F32)),
        (pairs, rows // blk),
        [
            spec,
            pl.BlockSpec((blk, 128), lambda h, i, t: (i, h + pairs)),
            pl.BlockSpec((blk, 128), lambda h, i, t: (i, h + 2 * pairs)),
            pl.BlockSpec((IMG_BLOCK, 1, 128), lambda h, i, t: (i, 0, 0)),
            spec,
        ],
        (
            pl.BlockSpec((3, blk, 128), lambda h, i, t: (0, i, h)),
            pl.BlockSpec((8, 128), lambda h, i, t: (0, h)),
        ),
        [pltpu.VMEM((blk + 16, 128), F32)] * 7 + [pltpu.VMEM((tall, 128), F32)] * 2,
        20 * rows * 128 * width * 2,
        2 * 7 * rows * width,
        "attention_back",
    )(tab, qkv, qkv, qkv, key_bias, grad_mixed)


def out_product(tab, mixed, x, bias_out, gain, bias, pieces, slots):
    rows, width = mixed.shape
    blk = IMG_BLOCK * slots
    count = len(pieces)

    def body(tab_ref, m_ref, x_ref, c_ref, g_ref, b_ref, *rest):
        piece_refs, (r_ref, n_ref, store, sem) = rest[:count], rest[count:]

        @pl.when(pl.program_id(0) == 0)
        def _():
            copies = load_copies(tab_ref, piece_refs, store, sem, width // tab.shape[0])
            for c in copies:
                c.start()
            for c in copies:
                c.wait()

        r = x_ref[...].astype(F32) + dot_nn(m_ref[...], store[...]) + c_ref[...]
        r_ref[...] = r
        n, _unused = normalize(r)
        n_ref[...] = (n * g_ref[...] + b_ref[...]).astype(BF)

    spec = pl.BlockSpec((blk, width), lambda i, t: (i, 0))
    return call(
        body,
        (sds((rows, width), F32), sds((rows, width), BF)),
        (rows // blk,),
        [spec, spec] + [full((1, width))] * 3 + anywhere(count),
        (spec, spec),
        [pltpu.VMEM((width, width), BF), pltpu.SemaphoreType.DMA((tab.shape[0],))],
        2 * rows * width * width,
        10 * rows * width + 2 * width * width,
        "out_product",
    )(tab, mixed, x, bias_out, gain, bias, *pieces)


def up_product(tab, n2, bias_up, pieces):
    rows, width = n2.shape
    hid = pieces[0].shape[1]
    count = len(pieces)
    groups = tab.shape[0]
    tn = hid // groups
    size = pieces[0].shape[0]

    def body(tab_ref, n_ref, c_ref, *rest):
        piece_refs, (a_ref, d_ref, tile) = rest[:count], rest[count:]
        fill_tile(tab_ref, piece_refs, tile, width // groups)
        u = dot_nn(n_ref[...], tile[...]) + c_ref[...]
        phi = 0.5 + 0.5 * lax.erf(u * np.float32(0.5**0.5))
        a_ref[...] = (u * phi).astype(BF)
        slope = phi + u * jnp.exp(-0.5 * u * u) * np.float32((2 * np.pi) ** -0.5)
        d_ref[...] = slope.astype(BF)

    spec = pl.BlockSpec((rows, tn), lambda p, t: (0, p))
    return call(
        body,
        (sds((rows, hid), BF), sds((rows, hid), BF)),
        (groups,),
        [full((rows, width)), pl.BlockSpec((1, tn), lambda p, t: (0, t[p]))]
        + [pl.BlockSpec((size, tn), lambda p, t: (0, t[p]))] * count,
        (spec, spec),
        [pltpu.VMEM((width, tn), BF)],
        2 * rows * width * hid + 30 * rows * hid,
        2 * (rows * width + 2 * rows * hid + width * hid),
        "up_product",
        2 * rows * hid,
    )(tab, n2, bias_up, *pieces)


def down_product(tab, act, residual, bias_down, keep, pieces, shape, first, last, before=None):
    images, slots, width = shape
    rows, hid = act.shape
    blk = IMG_BLOCK * slots
    count = len(pieces)
    size = pieces[0].shape[0]

    def body(tab_ref, a_ref, r_ref, c_ref, k_ref, *rest):
        piece_refs, (o_ref, store, sem) = rest[:count], rest[-3:]

        @pl.when(pl.program_id(0) == 0)
        def _():
            copies = [
                pltpu.make_async_copy(ref, store.at[pl.ds(p * size, size)], sem.at[p])
                for p, ref in enumerate(piece_refs)
            ]
            for c in copies:
                c.start()
            for c in copies:
                c.wait()

        y = r_ref[...] + dot_nn(a_ref[...], store[...]) + c_ref[...]
        y = jnp.where(k_ref[...] > 0.0, y, 0.0)
        for b in range(IMG_BLOCK):
            o_ref[b] = y[slots * b : slots * (b + 1)].astype(BF)

    share = blk * (last - first)
    more = [] if before is None else [before]
    return call(
        body,
        sds((images, slots, width), BF),
        (last - first,),
        [
            pl.BlockSpec((blk, hid), lambda i, t: (i + first, 0)),
            pl.BlockSpec((blk, width), lambda i, t: (i + first, 0)),
            full((1, width)),
            pl.BlockSpec((blk, 1), lambda i, t: (i + first, 0)),
        ]
        + anywhere(count + len(more)),
        pl.BlockSpec((IMG_BLOCK, slots, width), lambda i, t: (i + first, 0, 0)),
        [pltpu.VMEM((hid, width), BF), pltpu.SemaphoreType.DMA((count,))],
        2 * share * width * hid,
        2 * (share * hid + 3 * share * width + width * hid),
        "down_product",
        aliases={} if before is None else {5 + count: 0},
    )(tab, act, residual, bias_down, keep, *pieces, *more)


def hidden_back(tab, top, slope, pieces):
    rows, width = top.shape
    hid = slope.shape[1]
    count = len(pieces)
    groups = tab.shape[0]
    tn = hid // groups
    per = groups // count

    def body(tab_ref, t_ref, d_ref, *rest):
        piece_refs, (o_ref, s_ref, store, sem) = rest[:count], rest[count:]
        p = pl.program_id(0)
        copies = [
            pltpu.make_async_copy(
                piece_refs[g // per].at[pl.ds(g % per * tn, tn)], store.at[g], sem.at[g]
            )
            for g in range(groups)
        ]

        @pl.when(p == 0)
        def _():
            for c in copies:
                c.start()

        pltpu.make_async_copy(store.at[p], store.at[p], sem.at[p]).wait()
        g = (dot_nt(t_ref[...], store[p]) * d_ref[...].astype(F32)).astype(BF)
        o_ref[...] = g
        s_ref[...] = col_sum(g.astype(F32))

    spec = pl.BlockSpec((rows, tn), lambda p, t: (0, p))
    return call(
        body,
        (sds((rows, hid), BF), sds((1, hid), F32)),
        (groups,),
        [full((rows, width)), spec] + anywhere(count),
        (spec, pl.BlockSpec((1, tn), lambda p, t: (0, t[p]))),
        [pltpu.VMEM((groups, tn, width), BF), pltpu.SemaphoreType.DMA((groups,))],
        2 * rows * width * hid,
        2 * (rows * width + 2 * rows * hid + width * hid),
        "hidden_back",
    )(tab, top, slope, *pieces)


def up_back(tab, grad_hidden, residual, top, gain, pieces, out_pieces):
    rows, hid = grad_hidden.shape
    width = residual.shape[1]
    count = len(pieces)
    groups = tab.shape[0]
    tn = hid // groups
    size = pieces[0].shape[0]
    chunk = row_chunk(rows)

    def body(tab_ref, h_ref, r_ref, t_ref, g_ref, *rest):
        piece_refs, out_refs = rest[:count], rest[count : 2 * count]
        gr_ref, gb_ref, gm_ref, s_ref, tile, acc, store, sem = rest[2 * count :]
        p = pl.program_id(0)
        copies = load_copies(tab_ref, out_refs, store, sem, width // groups)

        @pl.when(p == 0)
        def _():
            for c in copies:
                c.start()

        fill_tile(tab_ref, piece_refs, tile, width // groups)
        part = dot_nt(h_ref[...], tile[...])

        @pl.when(p == 0)
        def _():
            acc[...] = part

        @pl.when(p > 0)
        def _():
            acc[...] += part

        @pl.when(p == groups - 1)
        def _():
            for c in copies:
                c.wait()
            s_ref[...] = jnp.zeros_like(s_ref)

            @pl.loop(0, rows // chunk)
            def _(i):
                at = pl.ds(pl.multiple_of(i * chunk, chunk), chunk)
                n, rinv = normalize(r_ref[at, :])
                up = acc[at, :]
                grad = t_ref[at, :].astype(F32) + norm_back(up, g_ref[...], n, rinv)
                branch = grad.astype(BF)
                gr_ref[at, :] = grad
                gb_ref[at, :] = branch
                gm_ref[at, :] = dot_nt(branch, store[...]).astype(BF)
                s_ref[0:1, :] += col_sum(up * n)
                s_ref[1:2, :] += col_sum(up)
                s_ref[2:3, :] += col_sum(branch.astype(F32))
                s_ref[3:4, :] += col_sum(t_ref[at, :].astype(F32))

    whole = full((rows, width))
    return call(
        body,
        (
            sds((rows, width), F32),
            sds((rows, width), BF),
            sds((rows, width), BF),
            sds((8, width), F32),
        ),
        (groups,),
        [pl.BlockSpec((rows, tn), lambda p, t: (0, p)), whole, whole, full((1, width))]
        + [pl.BlockSpec((size, tn), lambda p, t: (0, t[p]))] * count
        + anywhere(count),
        (whole, whole, whole, full((8, width))),
        [
            pltpu.VMEM((width, tn), BF),
            pltpu.VMEM((rows, width), F32),
            pltpu.VMEM((width, width), BF),
            pltpu.SemaphoreType.DMA((groups,)),
        ],
        2 * rows * width * (hid + width),
        2 * (rows * hid + 8 * rows * width + width * hid),
        "up_back",
    )(tab, grad_hidden, residual, top, gain, *pieces, *out_pieces)


def qkv_back(tab, grads, x, grad_residual, gain, pieces, images, slots):
    _three, rows, width = grads.shape
    blk = IMG_BLOCK * slots
    count = len(pieces)

    def body(tab_ref, d_ref, x_ref, r_ref, g_ref, *rest):
        piece_refs, (o_ref, s_ref, store, sem) = rest[:count], rest[count:]

        @pl.when(pl.program_id(0) == 0)
        def _():
            copies = load_copies(tab_ref, piece_refs, store, sem, width // tab.shape[0])
            for c in copies:
                c.start()
            s_ref[...] = jnp.zeros_like(s_ref)
            for c in copies:
                c.wait()

        up = dot_nt(d_ref[0], store[:, 0:width])
        up += dot_nt(d_ref[1], store[:, width : 2 * width])
        up += dot_nt(d_ref[2], store[:, 2 * width :])
        n, rinv = normalize(x_ref[...].astype(F32))
        y = r_ref[...] + norm_back(up, g_ref[...], n, rinv)
        s_ref[0:1, :] += col_sum(up * n)
        s_ref[1:2, :] += col_sum(up)
        for b in range(IMG_BLOCK):
            o_ref[b] = y[slots * b : slots * (b + 1)].astype(BF)

    spec = pl.BlockSpec((blk, width), lambda i, t: (i, 0))
    return call(
        body,
        (sds((images, slots, width), BF), sds((8, width), F32)),
        (rows // blk,),
        [pl.BlockSpec((3, blk, width), lambda i, t: (0, i, 0)), spec, spec, full((1, width))]
        + anywhere(count),
        (pl.BlockSpec((IMG_BLOCK, slots, width), lambda i, t: (i, 0, 0)), full((8, width))),
        [pltpu.VMEM((width, 3 * width), BF), pltpu.SemaphoreType.DMA((tab.shape[0],))],
        6 * rows * width * width,
        2 * (3 * rows * width + 4 * rows * width + 3 * width * width),
        "qkv_back",
    )(tab, grads, x, grad_residual, gain, *pieces)


def weight_grad(order, x, g, pieces_of, name, places=None):
    parts, rows, width = g.shape
    count = order.shape[0]
    size = x.shape[1] // pieces_of

    def body(tab_ref, *rest):
        x_refs, (g_ref, o_ref, xs) = rest[:count], rest[count:]

        @pl.when(pl.program_id(0) == 0)
        def _():
            for p in range(count):
                xs[:, size * p : size * (p + 1)] = x_refs[p][...]

        o_ref[...] = dot_tn(xs[...], g_ref[0]).astype(BF)

    tn = width if places is None else width // places.shape[0]
    per = width // tn
    if places is None:
        table = order
        put = pl.BlockSpec((count * size, tn), lambda j, t: (0, j))
    else:
        table = jnp.concatenate([order, places])
        put = pl.BlockSpec((count * size, tn), lambda j, t: (0, t[count + j]))

    def column(p):
        return lambda j, t: (0, t[p])

    return call(
        body,
        sds((count * size, parts * width), BF),
        (parts * per,),
        [pl.BlockSpec((rows, size), column(p)) for p in range(count)]
        + [pl.BlockSpec((1, rows, tn), lambda j, t: (j // per, 0, j % per))],
        put,
        [pltpu.VMEM((rows, count * size), BF)],
        2 * rows * count * size * parts * width,
        2 * (rows * count * size + parts * rows * width + count * size * parts * width),
        name,
    )(table, *([x] * count), g)


def down_grad(order, act, top, pieces_of, name):
    rows, hid = act.shape
    width = top.shape[1]
    count = order.shape[0]
    size = hid // pieces_of

    def body(tab_ref, a_ref, t_ref, o_ref):
        o_ref[...] = dot_tn(a_ref[...], t_ref[...]).astype(BF)

    return call(
        body,
        sds((count * size, width), BF),
        (count,),
        [pl.BlockSpec((rows, size), lambda p, t: (0, t[p])), full((rows, width))],
        pl.BlockSpec((size, width), lambda p, t: (p, 0)),
        [],
        2 * rows * count * size * width,
        2 * (rows * count * size + rows * width + count * size * width),
        name,
    )(order, act, top)


def kept_slots(keep_order, keep_count):
    slot_ids = lax.iota(jnp.int32, keep_order.shape[-1])
    listed = keep_order[:, :, None] == slot_ids[None, None, :]
    within = slot_ids[None, :] < keep_count[:, None]
    return jnp.any(jnp.logical_and(listed, within[:, :, None]), axis=1)


def local(lay, *args):
    (
        patches,
        keep_order,
        keep_count,
        ln1_gain,
        ln1_bias,
        w_qkv,
        bias_q,
        bias_v,
        w_out,
        bias_out,
        ln2_gain,
        ln2_bias,
        w_up,
        bias_up,
        w_down,
        bias_down,
        cotangent,
    ) = args
    images, slots, width = patches.shape
    rows = images * slots
    ndev = lay.count
    own = width // ndev
    own_up = bias_up.shape[0]
    hid = own_up * ndev

    tab = lay.table()
    groups = lay.wide
    half = groups // 2
    clock = Clock(tab)

    small = jnp.concatenate(
        [ln1_gain, ln1_bias, bias_q, bias_v, bias_out, ln2_gain, ln2_bias, bias_down, bias_up]
    )[None, :]
    vec_chain = Chain(gather_small_steps(lay, small))
    qkv_chain = Chain(gather_steps(lay, w_qkv))
    out_chain = Chain(gather_steps(lay, w_out))
    up_chain = Chain(gather_steps(lay, w_up))
    down_chain = Chain(gather_steps(lay, w_down))

    def masks(_tab):
        keep_mask = kept_slots(keep_order, keep_count)
        keep_rows = keep_mask.reshape(rows, 1)
        pad_keys = jnp.pad(
            jnp.where(keep_mask, 0.0, NEG), ((0, 0), (0, 64 - slots)), constant_values=NEG
        )
        key_bias = jnp.concatenate([pad_keys, pad_keys], 1).reshape(images, 1, 128)
        return keep_rows.astype(F32), key_bias

    keep_f, key_bias = clock.tick(masks, [qkv_chain, vec_chain])
    x = clock.tick(lambda t: patches.reshape(rows, width), [qkv_chain, vec_chain])
    early = [qkv_chain, vec_chain, out_chain, up_chain]
    top = clock.tick(
        lambda t: jnp.where(keep_f > 0, cotangent.reshape(rows, width), jnp.zeros((), BF)), early
    )
    for _ in range(lay.chip_bits + lay.line_bits - 3):
        clock.tick(None, early)
    clock.tick(None, [qkv_chain, vec_chain], early)
    clock.drain(qkv_chain, vec_chain)

    vec = vec_chain.result.astype(F32)
    eight = vec[:, : 8 * own].reshape(ndev, 8, own).transpose(1, 0, 2).reshape(8, 1, width)
    gain_one, offset_one, vec_q, vec_v, vec_out, gain_two, offset_two, vec_down = eight
    vec_up = vec[:, 8 * own :].reshape(1, hid)
    vec_qkv = jnp.concatenate([vec_q, jnp.zeros_like(vec_q), vec_v], axis=1)

    qkv_pieces = qkv_chain.result
    normed_one, qkv = clock.tick(
        lambda t: qkv_product(t, x, gain_one, offset_one, vec_qkv, qkv_pieces),
        [out_chain, up_chain, down_chain],
    )
    mixed = clock.tick(
        lambda t: attention(t, qkv, key_bias, slots), [out_chain, up_chain, down_chain]
    )
    clock.drain(out_chain)
    out_pieces = out_chain.result
    residual, normed_two = clock.tick(
        lambda t: out_product(t, mixed, x, vec_out, gain_two, offset_two, out_pieces, slots),
        [up_chain, down_chain],
    )
    clock.drain(up_chain)
    up_pieces = up_chain.result
    act, slope = clock.tick(
        lambda t: up_product(t, normed_two, vec_up, up_pieces), [down_chain]
    )

    straight = jnp.arange(groups, dtype=jnp.int32)
    size = width // groups
    fits = size % 128 == 0

    def rows_of(t, part):
        if fits:
            return t[half * part : half * (part + 1)]
        return straight[part : part + 1] + 0 * t[:1]

    def placed(a):
        return a if fits else a.reshape(rows, groups, size)[:, tab].reshape(rows, width)

    many = groups if fits else 2

    give = clock.tick(
        lambda t: down_grad(straight[half:] + 0 * t[:half], act, top, groups, "down_grad_give"),
        [down_chain],
    )
    keep = []
    down_rs = Chain(scatter_steps(lay, give, keep))
    keep.append(
        clock.tick(
            lambda t: down_grad(straight[:half] + 0 * t[:half], act, top, groups, "down_grad_keep"),
            [down_rs, down_chain],
            [down_chain],
        )
    )
    clock.drain(down_chain)
    down_pieces = down_chain.result
    clock.tick(None, [], [down_rs])
    grad_hidden, sum_up = clock.tick(
        lambda t: hidden_back(t, top, slope, down_pieces), [down_rs]
    )

    n2 = placed(normed_two)
    gh = grad_hidden[None]
    give = clock.tick(
        lambda t: weight_grad(rows_of(t, 1), n2, gh, many, "up_grad_give", tab), [down_rs]
    )
    keep = []
    up_rs = Chain(scatter_steps(lay, give, keep))
    keep.append(
        clock.tick(
            lambda t: weight_grad(rows_of(t, 0), n2, gh, many, "up_grad_keep", tab),
            [up_rs, down_rs],
            [down_rs],
        )
    )
    clock.tick(None, [], [up_rs])
    grad_residual, branch, grad_mixed, sums_two = clock.tick(
        lambda t: up_back(t, grad_hidden, residual, top, gain_two, up_pieces, out_pieces),
        [up_rs, down_rs],
    )
    mx = placed(mixed)
    give = clock.tick(
        lambda t: weight_grad(rows_of(t, 1), mx, branch[None], many, "out_grad_give"),
        [up_rs, down_rs],
        [],
    )
    keep = []
    out_rs = Chain(scatter_steps(lay, give, keep))
    keep.append(
        clock.tick(
            lambda t: weight_grad(rows_of(t, 0), mx, branch[None], many, "out_grad_keep"),
            [out_rs],
            [up_rs, down_rs],
        )
    )
    clock.tick(None, [], [out_rs])
    grads, sums_att = clock.tick(
        lambda t: attention_back(t, qkv, key_bias, grad_mixed, slots), [up_rs, down_rs, out_rs]
    )
    n1 = placed(normed_one)
    give = clock.tick(
        lambda t: weight_grad(rows_of(t, 1), n1, grads, many, "qkv_grad_give"),
        [up_rs, down_rs, out_rs],
    )
    keep = []
    qkv_rs = Chain(scatter_steps(lay, give, keep))
    keep.append(
        clock.tick(
            lambda t: weight_grad(rows_of(t, 0), n1, grads, many, "qkv_grad_keep"),
            [qkv_rs, out_rs, up_rs, down_rs],
            [out_rs, up_rs, down_rs],
        )
    )
    clock.tick(None, [], [qkv_rs])
    grad_patches, sums_one = clock.tick(
        lambda t: qkv_back(t, grads, x, grad_residual, gain_one, qkv_pieces, images, slots),
        [qkv_rs, out_rs, up_rs, down_rs],
    )
    eight_sums = jnp.stack(
        [
            sums_one[0],
            sums_one[1],
            sums_att[0],
            sums_att[2],
            sums_two[2],
            sums_two[0],
            sums_two[1],
            sums_two[3],
        ]
    )
    packed = jnp.concatenate(
        [
            eight_sums.reshape(8, ndev, own).transpose(1, 0, 2).reshape(ndev, 8 * own),
            sum_up.reshape(ndev, own_up),
        ],
        axis=1,
    )
    vec_rs = Chain(scatter_small_steps(lay, packed))
    late = [qkv_rs, vec_rs, out_rs, up_rs, down_rs]
    blocks = images // IMG_BLOCK
    split = blocks // 3
    shape = (images, slots, width)
    first_out = clock.tick(
        lambda t: down_product(
            t, act, residual, vec_down, keep_f, down_pieces, shape, 0, split
        ),
        late,
    )
    block_out = clock.tick(
        lambda t: down_product(
            t, act, residual, vec_down, keep_f, down_pieces, shape, split, blocks, first_out
        ),
        late,
    )
    clock.drain(*late)
    mine = vec_rs.result[0]
    vecs = [mine[own * i : own * (i + 1)] for i in range(8)]
    return (
        block_out,
        grad_patches,
        vecs[0],
        vecs[1],
        qkv_rs.result,
        vecs[2],
        vecs[3],
        out_rs.result,
        vecs[4],
        vecs[5],
        vecs[6],
        up_rs.result,
        mine[8 * own :],
        down_rs.result,
        vecs[7],
    )


def solution(mesh):
    both = P(AXES)
    mat = P(AXES, None)
    cube = P(AXES, None, None)
    in_specs = (
        cube, mat, both, both, both, mat, both, both, mat, both, both, both, mat, both, mat, both,
        cube,
    )
    out_specs = (
        cube, cube, both, both, mat, both, both, mat, both, both, both, mat, both, mat, both,
    )
    return jax.shard_map(
        functools.partial(local, Layout(mesh)),
        mesh=mesh,
        in_specs=in_specs,
        out_specs=out_specs,
        check_vma=False,
    )
```

```python
import functools

import jax
import jax.numpy as jnp
import numpy as np
from jax import lax
from jax.experimental import pallas as pl
from jax.experimental.pallas import tpu as pltpu
from jax.sharding import PartitionSpec as P

HEADS = 16
EPS = 1e-06
AXES = ("wide", "narrow")
BF = jnp.bfloat16
F32 = jnp.float32
NEG = -1e30
VMEM_LIMIT = 62 << 20
IMG_BLOCK = 8


class Layout:
    def __init__(self, mesh):
        self.wide = mesh.shape["wide"]
        self.narrow = mesh.shape["narrow"]
        self.count = self.wide * self.narrow
        self.chip_bits = (self.wide // 2).bit_length() - 1
        self.line_bits = self.narrow.bit_length() - 1

    def bit_of(self, core, level):
        return level if core == 0 else self.chip_bits - 1 - level

    def flip(self, core, piece):
        total = 0
        for level in range(self.chip_bits):
            if piece >> level & 1:
                total ^= 1 << self.bit_of(core, level)
        return total

    def swap_line(self, bit):
        return [(d, d ^ (1 << bit)) for d in range(self.count)]

    def swap_core(self):
        return [(d, d ^ self.narrow) for d in range(self.count)]

    def swap_chip(self, level):
        pairs = []
        for d in range(self.count):
            place, line = divmod(d, self.narrow)
            chip, core = divmod(place, 2)
            other = chip ^ (1 << self.bit_of(core, level))
            pairs.append((d, (other * 2 + core) * self.narrow + line))
        return pairs

    def shift_line(self, by):
        return [(d, d ^ by) for d in range(self.count)]

    def shift_chip(self, by):
        return [(d, d ^ (2 * self.narrow * by)) for d in range(self.count)]

    def swap_chip_bit(self, bit):
        return [(d, d ^ (2 * self.narrow << bit)) for d in range(self.count)]

    def table(self):
        place = lax.axis_index("wide")
        chip, core = place // 2, place % 2
        half = 1 << self.chip_bits
        even = np.array([self.flip(0, q) for q in range(half)], np.int32)
        odd = np.array([self.flip(1, q) for q in range(half)], np.int32)
        mine = jnp.where(core == 0, even, odd)
        other = jnp.where(core == 0, odd, even)
        return jnp.concatenate(
            [(chip ^ mine) * 2 + core, (chip ^ other) * 2 + (1 - core)]
        ).astype(jnp.int32)


def move(x, pairs):
    return lax.ppermute(x, AXES, pairs)


def in_order(bit, mine, theirs):
    return jnp.where(
        bit == 0, jnp.concatenate([mine, theirs], 0), jnp.concatenate([theirs, mine], 0)
    )


def gather_steps(lay, x):
    x = yield from gather_line_steps(lay, x)
    parts = [x]
    for level in range(lay.chip_bits):
        x = parts[0] if len(parts) == 1 else jnp.concatenate(parts, 0)
        if level < lay.chip_bits - 1:
            (got,) = yield [(x, lay.swap_chip(level))]
            parts = [x, got]
        else:
            got, other = yield [(x, lay.swap_chip(level)), (x, lay.swap_core())]
    (last,) = yield [(got, lay.swap_core())]
    return [x, got, other, last]


def gather_line_steps(lay, x):
    line = lax.axis_index("narrow")
    x = x[None]
    for b in reversed(range(lay.line_bits)):
        (got,) = yield [(x, lay.swap_line(b))]
        bit = (line >> b) & 1
        a, c = x[:, None], got[:, None]
        both = jnp.where(bit == 0, jnp.concatenate([a, c], 1), jnp.concatenate([c, a], 1))
        x = both.reshape(-1, *x.shape[1:])
    return x.reshape(-1, x.shape[-1])


def gather_small_steps(lay, x):
    line, place = lax.axis_index("narrow"), lax.axis_index("wide")
    for b in range(lay.line_bits):
        (got,) = yield [(x, lay.swap_line(b))]
        x = in_order((line >> b) & 1, x, got)
    (got,) = yield [(x, lay.swap_core())]
    x = in_order(place & 1, x, got)
    for b in range(lay.chip_bits):
        (got,) = yield [(x, lay.swap_chip_bit(b))]
        x = in_order((place >> (b + 1)) & 1, x, got)
    return x


def total(terms, dtype=BF):
    out = terms[0].astype(F32)
    for t in terms[1:]:
        out += t.astype(F32)
    return out.astype(dtype)


def scatter_line_steps(lay, terms, dtype=BF):
    line = lax.axis_index("narrow")
    own, cols = terms[0].shape[0] // lay.narrow, terms[0].shape[1]
    terms = [t.reshape((2,) * lay.line_bits + (own, cols)) for t in terms]
    for b in range(lay.line_bits):
        bit, axis = (line >> b) & 1, lay.line_bits - 1 - b
        give = [lax.dynamic_index_in_dim(t, 1 - bit, axis, False) for t in terms]
        (got,) = yield [(total(give, dtype), lay.swap_line(b))]
        terms = [lax.dynamic_index_in_dim(t, bit, axis, False) for t in terms] + [got]
    return total(terms, F32)


def scatter_steps(lay, give, keep):
    (got,) = yield [(give, lay.swap_core())]
    terms = [keep[0], got]
    for level in reversed(range(lay.chip_bits)):
        size = terms[0].shape[0] // 2
        (got,) = yield [(total([t[size:] for t in terms]), lay.swap_chip(level))]
        terms = [t[:size] for t in terms] + [got]
    return (yield from scatter_line_steps(lay, [total(terms)]))


def direct(x, at, pairs):
    gives = [
        (lax.dynamic_index_in_dim(x, at ^ k, 0, False), pairs(k)) for k in range(1, x.shape[0])
    ]
    got = yield gives
    return total([lax.dynamic_index_in_dim(x, at, 0, False)] + list(got), F32)


def scatter_small_steps(lay, x):
    place, line = lax.axis_index("wide"), lax.axis_index("narrow")
    cols = x.shape[1]
    x = x.reshape(lay.wide // 2, -1, cols)
    x = yield from direct(x, place // 2, lay.shift_chip)
    x = x.reshape(2, lay.narrow, cols)
    x = yield from direct(x, place % 2, lambda k: lay.swap_core())
    return (yield from direct(x, line, lay.shift_line))


class Chain:
    def __init__(self, steps):
        self.steps = steps
        self.want = next(steps)
        self.flying = None
        self.result = None

    def take(self, got):
        self.flying = None
        try:
            self.want = self.steps.send(got)
        except StopIteration as end:
            self.want, self.result = None, end.value


class Clock:
    def __init__(self, tab):
        self.tab = tab
        self.chains = []

    def begin(self, *chains):
        for c in chains:
            if c.want is None or c.flying is not None:
                continue
            operands, self.tab = lax.optimization_barrier(([w[0] for w in c.want], self.tab))
            c.flying = [move(x, w[1]) for x, w in zip(operands, c.want)]

    def tick(self, compute=None, start=(), finish=None):
        self.begin(*start)
        out = compute(self.tab) if compute is not None else ()
        done = [c for c in (start if finish is None else finish) if c.flying is not None]
        self.tab, got, out = lax.optimization_barrier((self.tab, [c.flying for c in done], out))
        for c, g in zip(done, got):
            c.take(g)
        return out

    def drain(self, *chains):
        while any(c.want is not None for c in chains):
            self.tick(None, chains)


def dot_nn(a, b):
    return jnp.dot(a, b, preferred_element_type=F32)


def dot_nt(a, b):
    return lax.dot_general(a, b, (((1,), (1,)), ((), ())), preferred_element_type=F32)


def dot_tn(a, b):
    return lax.dot_general(a, b, (((0,), (0,)), ((), ())), preferred_element_type=F32)


def normalize(r):
    center = r - jnp.mean(r, axis=-1, keepdims=True)
    spread = jnp.mean(center * center, axis=-1, keepdims=True)
    rinv = lax.rsqrt(spread + EPS)
    return center * rinv, rinv


def norm_back(up, gain, n, rinv):
    u = up * gain
    return rinv * (
        u - jnp.mean(u, axis=-1, keepdims=True) - n * jnp.mean(u * n, axis=-1, keepdims=True)
    )


def col_sum(x):
    return jnp.sum(x, axis=0, keepdims=True)


def call(body, outs, grid, in_specs, out_specs, scratch, flops, nbytes, name, trans=0, aliases={}):
    return pl.pallas_call(
        body,
        out_shape=outs,
        grid_spec=pltpu.PrefetchScalarGridSpec(
            num_scalar_prefetch=1,
            grid=grid,
            in_specs=in_specs,
            out_specs=out_specs,
            scratch_shapes=scratch,
        ),
        compiler_params=pltpu.CompilerParams(vmem_limit_bytes=VMEM_LIMIT),
        cost_estimate=pl.CostEstimate(flops=flops, bytes_accessed=nbytes, transcendentals=trans),
        name=name,
        input_output_aliases=aliases,
    )


def full(shape):
    zeros = (0,) * len(shape)
    return pl.BlockSpec(shape, lambda *_: zeros)


def anywhere(count):
    return [pl.BlockSpec(memory_space=pl.ANY)] * count


def sds(shape, dtype):
    return jax.ShapeDtypeStruct(shape, dtype)


def fill_tile(tab, pieces, tile, size):
    per = pieces[0].shape[0] // size
    for a, piece in enumerate(pieces):
        for i in range(per):
            at = pl.multiple_of(tab[a * per + i] * size, size)
            tile[pl.ds(at, size), :] = piece[i * size : (i + 1) * size, :]


def load_copies(tab, pieces, store, sem, size):
    per = pieces[0].shape[0] // size
    copies = []
    for a, piece in enumerate(pieces):
        for i in range(per):
            at = pl.multiple_of(tab[a * per + i] * size, size)
            copies.append(
                pltpu.make_async_copy(
                    piece.at[pl.ds(i * size, size)],
                    store.at[pl.ds(at, size)],
                    sem.at[a * per + i],
                )
            )
    return copies


def by_slot(y, o_ref, turn, slots):
    for b in range(IMG_BLOCK):
        turn[:, b, :] = y[slots * b : slots * (b + 1)]
    o_ref[...] = turn[...].astype(BF)


def row_chunk(rows):
    for size in (240, 200, 160, 80, 48, 16):
        if rows % size == 0:
            return size
    return rows


def qkv_product(tab, x, gain, bias, bias_qkv, pieces):
    rows, width = x.shape
    cols = pieces[0].shape[1]
    tn = 512
    count = len(pieces)
    chunk = row_chunk(rows)

    def body(tab_ref, x_ref, g_ref, b_ref, c_ref, *rest):
        piece_refs, (n_ref, o_ref, tile) = rest[:count], rest[count:]

        @pl.when(pl.program_id(0) == 0)
        def _():
            @pl.loop(0, rows // chunk)
            def _(i):
                at = pl.ds(pl.multiple_of(i * chunk, chunk), chunk)
                n, _unused = normalize(x_ref[at, :].astype(F32))
                n_ref[at, :] = (n * g_ref[...] + b_ref[...]).astype(BF)

        fill_tile(tab_ref, piece_refs, tile, width // tab.shape[0])
        o_ref[...] = (dot_nn(n_ref[...], tile[...]) + c_ref[...]).astype(BF)

    size = pieces[0].shape[0]
    return call(
        body,
        (sds((rows, width), BF), sds((rows, cols), BF)),
        (cols // tn,),
        [full((rows, width)), full((1, width)), full((1, width))]
        + [pl.BlockSpec((1, tn), lambda j, t: (0, j))]
        + [pl.BlockSpec((size, tn), lambda j, t: (0, j))] * count,
        (full((rows, width)), pl.BlockSpec((rows, tn), lambda j, t: (0, j))),
        [pltpu.VMEM((width, tn), BF)],
        2 * rows * width * cols,
        2 * (2 * rows * width + rows * cols + width * cols),
        "qkv_product",
    )(tab, x, gain, bias, bias_qkv, *pieces)


def two_heads(x, lane):
    return jnp.concatenate([jnp.where(lane < 64, x, 0.0), jnp.where(lane < 64, 0.0, x)], 0).astype(
        BF
    )


def half_max(s, low):
    a = jnp.max(jnp.where(low, s, NEG), axis=-1, keepdims=True)
    b = jnp.max(jnp.where(low, NEG, s), axis=-1, keepdims=True)
    return jnp.where(low, a, b)


def half_sum(s, ones):
    high = s.astype(BF)
    rest = (s - high.astype(F32)).astype(BF)
    return dot_nn(high, ones) + dot_nn(rest, ones)


def softmax_pair(s, low, ones):
    e = jnp.exp(s - half_max(s, low))
    return e / half_sum(e, ones)


def head_ones():
    row = lax.broadcasted_iota(jnp.int32, (128, 128), 0) < 64
    col = lax.broadcasted_iota(jnp.int32, (128, 128), 1) < 64
    return jnp.where(row == col, 1.0, 0.0).astype(BF)


def attention(tab, qkv, key_bias, slots):
    rows, three = qkv.shape
    width = three // 3
    pairs = width // 128
    blk = IMG_BLOCK * slots
    pad = -(-slots // 8) * 8
    scale = float(64**-0.5)

    def body(tab_ref, q_ref, k_ref, v_ref, kb_ref, o_ref, qf, kf, vf, of, sf):
        for ref, src in ((qf, q_ref), (kf, k_ref), (vf, v_ref)):
            ref[0:blk, :] = src[...].astype(F32)
            ref[blk : blk + 16, :] = jnp.zeros((16, 128), F32)
        lane = lax.broadcasted_iota(jnp.int32, (64, 128), 1)
        low = lax.broadcasted_iota(jnp.int32, (pad, 128), 1) < 64
        ones = head_ones()
        for b in range(IMG_BLOCK):
            at = slots * b
            kk = two_heads(kf[at : at + 64, :], lane)
            q = qf[at : at + pad, :].astype(BF)
            sf[pad * b : pad * (b + 1), :] = dot_nt(q, kk) * scale + kb_ref[b]
        low = lax.broadcasted_iota(jnp.int32, (pad * IMG_BLOCK, 128), 1) < 64
        p = softmax_pair(sf[...], low, ones)
        outs = []
        for b in range(IMG_BLOCK):
            at = slots * b
            vv = two_heads(vf[at : at + 64, :], lane)
            outs.append(dot_nn(p[pad * b : pad * (b + 1)].astype(BF), vv))
        for b in range(IMG_BLOCK):
            at = slots * b
            of[at : at + pad, :] = outs[b]
        o_ref[...] = of[0:blk, :].astype(BF)

    return call(
        body,
        sds((rows, width), BF),
        (pairs, rows // blk),
        [
            pl.BlockSpec((blk, 128), lambda h, i, t: (i, h)),
            pl.BlockSpec((blk, 128), lambda h, i, t: (i, h + pairs)),
            pl.BlockSpec((blk, 128), lambda h, i, t: (i, h + 2 * pairs)),
            pl.BlockSpec((IMG_BLOCK, 1, 128), lambda h, i, t: (i, 0, 0)),
        ],
        pl.BlockSpec((blk, 128), lambda h, i, t: (i, h)),
        [pltpu.VMEM((blk + 16, 128), F32)] * 4 + [pltpu.VMEM((pad * IMG_BLOCK, 128), F32)],
        8 * rows * 128 * width * 2,
        2 * 4 * rows * width,
        "attention",
    )(tab, qkv, qkv, qkv, key_bias)


def attention_back(tab, qkv, key_bias, grad_mixed, slots, first, last, before=()):
    rows, three = qkv.shape
    width = three // 3
    pairs = width // 128
    blk = IMG_BLOCK * slots
    pad = -(-slots // 8) * 8
    tall = pad * IMG_BLOCK
    scale = float(64**-0.5)

    def body(tab_ref, q_ref, k_ref, v_ref, kb_ref, g_ref, *rest):
        o_ref, s_ref, qf, kf, vf, gf, dqf, dkf, dvf, sf, pf = rest[len(before) :]
        for ref, src in ((qf, q_ref), (kf, k_ref), (vf, v_ref), (gf, g_ref)):
            ref[0:blk, :] = src[...].astype(F32)
            ref[blk : blk + 16, :] = jnp.zeros((16, 128), F32)
        lane = lax.broadcasted_iota(jnp.int32, (64, 128), 1)
        low = lax.broadcasted_iota(jnp.int32, (pad, 128), 1) < 64
        real = lax.broadcasted_iota(jnp.int32, (pad, 128), 0) < slots
        ones = head_ones()
        kks, qs, gs = [], [], []
        for b in range(IMG_BLOCK):
            at = slots * b
            kks.append(two_heads(kf[at : at + 64, :], lane))
            vv = two_heads(vf[at : at + 64, :], lane)
            qs.append(jnp.where(real, qf[at : at + pad, :], 0.0).astype(BF))
            gs.append(jnp.where(real, gf[at : at + pad, :], 0.0).astype(BF))
            sf[pad * b : pad * (b + 1), :] = dot_nt(qs[b], kks[b]) * scale + kb_ref[b]
            pf[pad * b : pad * (b + 1), :] = dot_nt(gs[b], vv)
        p = softmax_pair(sf[...], lax.broadcasted_iota(jnp.int32, (tall, 128), 1) < 64, ones)
        dp = pf[...]
        ds = p * (dp - half_sum(p * dp, ones))
        res = []
        for b in range(IMG_BLOCK):
            d = ds[pad * b : pad * (b + 1)].astype(BF)
            w = p[pad * b : pad * (b + 1)].astype(BF)
            res.append((dot_nn(d, kks[b]), dot_tn(d, qs[b]), dot_tn(w, gs[b])))
        for b in range(IMG_BLOCK):
            at = slots * b
            dq, dk, dv = res[b]
            dqf[at : at + pad, :] = dq * scale
            dkf[at : at + pad, :] = jnp.where(low, dk[0:pad], dk[64 : 64 + pad]) * scale
            dvf[at : at + pad, :] = jnp.where(low, dv[0:pad], dv[64 : 64 + pad])

        @pl.when(pl.program_id(1) == 0)
        def _():
            s_ref[...] = jnp.zeros_like(s_ref)

        for at, ref in enumerate((dqf, dkf, dvf)):
            rounded = ref[0:blk, :].astype(BF)
            o_ref[at] = rounded
            if at != 1:
                s_ref[at : at + 1, :] += col_sum(rounded.astype(F32))

    def pair(skip):
        return pl.BlockSpec((blk, 128), lambda h, i, t: (i, h + first + skip))

    return call(
        body,
        (sds((3, rows, width), BF), sds((8, width), F32)),
        (last - first, rows // blk),
        [
            pair(0),
            pair(pairs),
            pair(2 * pairs),
            pl.BlockSpec((IMG_BLOCK, 1, 128), lambda h, i, t: (i, 0, 0)),
            pair(0),
        ]
        + anywhere(len(before)),
        (
            pl.BlockSpec((3, blk, 128), lambda h, i, t: (0, i, h + first)),
            pl.BlockSpec((8, 128), lambda h, i, t: (0, h + first)),
        ),
        [pltpu.VMEM((blk + 16, 128), F32)] * 7 + [pltpu.VMEM((tall, 128), F32)] * 2,
        20 * rows * 128 * width * 2 * (last - first) // pairs,
        2 * 7 * rows * width * (last - first) // pairs,
        "attention_back",
        aliases={6: 0, 7: 1} if before else {},
    )(tab, qkv, qkv, qkv, key_bias, grad_mixed, *before)


def out_product(tab, mixed, x, bias_out, gain, bias, pieces, slots):
    rows, width = mixed.shape
    blk = IMG_BLOCK * slots
    count = len(pieces)

    def body(tab_ref, m_ref, x_ref, c_ref, g_ref, b_ref, *rest):
        piece_refs, (r_ref, n_ref, store, sem) = rest[:count], rest[count:]

        @pl.when(pl.program_id(0) == 0)
        def _():
            copies = load_copies(tab_ref, piece_refs, store, sem, width // tab.shape[0])
            for c in copies:
                c.start()
            for c in copies:
                c.wait()

        r = x_ref[...].astype(F32) + dot_nn(m_ref[...], store[...]) + c_ref[...]
        r_ref[...] = r
        n, _unused = normalize(r)
        n_ref[...] = (n * g_ref[...] + b_ref[...]).astype(BF)

    spec = pl.BlockSpec((blk, width), lambda i, t: (i, 0))
    return call(
        body,
        (sds((rows, width), F32), sds((rows, width), BF)),
        (rows // blk,),
        [spec, spec] + [full((1, width))] * 3 + anywhere(count),
        (spec, spec),
        [pltpu.VMEM((width, width), BF), pltpu.SemaphoreType.DMA((tab.shape[0],))],
        2 * rows * width * width,
        10 * rows * width + 2 * width * width,
        "out_product",
    )(tab, mixed, x, bias_out, gain, bias, *pieces)


def up_product(tab, n2, bias_up, pieces):
    rows, width = n2.shape
    hid = pieces[0].shape[1]
    count = len(pieces)
    groups = tab.shape[0]
    tn = hid // groups
    size = pieces[0].shape[0]

    def body(tab_ref, n_ref, c_ref, *rest):
        piece_refs, (a_ref, d_ref, tile) = rest[:count], rest[count:]
        fill_tile(tab_ref, piece_refs, tile, width // groups)
        u = dot_nn(n_ref[...], tile[...]) + c_ref[...]
        phi = 0.5 + 0.5 * lax.erf(u * np.float32(0.5**0.5))
        a_ref[...] = (u * phi).astype(BF)
        slope = phi + u * jnp.exp(-0.5 * u * u) * np.float32((2 * np.pi) ** -0.5)
        d_ref[...] = slope.astype(BF)

    spec = pl.BlockSpec((rows, tn), lambda p, t: (0, p))
    return call(
        body,
        (sds((rows, hid), BF), sds((rows, hid), BF)),
        (groups,),
        [full((rows, width)), pl.BlockSpec((1, tn), lambda p, t: (0, t[p]))]
        + [pl.BlockSpec((size, tn), lambda p, t: (0, t[p]))] * count,
        (spec, spec),
        [pltpu.VMEM((width, tn), BF)],
        2 * rows * width * hid + 30 * rows * hid,
        2 * (rows * width + 2 * rows * hid + width * hid),
        "up_product",
        2 * rows * hid,
    )(tab, n2, bias_up, *pieces)


def down_product(tab, act, residual, bias_down, keep, pieces, shape, first, last, before=None):
    images, slots, width = shape
    rows, hid = act.shape
    blk = IMG_BLOCK * slots
    count = len(pieces)
    size = pieces[0].shape[0]

    def body(tab_ref, a_ref, r_ref, c_ref, k_ref, *rest):
        piece_refs, (o_ref, store, turn, sem) = rest[:count], rest[-4:]

        def dma(p):
            return pltpu.make_async_copy(
                piece_refs[p], store.at[pl.ds(p * size, size)], sem.at[p]
            )

        @pl.when(pl.program_id(0) == 0)
        def _():
            for p in range(count):
                dma(p).start()
            if last - first > 1:
                for p in range(count):
                    dma(p).wait()

        y = r_ref[...] + c_ref[...]
        for p in range(count):
            if last - first == 1:
                dma(p).wait()
            part = slice(p * size, (p + 1) * size)
            y += dot_nn(a_ref[:, part], store[part, :])
        y = jnp.where(k_ref[...] > 0.0, y, 0.0)
        by_slot(y, o_ref, turn, slots)

    share = blk * (last - first)
    more = [] if before is None else [before]
    return call(
        body,
        sds((slots, images, width), BF),
        (last - first,),
        [
            pl.BlockSpec((blk, hid), lambda i, t: (i + first, 0)),
            pl.BlockSpec((blk, width), lambda i, t: (i + first, 0)),
            full((1, width)),
            pl.BlockSpec((blk, 1), lambda i, t: (i + first, 0)),
        ]
        + anywhere(count + len(more)),
        pl.BlockSpec((slots, IMG_BLOCK, width), lambda i, t: (0, i + first, 0)),
        [
            pltpu.VMEM((hid, width), BF),
            pltpu.VMEM((slots, IMG_BLOCK, width), F32),
            pltpu.SemaphoreType.DMA((count,)),
        ],
        2 * share * width * hid,
        2 * (share * hid + 3 * share * width + width * hid),
        "down_product",
        aliases={} if before is None else {5 + count: 0},
    )(tab, act, residual, bias_down, keep, *pieces, *more)


def hidden_back(tab, top, slope, pieces):
    rows, width = top.shape
    hid = slope.shape[1]
    count = len(pieces)
    groups = tab.shape[0]
    tn = hid // groups
    per = groups // count

    def body(tab_ref, t_ref, d_ref, *rest):
        piece_refs, (o_ref, s_ref, store, sem) = rest[:count], rest[count:]
        p = pl.program_id(0)
        copies = [
            pltpu.make_async_copy(
                piece_refs[g // per].at[pl.ds(g % per * tn, tn)], store.at[g], sem.at[g]
            )
            for g in range(groups)
        ]

        @pl.when(p == 0)
        def _():
            for c in copies:
                c.start()

        pltpu.make_async_copy(store.at[p], store.at[p], sem.at[p]).wait()
        g = (dot_nt(t_ref[...], store[p]) * d_ref[...].astype(F32)).astype(BF)
        o_ref[...] = g
        s_ref[...] = col_sum(g.astype(F32))

    spec = pl.BlockSpec((rows, tn), lambda p, t: (0, p))
    return call(
        body,
        (sds((rows, hid), BF), sds((1, hid), F32)),
        (groups,),
        [full((rows, width)), spec] + anywhere(count),
        (
            pl.BlockSpec((rows, tn), lambda p, t: (0, t[p])),
            pl.BlockSpec((1, tn), lambda p, t: (0, t[p])),
        ),
        [pltpu.VMEM((groups, tn, width), BF), pltpu.SemaphoreType.DMA((groups,))],
        2 * rows * width * hid,
        2 * (rows * width + 2 * rows * hid + width * hid),
        "hidden_back",
    )(tab, top, slope, *pieces)


def up_back(tab, grad_hidden, residual, top, gain, pieces, out_pieces, slots):
    rows, hid = grad_hidden.shape
    width = residual.shape[1]
    count = len(pieces)
    groups = tab.shape[0]
    blk = IMG_BLOCK * slots

    def body(tab_ref, h_ref, r_ref, t_ref, g_ref, *rest):
        piece_refs, out_refs = rest[:count], rest[count : 2 * count]
        gr_ref, gb_ref, gm_ref, s_ref, up_store, store, up_sem, sem = rest[2 * count :]

        @pl.when(pl.program_id(0) == 0)
        def _():
            ups = load_copies(tab_ref, piece_refs, up_store, up_sem, width // groups)
            outs = load_copies(tab_ref, out_refs, store, sem, width // groups)
            for c in ups + outs:
                c.start()
            s_ref[...] = jnp.zeros_like(s_ref)
            for c in ups + outs:
                c.wait()

        up = dot_nt(h_ref[...], up_store[...])
        n, rinv = normalize(r_ref[...])
        top_rows = t_ref[...].astype(F32)
        grad = top_rows + norm_back(up, g_ref[...], n, rinv)
        branch = grad.astype(BF)
        gr_ref[...] = grad
        gb_ref[...] = branch
        gm_ref[...] = dot_nt(branch, store[...]).astype(BF)
        s_ref[0:1, :] += col_sum(up * n)
        s_ref[1:2, :] += col_sum(up)
        s_ref[2:3, :] += col_sum(branch.astype(F32))
        s_ref[3:4, :] += col_sum(top_rows)

    spec = pl.BlockSpec((blk, width), lambda i, t: (i, 0))
    return call(
        body,
        (
            sds((rows, width), F32),
            sds((rows, width), BF),
            sds((rows, width), BF),
            sds((8, width), F32),
        ),
        (rows // blk,),
        [pl.BlockSpec((blk, hid), lambda i, t: (i, 0)), spec, spec, full((1, width))]
        + anywhere(2 * count),
        (spec, spec, spec, full((8, width))),
        [
            pltpu.VMEM((width, hid), BF),
            pltpu.VMEM((width, width), BF),
            pltpu.SemaphoreType.DMA((groups,)),
            pltpu.SemaphoreType.DMA((groups,)),
        ],
        2 * rows * width * (hid + width),
        2 * (rows * hid + 8 * rows * width + width * hid),
        "up_back",
    )(tab, grad_hidden, residual, top, gain, *pieces, *out_pieces)


def qkv_back(tab, grads, x, grad_residual, gain, pieces, images, slots):
    _three, rows, width = grads.shape
    blk = IMG_BLOCK * slots
    count = len(pieces)

    def body(tab_ref, d_ref, x_ref, r_ref, g_ref, *rest):
        piece_refs, (o_ref, s_ref, store, turn, sem) = rest[:count], rest[count:]

        @pl.when(pl.program_id(0) == 0)
        def _():
            copies = load_copies(tab_ref, piece_refs, store, sem, width // tab.shape[0])
            for c in copies:
                c.start()
            s_ref[...] = jnp.zeros_like(s_ref)
            for c in copies:
                c.wait()

        up = dot_nt(d_ref[0], store[:, 0:width])
        up += dot_nt(d_ref[1], store[:, width : 2 * width])
        up += dot_nt(d_ref[2], store[:, 2 * width :])
        n, rinv = normalize(x_ref[...].astype(F32))
        y = r_ref[...] + norm_back(up, g_ref[...], n, rinv)
        s_ref[0:1, :] += col_sum(up * n)
        s_ref[1:2, :] += col_sum(up)
        by_slot(y, o_ref, turn, slots)

    spec = pl.BlockSpec((blk, width), lambda i, t: (i, 0))
    return call(
        body,
        (sds((slots, images, width), BF), sds((8, width), F32)),
        (rows // blk,),
        [pl.BlockSpec((3, blk, width), lambda i, t: (0, i, 0)), spec, spec, full((1, width))]
        + anywhere(count),
        (pl.BlockSpec((slots, IMG_BLOCK, width), lambda i, t: (0, i, 0)), full((8, width))),
        [
            pltpu.VMEM((width, 3 * width), BF),
            pltpu.VMEM((slots, IMG_BLOCK, width), F32),
            pltpu.SemaphoreType.DMA((tab.shape[0],)),
        ],
        6 * rows * width * width,
        2 * (3 * rows * width + 4 * rows * width + 3 * width * width),
        "qkv_back",
    )(tab, grads, x, grad_residual, gain, *pieces)


def weight_grad(order, x, g, pieces_of, name, places=None):
    parts, rows, width = g.shape
    count = order.shape[0]
    size = x.shape[1] // pieces_of

    def body(tab_ref, *rest):
        x_refs, (g_ref, o_ref, xs) = rest[:count], rest[count:]

        @pl.when(pl.program_id(0) == 0)
        def _():
            for p in range(count):
                xs[:, size * p : size * (p + 1)] = x_refs[p][...]

        o_ref[...] = dot_tn(xs[...], g_ref[0]).astype(BF)

    tn = min(width, 1024) if places is None else width // places.shape[0]
    per = width // tn
    if places is None:
        table = order
        put = pl.BlockSpec((count * size, tn), lambda j, t: (0, j))
    else:
        table = jnp.concatenate([order, places])
        put = pl.BlockSpec((count * size, tn), lambda j, t: (0, t[count + j]))

    def column(p):
        return lambda j, t: (0, t[p])

    return call(
        body,
        sds((count * size, parts * width), BF),
        (parts * per,),
        [pl.BlockSpec((rows, size), column(p)) for p in range(count)]
        + [pl.BlockSpec((1, rows, tn), lambda j, t: (j // per, 0, j % per))],
        put,
        [pltpu.VMEM((rows, count * size), BF)],
        2 * rows * count * size * parts * width,
        2 * (rows * count * size + parts * rows * width + count * size * parts * width),
        name,
    )(table, *([x] * count), g)


def down_grad(order, act, top, pieces_of, name):
    rows, hid = act.shape
    width = top.shape[1]
    count = order.shape[0]
    size = hid // pieces_of

    def body(tab_ref, a_ref, t_ref, o_ref):
        o_ref[...] = dot_tn(a_ref[...], t_ref[...]).astype(BF)

    return call(
        body,
        sds((count * size, width), BF),
        (count,),
        [pl.BlockSpec((rows, size), lambda p, t: (0, t[p])), full((rows, width))],
        pl.BlockSpec((size, width), lambda p, t: (p, 0)),
        [],
        2 * rows * count * size * width,
        2 * (rows * count * size + rows * width + count * size * width),
        name,
    )(order, act, top)


def kept_slots(keep_order, keep_count):
    slot_ids = lax.iota(jnp.int32, keep_order.shape[-1])
    listed = keep_order[:, :, None] == slot_ids[None, None, :]
    within = slot_ids[None, :] < keep_count[:, None]
    return jnp.any(jnp.logical_and(listed, within[:, :, None]), axis=1)


def local(lay, *args):
    (
        patches,
        keep_order,
        keep_count,
        ln1_gain,
        ln1_bias,
        w_qkv,
        bias_q,
        bias_v,
        w_out,
        bias_out,
        ln2_gain,
        ln2_bias,
        w_up,
        bias_up,
        w_down,
        bias_down,
        cotangent,
    ) = args
    images, slots, width = patches.shape
    rows = images * slots
    ndev = lay.count
    own = width // ndev
    own_up = bias_up.shape[0]
    hid = own_up * ndev

    tab = lay.table()
    groups = lay.wide
    half = groups // 2
    clock = Clock(tab)

    small = jnp.concatenate(
        [ln1_gain, ln1_bias, bias_q, bias_v, bias_out, ln2_gain, ln2_bias, bias_down, bias_up]
    )[None, :]
    vec_chain = Chain(gather_small_steps(lay, small))
    qkv_chain = Chain(gather_steps(lay, w_qkv))
    out_chain = Chain(gather_steps(lay, w_out))
    up_chain = Chain(gather_steps(lay, w_up))
    down_chain = Chain(gather_steps(lay, w_down))

    def masks(_tab):
        keep_mask = kept_slots(keep_order, keep_count)
        keep_rows = keep_mask.reshape(rows, 1)
        pad_keys = jnp.pad(
            jnp.where(keep_mask, 0.0, NEG), ((0, 0), (0, 64 - slots)), constant_values=NEG
        )
        key_bias = jnp.concatenate([pad_keys, pad_keys], 1).reshape(images, 1, 128)
        return keep_rows.astype(F32), key_bias

    keep_f, key_bias = clock.tick(masks, [qkv_chain, vec_chain])
    x = clock.tick(lambda t: patches.reshape(rows, width), [qkv_chain, vec_chain])
    early = [qkv_chain, vec_chain, out_chain, up_chain]
    top = clock.tick(
        lambda t: jnp.where(keep_f > 0, cotangent.reshape(rows, width), jnp.zeros((), BF)), early
    )
    for _ in range(lay.chip_bits + lay.line_bits - 3):
        clock.tick(None, early)
    clock.tick(None, [qkv_chain, vec_chain], early)
    clock.drain(qkv_chain, vec_chain)

    vec = vec_chain.result.astype(F32)
    eight = vec[:, : 8 * own].reshape(ndev, 8, own).transpose(1, 0, 2).reshape(8, 1, width)
    gain_one, offset_one, vec_q, vec_v, vec_out, gain_two, offset_two, vec_down = eight
    vec_up = vec[:, 8 * own :].reshape(1, hid)
    vec_qkv = jnp.concatenate([vec_q, jnp.zeros_like(vec_q), vec_v], axis=1)

    qkv_pieces = qkv_chain.result
    normed_one, qkv = clock.tick(
        lambda t: qkv_product(t, x, gain_one, offset_one, vec_qkv, qkv_pieces),
        [out_chain, up_chain, down_chain],
    )
    mixed = clock.tick(
        lambda t: attention(t, qkv, key_bias, slots), [out_chain, up_chain, down_chain]
    )
    clock.drain(out_chain)
    out_pieces = out_chain.result
    residual, normed_two = clock.tick(
        lambda t: out_product(t, mixed, x, vec_out, gain_two, offset_two, out_pieces, slots),
        [up_chain, down_chain],
    )
    clock.drain(up_chain)
    up_pieces = up_chain.result
    act, slope = clock.tick(
        lambda t: up_product(t, normed_two, vec_up, up_pieces), [down_chain]
    )

    straight = jnp.arange(groups, dtype=jnp.int32)
    size = width // groups
    fits = size % 128 == 0

    def rows_of(t, part):
        if fits:
            return t[half * part : half * (part + 1)]
        return straight[part : part + 1] + 0 * t[:1]

    def placed(a):
        return a if fits else a.reshape(rows, groups, size)[:, tab].reshape(rows, width)

    many = groups if fits else 2

    give = clock.tick(
        lambda t: down_grad(straight[half:] + 0 * t[:half], act, top, groups, "down_grad_give"),
        [down_chain],
    )
    keep = []
    down_rs = Chain(scatter_steps(lay, give, keep))
    keep.append(
        clock.tick(
            lambda t: down_grad(straight[:half] + 0 * t[:half], act, top, groups, "down_grad_keep"),
            [down_rs, down_chain],
            [down_chain],
        )
    )
    clock.drain(down_chain)
    down_pieces = down_chain.result
    clock.tick(None, [], [down_rs])
    grad_hidden, sum_up = clock.tick(
        lambda t: hidden_back(t, top, slope, down_pieces), [down_rs], []
    )

    n2 = placed(normed_two)
    gh = grad_hidden[None]
    give = clock.tick(
        lambda t: weight_grad(rows_of(t, 1), n2, gh, many, "up_grad_give"), [], [down_rs]
    )
    keep = []
    up_rs = Chain(scatter_steps(lay, give, keep))
    keep.append(
        clock.tick(
            lambda t: weight_grad(rows_of(t, 0), n2, gh, many, "up_grad_keep"),
            [up_rs, down_rs],
            [],
        )
    )
    clock.tick(None, [], [up_rs])
    grad_residual, branch, grad_mixed, sums_two = clock.tick(
        lambda t: up_back(t, grad_hidden, residual, top, gain_two, up_pieces, out_pieces, slots),
        [up_rs],
        [down_rs],
    )
    mx = placed(mixed)
    give = clock.tick(
        lambda t: weight_grad(rows_of(t, 1), mx, branch[None], many, "out_grad_give"),
        [down_rs],
        [up_rs],
    )
    keep = []
    out_rs = Chain(scatter_steps(lay, give, keep))
    keep.append(
        clock.tick(
            lambda t: weight_grad(rows_of(t, 0), mx, branch[None], many, "out_grad_keep"),
            [out_rs, up_rs],
            [down_rs],
        )
    )
    clock.tick(None, [], [out_rs])
    pairs = width // 128
    half_pairs = pairs // 2
    part = clock.tick(
        lambda t: attention_back(t, qkv, key_bias, grad_mixed, slots, 0, half_pairs),
        [down_rs, out_rs],
        [up_rs, down_rs, out_rs],
    )
    grads, sums_att = clock.tick(
        lambda t: attention_back(t, qkv, key_bias, grad_mixed, slots, half_pairs, pairs, part),
        [up_rs, out_rs],
    )
    n1 = placed(normed_one)
    give = clock.tick(
        lambda t: weight_grad(rows_of(t, 1), n1, grads, many, "qkv_grad_give"),
        [up_rs, out_rs],
        [out_rs],
    )
    keep = []
    qkv_rs = Chain(scatter_steps(lay, give, keep))
    keep.append(
        clock.tick(
            lambda t: weight_grad(rows_of(t, 0), n1, grads, many, "qkv_grad_keep"),
            [qkv_rs, out_rs],
            [out_rs, up_rs],
        )
    )
    clock.tick(None, [], [qkv_rs])
    grad_patches, sums_one = clock.tick(
        lambda t: qkv_back(t, grads, x, grad_residual, gain_one, qkv_pieces, images, slots),
        [qkv_rs, out_rs, up_rs, down_rs],
    )
    eight_sums = jnp.stack(
        [
            sums_one[0],
            sums_one[1],
            sums_att[0],
            sums_att[2],
            sums_two[2],
            sums_two[0],
            sums_two[1],
            sums_two[3],
        ]
    )
    packed = jnp.concatenate(
        [
            eight_sums.reshape(8, ndev, own).transpose(1, 0, 2).reshape(ndev, 8 * own),
            sum_up.reshape(ndev, own_up),
        ],
        axis=1,
    )
    vec_rs = Chain(scatter_small_steps(lay, packed))
    late = [qkv_rs, vec_rs, out_rs, up_rs, down_rs]
    shape = (images, slots, width)
    block_out = None
    for i in range(images // IMG_BLOCK):
        block_out = clock.tick(
            lambda t: down_product(
                t, act, residual, vec_down, keep_f, down_pieces, shape, i, i + 1, block_out
            ),
            late,
        )
    clock.drain(*late)
    mine = vec_rs.result
    vecs = [mine[own * i : own * (i + 1)] for i in range(8)]
    return (
        block_out.transpose(1, 0, 2),
        grad_patches.transpose(1, 0, 2),
        vecs[0],
        vecs[1],
        qkv_rs.result,
        vecs[2],
        vecs[3],
        out_rs.result,
        vecs[4],
        vecs[5],
        vecs[6],
        up_rs.result,
        mine[8 * own :],
        down_rs.result,
        vecs[7],
    )


def solution(mesh):
    both = P(AXES)
    mat = P(AXES, None)
    cube = P(AXES, None, None)
    in_specs = (
        cube, mat, both, both, both, mat, both, both, mat, both, both, both, mat, both, mat, both,
        cube,
    )
    out_specs = (
        cube, cube, both, both, mat, both, both, mat, both, both, both, mat, both, mat, both,
    )
    return jax.shard_map(
        functools.partial(local, Layout(mesh)),
        mesh=mesh,
        in_specs=in_specs,
        out_specs=out_specs,
        check_vma=False,
    )
```

```python
import functools

import jax
import jax.numpy as jnp
import numpy as np
from jax import lax
from jax.experimental import pallas as pl
from jax.experimental.pallas import tpu as pltpu
from jax.sharding import PartitionSpec as P

HEADS = 16
EPS = 1e-06
AXES = ("wide", "narrow")
BF = jnp.bfloat16
F32 = jnp.float32
NEG = -1e30
VMEM_LIMIT = 62 << 20
IMG_BLOCK = 8
LN1_GAIN, LN1_BIAS, BIAS_Q, BIAS_V, BIAS_OUT, LN2_GAIN, LN2_BIAS, BIAS_DOWN, BIAS_UP = range(9)
VECS = 16
LOW = 1000


class Layout:
    def __init__(self, mesh):
        self.wide = mesh.shape["wide"]
        self.narrow = mesh.shape["narrow"]
        self.count = self.wide * self.narrow
        self.chip_bits = (self.wide // 2).bit_length() - 1
        self.line_bits = self.narrow.bit_length() - 1

    def bit_of(self, core, level):
        return level if core == 0 else self.chip_bits - 1 - level

    def flip(self, core, piece):
        total = 0
        for level in range(self.chip_bits):
            if piece >> level & 1:
                total ^= 1 << self.bit_of(core, level)
        return total

    def swap_line(self, bit):
        return [(d, d ^ (1 << bit)) for d in range(self.count)]

    def swap_core(self):
        return [(d, d ^ self.narrow) for d in range(self.count)]

    def swap_chip(self, level):
        pairs = []
        for d in range(self.count):
            place, line = divmod(d, self.narrow)
            chip, core = divmod(place, 2)
            other = chip ^ (1 << self.bit_of(core, level))
            pairs.append((d, (other * 2 + core) * self.narrow + line))
        return pairs

    def shift_line(self, by):
        return [(d, d ^ by) for d in range(self.count)]

    def shift_chip(self, by):
        return [(d, d ^ (2 * self.narrow * by)) for d in range(self.count)]

    def swap_chip_bit(self, bit):
        return [(d, d ^ (2 * self.narrow << bit)) for d in range(self.count)]

    def table(self):
        place = lax.axis_index("wide")
        chip, core = place // 2, place % 2
        half = 1 << self.chip_bits
        even = np.array([self.flip(0, q) for q in range(half)], np.int32)
        odd = np.array([self.flip(1, q) for q in range(half)], np.int32)
        mine = jnp.where(core == 0, even, odd)
        other = jnp.where(core == 0, odd, even)
        return jnp.concatenate(
            [(chip ^ mine) * 2 + core, (chip ^ other) * 2 + (1 - core)]
        ).astype(jnp.int32)


def move(x, pairs):
    return lax.ppermute(x, AXES, pairs)


def gather_steps(lay, x, join=None):
    x = yield from gather_line_steps(lay, x, join)
    parts = [x]
    for level in range(lay.chip_bits):
        x = parts[0] if len(parts) == 1 else jnp.concatenate(parts, 0)
        if level < lay.chip_bits - 1:
            (got,) = yield [(x, lay.swap_chip(level))]
            parts = [x, got]
        else:
            got, other = yield [(x, lay.swap_chip(level)), (x, lay.swap_core())]
    (last,) = yield [(got, lay.swap_core())]
    return [x, got, other, last]


def vector_step(lay, v, join):
    (got,) = yield [(v[None], lay.swap_line(lay.line_bits - 1))]
    join.append((v[None], got))


def gather_line_steps(lay, x, join=None):
    line = lax.axis_index("narrow")
    x = x[None]
    for b in reversed(range(lay.line_bits)):
        (got,) = yield [(x, lay.swap_line(b))]
        if join:
            mine, theirs = join.pop()
            x, got = jnp.concatenate([x, mine], -1), jnp.concatenate([got, theirs], -1)
        bit = (line >> b) & 1
        a, c = x[:, None], got[:, None]
        both = jnp.where(bit == 0, jnp.concatenate([a, c], 1), jnp.concatenate([c, a], 1))
        x = both.reshape(-1, *x.shape[1:])
    return x.reshape(-1, x.shape[-1])


def total(terms, dtype=BF):
    out = terms[0].astype(F32)
    for t in terms[1:]:
        out += t.astype(F32)
    return out.astype(dtype)


def scatter_line_steps(lay, terms, dtype=BF):
    line = lax.axis_index("narrow")
    own, cols = terms[0].shape[0] // lay.narrow, terms[0].shape[1]
    terms = [t.reshape((2,) * lay.line_bits + (own, cols)) for t in terms]
    for b in range(lay.line_bits):
        bit, axis = (line >> b) & 1, lay.line_bits - 1 - b
        give = [lax.dynamic_index_in_dim(t, 1 - bit, axis, False) for t in terms]
        (got,) = yield [(total(give, dtype), lay.swap_line(b))]
        terms = [lax.dynamic_index_in_dim(t, bit, axis, False) for t in terms] + [got]
    return total(terms, F32)


def scatter_steps(lay, give, keep):
    (got,) = yield [(give, lay.swap_core())]
    terms = [keep[0], got]
    for level in reversed(range(lay.chip_bits)):
        size = terms[0].shape[0] // 2
        (got,) = yield [(total([t[size:] for t in terms]), lay.swap_chip(level))]
        terms = [t[:size] for t in terms] + [got]
    return (yield from scatter_line_steps(lay, [total(terms)]))


def swap_step(lay, give):
    (got,) = yield [(give, lay.swap_core())]
    return got


def scatter_rest(lay, low, high):
    terms, give = [low], high
    for level in reversed(range(lay.chip_bits)):
        if give is None:
            size = terms[0].shape[0] // 2
            give = total([t[size:] for t in terms])
            terms = [t[:size] for t in terms]
        (got,) = yield [(give, lay.swap_chip(level))]
        terms, give = terms + [got], None
    return (yield from scatter_line_steps(lay, [total(terms)]))


def direct(x, at, pairs):
    gives = [
        (lax.dynamic_index_in_dim(x, at ^ k, 0, False), pairs(k)) for k in range(1, x.shape[0])
    ]
    got = yield gives
    return total([lax.dynamic_index_in_dim(x, at, 0, False)] + list(got), F32)


def scatter_small_steps(lay, x):
    place, line = lax.axis_index("wide"), lax.axis_index("narrow")
    cols = x.shape[1]
    x = x.reshape(lay.wide // 2, -1, cols)
    x = yield from direct(x, place // 2, lay.shift_chip)
    x = x.reshape(2, lay.narrow, cols)
    x = yield from direct(x, place % 2, lambda k: lay.swap_core())
    return (yield from direct(x, line, lay.shift_line))


class Chain:
    def __init__(self, steps):
        self.steps = steps
        self.want = next(steps)
        self.flying = None
        self.result = None

    def take(self, got):
        self.flying = None
        try:
            self.want = self.steps.send(got)
        except StopIteration as end:
            self.want, self.result = None, end.value


class Clock:
    def __init__(self, tab):
        self.tab = tab
        self.chains = []

    def begin(self, *chains):
        for c in chains:
            if c.want is None or c.flying is not None:
                continue
            operands, self.tab = lax.optimization_barrier(([w[0] for w in c.want], self.tab))
            c.flying = [move(x, w[1]) for x, w in zip(operands, c.want)]

    def tick(self, compute=None, start=(), finish=None):
        self.begin(*start)
        out = compute(self.tab) if compute is not None else ()
        done = [c for c in (start if finish is None else finish) if c.flying is not None]
        self.tab, got, out = lax.optimization_barrier((self.tab, [c.flying for c in done], out))
        for c, g in zip(done, got):
            c.take(g)
        return out

    def drain(self, *chains):
        while any(c.want is not None for c in chains):
            self.tick(None, chains)


def dot_nn(a, b):
    return jnp.dot(a, b, preferred_element_type=F32)


def dot_nt(a, b):
    return lax.dot_general(a, b, (((1,), (1,)), ((), ())), preferred_element_type=F32)


def dot_tn(a, b):
    return lax.dot_general(a, b, (((0,), (0,)), ((), ())), preferred_element_type=F32)


def normalize(r):
    center = r - jnp.mean(r, axis=-1, keepdims=True)
    spread = jnp.mean(center * center, axis=-1, keepdims=True)
    rinv = lax.rsqrt(spread + EPS)
    return center * rinv, rinv


def norm_back(up, gain, n, rinv):
    u = up * gain
    return rinv * (
        u - jnp.mean(u, axis=-1, keepdims=True) - n * jnp.mean(u * n, axis=-1, keepdims=True)
    )


def col_sum(x):
    return jnp.sum(x, axis=0, keepdims=True)


def call(body, outs, grid, in_specs, out_specs, scratch, flops, nbytes, name, trans=0, aliases={}):
    return pl.pallas_call(
        body,
        out_shape=outs,
        grid_spec=pltpu.PrefetchScalarGridSpec(
            num_scalar_prefetch=1,
            grid=grid,
            in_specs=in_specs,
            out_specs=out_specs,
            scratch_shapes=scratch,
        ),
        compiler_params=pltpu.CompilerParams(vmem_limit_bytes=VMEM_LIMIT),
        cost_estimate=pl.CostEstimate(
            flops=flops // LOW, bytes_accessed=nbytes // LOW, transcendentals=trans // LOW
        ),
        name=name,
        input_output_aliases=aliases,
    )


def full(shape):
    zeros = (0,) * len(shape)
    return pl.BlockSpec(shape, lambda *_: zeros)


def anywhere(count):
    return [pl.BlockSpec(memory_space=pl.ANY)] * count


def sds(shape, dtype):
    return jax.ShapeDtypeStruct(shape, dtype)


def fill_tile(tab, pieces, tile, size):
    per = pieces[0].shape[0] // size
    for a, piece in enumerate(pieces):
        for i in range(per):
            at = pl.multiple_of(tab[a * per + i] * size, size)
            tile[pl.ds(at, size), :] = piece[i * size : (i + 1) * size, :]


def load_copies(tab, pieces, store, sem, size, columns=slice(None)):
    per = pieces[0].shape[0] // size
    copies = []
    for a, piece in enumerate(pieces):
        for i in range(per):
            at = pl.multiple_of(tab[a * per + i] * size, size)
            copies.append(
                pltpu.make_async_copy(
                    piece.at[pl.ds(i * size, size), columns],
                    store.at[pl.ds(at, size)],
                    sem.at[a * per + i],
                )
            )
    return copies


def by_slot(y, o_ref, turn, slots):
    for b in range(IMG_BLOCK):
        turn[:, b, :] = y[slots * b : slots * (b + 1)]
    o_ref[...] = turn[...].astype(BF)


def row_chunk(rows):
    for size in (240, 200, 160, 80, 48, 16):
        if rows % size == 0:
            return size
    return rows


def qkv_product(tab, x, pieces):
    rows, width = x.shape
    tn = width // 2
    count = len(pieces)
    size = pieces[0].shape[0]
    chunk = row_chunk(rows)

    def body(tab_ref, x_ref, *rest):
        piece_refs, vec_refs = rest[:count], rest[count : 2 * count]
        n_ref, o_ref, v_ref, tile, cols = rest[2 * count :]
        j = pl.program_id(0)

        @pl.when(j == 0)
        def _():
            fill_tile(tab_ref, vec_refs, cols, width // tab.shape[0])
            v_ref[...] = cols[...].astype(F32).T[0:VECS]

            @pl.loop(0, rows // chunk)
            def _(i):
                at = pl.ds(pl.multiple_of(i * chunk, chunk), chunk)
                n, _unused = normalize(x_ref[at, :].astype(F32))
                n_ref[at, :] = (n * vec(v_ref, LN1_GAIN) + vec(v_ref, LN1_BIAS)).astype(BF)

        fill_tile(tab_ref, piece_refs, tile, width // tab.shape[0])
        part = vec(v_ref, BIAS_Q), jnp.zeros((1, width), F32), vec(v_ref, BIAS_V)
        bias = jnp.zeros((1, tn), F32)
        for at in range(6):
            lo = at % 2 * tn
            bias = jnp.where(j == at, part[at // 2][:, lo : lo + tn], bias)
        o_ref[...] = (dot_nn(n_ref[...], tile[...]) + bias).astype(BF)

    return call(
        body,
        (sds((rows, width), BF), sds((rows, 3 * width), BF), sds((VECS, width), F32)),
        (6,),
        [full((rows, width))]
        + [pl.BlockSpec((size, tn), lambda j, t: (0, j))] * count
        + [pl.BlockSpec((size, 128), lambda j, t: (0, 6 * tn // 128))] * count,
        (
            full((rows, width)),
            pl.BlockSpec((rows, tn), lambda j, t: (0, j)),
            full((VECS, width)),
        ),
        [pltpu.VMEM((width, tn), BF), pltpu.VMEM((width, 128), BF)],
        6 * rows * width * width,
        2 * (5 * rows * width + 3 * width * width),
        "qkv_product",
    )(tab, x, *pieces, *pieces)


def two_heads(x, lane):
    return jnp.concatenate([jnp.where(lane < 64, x, 0.0), jnp.where(lane < 64, 0.0, x)], 0).astype(
        BF
    )


def half_max(s, low):
    a = jnp.max(jnp.where(low, s, NEG), axis=-1, keepdims=True)
    b = jnp.max(jnp.where(low, NEG, s), axis=-1, keepdims=True)
    return jnp.where(low, a, b)


def half_sum(s, ones):
    high = s.astype(BF)
    rest = (s - high.astype(F32)).astype(BF)
    return dot_nn(high, ones) + dot_nn(rest, ones)


def softmax_pair(s, low, ones):
    e = jnp.exp(s - half_max(s, low))
    return e / half_sum(e, ones)


def head_ones():
    row = lax.broadcasted_iota(jnp.int32, (128, 128), 0) < 64
    col = lax.broadcasted_iota(jnp.int32, (128, 128), 1) < 64
    return jnp.where(row == col, 1.0, 0.0).astype(BF)


def attention(tab, qkv, key_bias, slots, first, last, before=()):
    rows, three = qkv.shape
    width = three // 3
    pairs = width // 128
    blk = IMG_BLOCK * slots
    pad = -(-slots // 8) * 8
    scale = float(64**-0.5)

    def body(tab_ref, q_ref, k_ref, v_ref, kb_ref, *rest):
        o_ref, qf, kf, vf, of, sf = rest[len(before) :]
        for ref, src in ((qf, q_ref), (kf, k_ref), (vf, v_ref)):
            ref[0:blk, :] = src[...].astype(F32)
            ref[blk : blk + 16, :] = jnp.zeros((16, 128), F32)
        lane = lax.broadcasted_iota(jnp.int32, (64, 128), 1)
        low = lax.broadcasted_iota(jnp.int32, (pad, 128), 1) < 64
        ones = head_ones()
        for b in range(IMG_BLOCK):
            at = slots * b
            kk = two_heads(kf[at : at + 64, :], lane)
            q = qf[at : at + pad, :].astype(BF)
            sf[pad * b : pad * (b + 1), :] = dot_nt(q, kk) * scale + kb_ref[b]
        low = lax.broadcasted_iota(jnp.int32, (pad * IMG_BLOCK, 128), 1) < 64
        p = softmax_pair(sf[...], low, ones)
        outs = []
        for b in range(IMG_BLOCK):
            at = slots * b
            vv = two_heads(vf[at : at + 64, :], lane)
            outs.append(dot_nn(p[pad * b : pad * (b + 1)].astype(BF), vv))
        for b in range(IMG_BLOCK):
            at = slots * b
            of[at : at + pad, :] = outs[b]
        o_ref[...] = of[0:blk, :].astype(BF)

    return call(
        body,
        sds((rows, width), BF),
        (last - first, rows // blk),
        [
            pl.BlockSpec((blk, 128), lambda h, i, t: (i, h + first)),
            pl.BlockSpec((blk, 128), lambda h, i, t: (i, h + first + pairs)),
            pl.BlockSpec((blk, 128), lambda h, i, t: (i, h + first + 2 * pairs)),
            pl.BlockSpec((IMG_BLOCK, 1, 128), lambda h, i, t: (i, 0, 0)),
        ]
        + anywhere(len(before)),
        pl.BlockSpec((blk, 128), lambda h, i, t: (i, h + first)),
        [pltpu.VMEM((blk + 16, 128), F32)] * 4 + [pltpu.VMEM((pad * IMG_BLOCK, 128), F32)],
        8 * rows * 128 * width * 2 * (last - first) // pairs,
        2 * 4 * rows * width * (last - first) // pairs,
        "attention",
        aliases={5: 0} if before else {},
    )(tab, qkv, qkv, qkv, key_bias, *before)


def attention_back(tab, qkv, key_bias, grad_mixed, slots, first, last, before=()):
    rows, three = qkv.shape
    width = three // 3
    pairs = width // 128
    blk = IMG_BLOCK * slots
    pad = -(-slots // 8) * 8
    tall = pad * IMG_BLOCK
    scale = float(64**-0.5)

    def body(tab_ref, q_ref, k_ref, v_ref, kb_ref, g_ref, *rest):
        o_ref, s_ref, qf, kf, vf, gf, dqf, dkf, dvf, sf, pf = rest[len(before) :]
        for ref, src in ((qf, q_ref), (kf, k_ref), (vf, v_ref), (gf, g_ref)):
            ref[0:blk, :] = src[...].astype(F32)
            ref[blk : blk + 16, :] = jnp.zeros((16, 128), F32)
        lane = lax.broadcasted_iota(jnp.int32, (64, 128), 1)
        low = lax.broadcasted_iota(jnp.int32, (pad, 128), 1) < 64
        real = lax.broadcasted_iota(jnp.int32, (pad, 128), 0) < slots
        ones = head_ones()
        kks, qs, gs = [], [], []
        for b in range(IMG_BLOCK):
            at = slots * b
            kks.append(two_heads(kf[at : at + 64, :], lane))
            vv = two_heads(vf[at : at + 64, :], lane)
            qs.append(jnp.where(real, qf[at : at + pad, :], 0.0).astype(BF))
            gs.append(jnp.where(real, gf[at : at + pad, :], 0.0).astype(BF))
            sf[pad * b : pad * (b + 1), :] = dot_nt(qs[b], kks[b]) * scale + kb_ref[b]
            pf[pad * b : pad * (b + 1), :] = dot_nt(gs[b], vv)
        p = softmax_pair(sf[...], lax.broadcasted_iota(jnp.int32, (tall, 128), 1) < 64, ones)
        dp = pf[...]
        ds = p * (dp - half_sum(p * dp, ones))
        res = []
        for b in range(IMG_BLOCK):
            d = ds[pad * b : pad * (b + 1)].astype(BF)
            w = p[pad * b : pad * (b + 1)].astype(BF)
            res.append((dot_nn(d, kks[b]), dot_tn(d, qs[b]), dot_tn(w, gs[b])))
        for b in range(IMG_BLOCK):
            at = slots * b
            dq, dk, dv = res[b]
            dqf[at : at + pad, :] = dq * scale
            dkf[at : at + pad, :] = jnp.where(low, dk[0:pad], dk[64 : 64 + pad]) * scale
            dvf[at : at + pad, :] = jnp.where(low, dv[0:pad], dv[64 : 64 + pad])

        @pl.when(pl.program_id(1) == 0)
        def _():
            s_ref[...] = jnp.zeros_like(s_ref)

        for at, ref in enumerate((dqf, dkf, dvf)):
            rounded = ref[0:blk, :].astype(BF)
            o_ref[at] = rounded
            if at != 1:
                s_ref[at : at + 1, :] += col_sum(rounded.astype(F32))

    def pair(skip):
        return pl.BlockSpec((blk, 128), lambda h, i, t: (i, h + first + skip))

    return call(
        body,
        (sds((3, rows, width), BF), sds((8, width), F32)),
        (last - first, rows // blk),
        [
            pair(0),
            pair(pairs),
            pair(2 * pairs),
            pl.BlockSpec((IMG_BLOCK, 1, 128), lambda h, i, t: (i, 0, 0)),
            pair(0),
        ]
        + anywhere(len(before)),
        (
            pl.BlockSpec((3, blk, 128), lambda h, i, t: (0, i, h + first)),
            pl.BlockSpec((8, 128), lambda h, i, t: (0, h + first)),
        ),
        [pltpu.VMEM((blk + 16, 128), F32)] * 7 + [pltpu.VMEM((tall, 128), F32)] * 2,
        20 * rows * 128 * width * 2 * (last - first) // pairs,
        2 * 7 * rows * width * (last - first) // pairs,
        "attention_back",
        aliases={6: 0, 7: 1} if before else {},
    )(tab, qkv, qkv, qkv, key_bias, grad_mixed, *before)


def vec(ref, at):
    return ref[at : at + 1, :]


def out_product(tab, mixed, x, vecs, pieces, slots):
    rows, width = mixed.shape
    blk = IMG_BLOCK * slots
    count = len(pieces)

    def body(tab_ref, m_ref, x_ref, v_ref, *rest):
        piece_refs, (r_ref, n_ref, store, sem) = rest[:count], rest[count:]

        @pl.when(pl.program_id(0) == 0)
        def _():
            copies = load_copies(tab_ref, piece_refs, store, sem, width // tab.shape[0])
            for c in copies:
                c.start()
            for c in copies:
                c.wait()

        r = x_ref[...].astype(F32) + dot_nn(m_ref[...], store[...]) + vec(v_ref, BIAS_OUT)
        r_ref[...] = r
        n, _unused = normalize(r)
        n_ref[...] = (n * vec(v_ref, LN2_GAIN) + vec(v_ref, LN2_BIAS)).astype(BF)

    spec = pl.BlockSpec((blk, width), lambda i, t: (i, 0))
    return call(
        body,
        (sds((rows, width), F32), sds((rows, width), BF)),
        (rows // blk,),
        [spec, spec, full((VECS, width))] + anywhere(count),
        (spec, spec),
        [pltpu.VMEM((width, width), BF), pltpu.SemaphoreType.DMA((tab.shape[0],))],
        2 * rows * width * width,
        10 * rows * width + 2 * width * width,
        "out_product",
    )(tab, mixed, x, vecs, *pieces)


def up_product(tab, n2, bias_up, pieces, first, last, before=()):
    rows, width = n2.shape
    hid = pieces[0].shape[1]
    count = len(pieces)
    groups = tab.shape[0]
    tn = hid // groups
    size = pieces[0].shape[0]

    def body(tab_ref, n_ref, c_ref, *rest):
        piece_refs, (a_ref, d_ref, tile) = rest[:count], rest[count + len(before) :]
        fill_tile(tab_ref, piece_refs, tile, width // groups)
        u = dot_nn(n_ref[...], tile[...]) + c_ref[...]
        phi = 0.5 + 0.5 * lax.erf(u * np.float32(0.5**0.5))
        a_ref[...] = (u * phi).astype(BF)
        slope = phi + u * jnp.exp(-0.5 * u * u) * np.float32((2 * np.pi) ** -0.5)
        d_ref[...] = slope.astype(BF)

    spec = pl.BlockSpec((rows, tn), lambda p, t: (0, p + first))
    return call(
        body,
        (sds((rows, hid), BF), sds((rows, hid), BF)),
        (last - first,),
        [full((rows, width)), pl.BlockSpec((1, tn), lambda p, t: (0, t[p + first]))]
        + [pl.BlockSpec((size, tn), lambda p, t: (0, t[p + first]))] * count
        + anywhere(len(before)),
        (spec, spec),
        [pltpu.VMEM((width, tn), BF)],
        2 * rows * width * hid + 30 * rows * hid,
        2 * (rows * width + 2 * rows * hid + width * hid),
        "up_product",
        2 * rows * hid,
        {3 + count: 0, 4 + count: 1} if before else {},
    )(tab, n2, bias_up, *pieces, *before)


def down_product(tab, act, residual, vecs, keep, pieces, shape, first, last, before=None):
    images, slots, width = shape
    rows, hid = act.shape
    blk = IMG_BLOCK * slots
    count = len(pieces)
    size = pieces[0].shape[0]

    def body(tab_ref, a_ref, r_ref, v_ref, k_ref, *rest):
        piece_refs, (o_ref, store, turn, sem) = rest[:count], rest[-4:]

        def dma(p):
            return pltpu.make_async_copy(
                piece_refs[p], store.at[pl.ds(p * size, size)], sem.at[p]
            )

        @pl.when(pl.program_id(0) == 0)
        def _():
            for p in range(count):
                dma(p).start()
            if last - first > 1:
                for p in range(count):
                    dma(p).wait()

        y = r_ref[...] + vec(v_ref, BIAS_DOWN)
        for p in range(count):
            if last - first == 1:
                dma(p).wait()
            part = slice(p * size, (p + 1) * size)
            y += dot_nn(a_ref[:, part], store[part, :])
        y = jnp.where(k_ref[...] > 0.0, y, 0.0)
        by_slot(y, o_ref, turn, slots)

    share = blk * (last - first)
    more = [] if before is None else [before]
    return call(
        body,
        sds((slots, images, width), BF),
        (last - first,),
        [
            pl.BlockSpec((blk, hid), lambda i, t: (i + first, 0)),
            pl.BlockSpec((blk, width), lambda i, t: (i + first, 0)),
            full((VECS, width)),
            pl.BlockSpec((blk, 1), lambda i, t: (i + first, 0)),
        ]
        + anywhere(count + len(more)),
        pl.BlockSpec((slots, IMG_BLOCK, width), lambda i, t: (0, i + first, 0)),
        [
            pltpu.VMEM((hid, width), BF),
            pltpu.VMEM((slots, IMG_BLOCK, width), F32),
            pltpu.SemaphoreType.DMA((count,)),
        ],
        2 * share * width * hid,
        2 * (share * hid + 3 * share * width + width * hid),
        "down_product",
        aliases={} if before is None else {5 + count: 0},
    )(tab, act, residual, vecs, keep, *pieces, *more)


def hidden_back(tab, top, slope, pieces):
    rows, width = top.shape
    hid = slope.shape[1]
    count = len(pieces)
    groups = tab.shape[0]
    tn = hid // groups
    per = groups // count

    def body(tab_ref, t_ref, d_ref, *rest):
        piece_refs, (o_ref, s_ref, store, sem) = rest[:count], rest[count:]
        p = pl.program_id(0)
        copies = [
            pltpu.make_async_copy(
                piece_refs[g // per].at[pl.ds(g % per * tn, tn)], store.at[g], sem.at[g]
            )
            for g in range(groups)
        ]

        @pl.when(p == 0)
        def _():
            for c in copies:
                c.start()

        pltpu.make_async_copy(store.at[p], store.at[p], sem.at[p]).wait()
        g = (dot_nt(t_ref[...], store[p]) * d_ref[...].astype(F32)).astype(BF)
        o_ref[...] = g
        s_ref[...] = col_sum(g.astype(F32))

    spec = pl.BlockSpec((rows, tn), lambda p, t: (0, p))
    return call(
        body,
        (sds((rows, hid), BF), sds((1, hid), F32)),
        (groups,),
        [full((rows, width)), spec] + anywhere(count),
        (
            pl.BlockSpec((rows, tn), lambda p, t: (0, t[p])),
            pl.BlockSpec((1, tn), lambda p, t: (0, t[p])),
        ),
        [pltpu.VMEM((groups, tn, width), BF), pltpu.SemaphoreType.DMA((groups,))],
        2 * rows * width * hid,
        2 * (rows * width + 2 * rows * hid + width * hid),
        "hidden_back",
    )(tab, top, slope, *pieces)


def up_back(tab, grad_hidden, residual, top, vecs, pieces, out_pieces, slots):
    rows, hid = grad_hidden.shape
    width = residual.shape[1]
    count = len(pieces)
    groups = tab.shape[0]
    blk = IMG_BLOCK * slots

    def body(tab_ref, h_ref, r_ref, t_ref, v_ref, *rest):
        piece_refs, out_refs = rest[:count], rest[count : 2 * count]
        gr_ref, gb_ref, gm_ref, s_ref, up_store, store, up_sem, sem = rest[2 * count :]

        @pl.when(pl.program_id(0) == 0)
        def _():
            ups = load_copies(tab_ref, piece_refs, up_store, up_sem, width // groups)
            outs = load_copies(tab_ref, out_refs, store, sem, width // groups)
            for c in ups + outs:
                c.start()
            s_ref[...] = jnp.zeros_like(s_ref)
            for c in ups + outs:
                c.wait()

        up = dot_nt(h_ref[...], up_store[...])
        n, rinv = normalize(r_ref[...])
        top_rows = t_ref[...].astype(F32)
        grad = top_rows + norm_back(up, vec(v_ref, LN2_GAIN), n, rinv)
        branch = grad.astype(BF)
        gr_ref[...] = grad
        gb_ref[...] = branch
        gm_ref[...] = dot_nt(branch, store[...]).astype(BF)
        s_ref[0:1, :] += col_sum(up * n)
        s_ref[1:2, :] += col_sum(up)
        s_ref[2:3, :] += col_sum(branch.astype(F32))
        s_ref[3:4, :] += col_sum(top_rows)

    spec = pl.BlockSpec((blk, width), lambda i, t: (i, 0))
    return call(
        body,
        (
            sds((rows, width), F32),
            sds((rows, width), BF),
            sds((rows, width), BF),
            sds((8, width), F32),
        ),
        (rows // blk,),
        [pl.BlockSpec((blk, hid), lambda i, t: (i, 0)), spec, spec, full((VECS, width))]
        + anywhere(2 * count),
        (spec, spec, spec, full((8, width))),
        [
            pltpu.VMEM((width, hid), BF),
            pltpu.VMEM((width, width), BF),
            pltpu.SemaphoreType.DMA((groups,)),
            pltpu.SemaphoreType.DMA((groups,)),
        ],
        2 * rows * width * (hid + width),
        2 * (rows * hid + 8 * rows * width + width * hid),
        "up_back",
    )(tab, grad_hidden, residual, top, vecs, *pieces, *out_pieces)


def qkv_back(tab, grads, x, grad_residual, vecs, pieces, images, slots):
    _three, rows, width = grads.shape
    blk = IMG_BLOCK * slots
    count = len(pieces)
    groups = tab.shape[0]

    def body(tab_ref, d_ref, x_ref, r_ref, v_ref, *rest):
        piece_refs, (o_ref, s_ref, store, turn, sem) = rest[:count], rest[count:]

        @pl.when(pl.program_id(0) == 0)
        def _():
            copies = load_copies(
                tab_ref, piece_refs, store, sem, width // groups, pl.ds(0, 3 * width)
            )
            for c in copies:
                c.start()
            s_ref[...] = jnp.zeros_like(s_ref)
            for c in copies:
                c.wait()

        up = dot_nt(d_ref[0], store[:, 0:width])
        up += dot_nt(d_ref[1], store[:, width : 2 * width])
        up += dot_nt(d_ref[2], store[:, 2 * width :])
        n, rinv = normalize(x_ref[...].astype(F32))
        y = r_ref[...] + norm_back(up, vec(v_ref, LN1_GAIN), n, rinv)
        s_ref[0:1, :] += col_sum(up * n)
        s_ref[1:2, :] += col_sum(up)
        by_slot(y, o_ref, turn, slots)

    spec = pl.BlockSpec((blk, width), lambda i, t: (i, 0))
    return call(
        body,
        (sds((slots, images, width), BF), sds((8, width), F32)),
        (rows // blk,),
        [pl.BlockSpec((3, blk, width), lambda i, t: (0, i, 0)), spec, spec, full((VECS, width))]
        + anywhere(count),
        (pl.BlockSpec((slots, IMG_BLOCK, width), lambda i, t: (0, i, 0)), full((8, width))),
        [
            pltpu.VMEM((width, 3 * width), BF),
            pltpu.VMEM((slots, IMG_BLOCK, width), F32),
            pltpu.SemaphoreType.DMA((groups,)),
        ],
        6 * rows * width * width,
        2 * (3 * rows * width + 4 * rows * width + 3 * width * width),
        "qkv_back",
    )(tab, grads, x, grad_residual, vecs, *pieces)


def weight_grad(order, x, g, pieces_of, name, got=None):
    parts, rows, width = g.shape
    count = order.shape[0]
    size = x.shape[1] // pieces_of
    tall = count * size
    tn = min(width, 1024)
    per = width // tn
    more = [] if got is None else [got]

    def body(tab_ref, *rest):
        x_refs, g_ref, (*o_refs, xs) = rest[:count], rest[count], rest[count + 1 + len(more) :]

        @pl.when(pl.program_id(0) == 0)
        def _():
            for p in range(count):
                xs[:, size * p : size * (p + 1)] = x_refs[p][...]

        y = dot_tn(xs[...], g_ref[0])
        if got is None:
            o_refs[0][...] = y.astype(BF)
        else:
            y += rest[count + 1][...].astype(F32)
            o_refs[0][...] = y[: tall // 2].astype(BF)
            o_refs[1][...] = y[tall // 2 :].astype(BF)

    def column(p):
        return lambda j, t: (0, t[p])

    def part(height):
        return pl.BlockSpec((height, tn), lambda j, t: (0, j))

    if got is None:
        outs, out_specs = sds((tall, parts * width), BF), part(tall)
    else:
        outs, out_specs = (sds((tall // 2, parts * width), BF),) * 2, (part(tall // 2),) * 2
    return call(
        body,
        outs,
        (parts * per,),
        [pl.BlockSpec((rows, size), column(p)) for p in range(count)]
        + [pl.BlockSpec((1, rows, tn), lambda j, t: (j // per, 0, j % per))]
        + [part(tall)] * len(more),
        out_specs,
        [pltpu.VMEM((rows, tall), BF)],
        2 * rows * tall * parts * width,
        2 * (rows * tall + parts * rows * width + tall * parts * width),
        name,
    )(order, *([x] * count), g, *more)


def down_grad(order, act, top, pieces_of, name):
    rows, hid = act.shape
    width = top.shape[1]
    count = order.shape[0]
    size = hid // pieces_of

    def body(tab_ref, a_ref, t_ref, o_ref):
        o_ref[...] = dot_tn(a_ref[...], t_ref[...]).astype(BF)

    return call(
        body,
        sds((count * size, width), BF),
        (count,),
        [pl.BlockSpec((rows, size), lambda p, t: (0, t[p])), full((rows, width))],
        pl.BlockSpec((size, width), lambda p, t: (p, 0)),
        [],
        2 * rows * count * size * width,
        2 * (rows * count * size + rows * width + count * size * width),
        name,
    )(order, act, top)


def kept_slots(keep_order, keep_count):
    slot_ids = lax.iota(jnp.int32, keep_order.shape[-1])
    listed = keep_order[:, :, None] == slot_ids[None, None, :]
    within = slot_ids[None, :] < keep_count[:, None]
    return jnp.any(jnp.logical_and(listed, within[:, :, None]), axis=1)


def local(lay, *args):
    (
        patches,
        keep_order,
        keep_count,
        ln1_gain,
        ln1_bias,
        w_qkv,
        bias_q,
        bias_v,
        w_out,
        bias_out,
        ln2_gain,
        ln2_bias,
        w_up,
        bias_up,
        w_down,
        bias_down,
        cotangent,
    ) = args
    images, slots, width = patches.shape
    rows = images * slots
    ndev = lay.count
    own = width // ndev
    own_up = bias_up.shape[0]
    hid = own_up * ndev

    tab = lay.table()
    groups = lay.wide
    half = groups // 2
    clock = Clock(tab)

    ups = own_up // own
    vectors = [ln1_gain, ln1_bias, bias_q, bias_v, bias_out, ln2_gain, ln2_bias, bias_down]
    columns = jnp.concatenate([jnp.stack(vectors), bias_up.reshape(ups, own)])
    columns = jnp.pad(columns.T, ((0, 0), (0, 128 - 8 - ups)))
    join = []
    qkv_chain = Chain(gather_steps(lay, w_qkv, join))
    vec_chain = Chain(vector_step(lay, columns, join))
    out_chain = Chain(gather_steps(lay, w_out))
    up_chain = Chain(gather_steps(lay, w_up))
    down_chain = Chain(gather_steps(lay, w_down))

    def masks(_tab):
        keep_mask = kept_slots(keep_order, keep_count)
        keep_rows = keep_mask.reshape(rows, 1)
        pad_keys = jnp.pad(
            jnp.where(keep_mask, 0.0, NEG), ((0, 0), (0, 64 - slots)), constant_values=NEG
        )
        key_bias = jnp.concatenate([pad_keys, pad_keys], 1).reshape(images, 1, 128)
        return keep_rows.astype(F32), key_bias

    def after(t, a):
        return lax.optimization_barrier((a, t))[0]

    keep_f, key_bias = clock.tick(masks, [qkv_chain, vec_chain], [vec_chain, qkv_chain])
    clock.tick(None, [qkv_chain])
    for _ in range(lay.chip_bits + lay.line_bits - 4):
        clock.tick(None, [qkv_chain])
    x = clock.tick(
        lambda t: after(t, patches).reshape(rows, width),
        [qkv_chain, out_chain, up_chain],
        [qkv_chain, out_chain],
    )
    top = clock.tick(
        lambda t: jnp.where(
            keep_f > 0, after(t, cotangent).reshape(rows, width), jnp.zeros((), BF)
        ),
        [qkv_chain, out_chain],
        [qkv_chain, out_chain, up_chain],
    )
    clock.tick(None, [qkv_chain, out_chain, up_chain], [qkv_chain, out_chain])
    clock.drain(qkv_chain)

    pairs = width // 128
    half_pairs = pairs // 2
    qkv_pieces = qkv_chain.result
    normed_one, qkv, vecs = clock.tick(
        lambda t: qkv_product(t, x, qkv_pieces), [out_chain], [out_chain, up_chain]
    )
    mixed = clock.tick(
        lambda t: attention(t, qkv, key_bias, slots, 0, half_pairs),
        [out_chain, up_chain, down_chain],
    )
    mixed = clock.tick(
        lambda t: attention(t, qkv, key_bias, slots, half_pairs, pairs, [mixed]),
        [out_chain, up_chain, down_chain],
        [out_chain, down_chain],
    )
    clock.drain(out_chain)
    out_pieces = out_chain.result
    residual, normed_two = clock.tick(
        lambda t: out_product(t, mixed, x, vecs, out_pieces, slots),
        [down_chain],
        [up_chain],
    )
    bias_rows = vecs[BIAS_UP : BIAS_UP + ups].reshape(ups, ndev, own)
    vec_up = bias_rows.transpose(1, 0, 2).reshape(1, hid)
    clock.drain(up_chain)
    up_pieces = up_chain.result
    part = clock.tick(
        lambda t: up_product(t, normed_two, vec_up, up_pieces, 0, half), [], [down_chain]
    )
    act, slope = clock.tick(
        lambda t: up_product(t, normed_two, vec_up, up_pieces, half, groups, part),
        [down_chain],
        [],
    )

    straight = jnp.arange(groups, dtype=jnp.int32)
    size = width // groups
    fits = size % 128 == 0

    def rows_of(t, part):
        if fits:
            return t[half * part : half * (part + 1)]
        return straight[part : part + 1] + 0 * t[:1]

    def placed(a):
        return a if fits else a.reshape(rows, groups, size)[:, tab].reshape(rows, width)

    many = groups if fits else 2

    give = clock.tick(
        lambda t: down_grad(straight[half:] + 0 * t[:half], act, top, groups, "down_grad_give"),
        [down_chain],
    )
    keep = []
    down_rs = Chain(scatter_steps(lay, give, keep))
    keep.append(
        clock.tick(
            lambda t: down_grad(straight[:half] + 0 * t[:half], act, top, groups, "down_grad_keep"),
            [down_rs, down_chain],
            [down_chain],
        )
    )
    clock.drain(down_chain)
    down_pieces = down_chain.result
    clock.tick(None, [], [down_rs])
    grad_hidden, sum_up = clock.tick(
        lambda t: hidden_back(t, top, slope, down_pieces), [down_rs], []
    )

    n2 = placed(normed_two)
    gh = grad_hidden[None]
    give = clock.tick(
        lambda t: weight_grad(rows_of(t, 1), n2, gh, many, "up_grad_give"), [], [down_rs]
    )
    up_swap = Chain(swap_step(lay, give))
    grad_residual, branch, grad_mixed, sums_two = clock.tick(
        lambda t: up_back(t, grad_hidden, residual, top, vecs, up_pieces, out_pieces, slots),
        [up_swap, down_rs],
    )
    mx = placed(mixed)
    give = clock.tick(
        lambda t: weight_grad(rows_of(t, 1), mx, branch[None], many, "out_grad_give"),
        [down_rs],
        [],
    )
    out_swap = Chain(swap_step(lay, give))
    halves = clock.tick(
        lambda t: weight_grad(rows_of(t, 0), n2, gh, many, "up_grad_keep", up_swap.result),
        [out_swap],
        [out_swap, down_rs],
    )
    up_rs = Chain(scatter_rest(lay, *halves))
    halves = clock.tick(
        lambda t: weight_grad(
            rows_of(t, 0), mx, branch[None], many, "out_grad_keep", out_swap.result
        ),
        [up_rs, down_rs],
        [],
    )
    out_rs = Chain(scatter_rest(lay, *halves))
    part = clock.tick(
        lambda t: attention_back(t, qkv, key_bias, grad_mixed, slots, 0, half_pairs),
        [],
        [up_rs, down_rs],
    )
    grads, sums_att = clock.tick(
        lambda t: attention_back(t, qkv, key_bias, grad_mixed, slots, half_pairs, pairs, part),
        [up_rs, out_rs],
    )
    n1 = placed(normed_one)
    give = clock.tick(
        lambda t: weight_grad(rows_of(t, 1), n1, grads, many, "qkv_grad_give"),
        [out_rs, up_rs],
        [out_rs],
    )
    keep = []
    qkv_rs = Chain(scatter_steps(lay, give, keep))
    keep.append(
        clock.tick(
            lambda t: weight_grad(rows_of(t, 0), n1, grads, many, "qkv_grad_keep"),
            [qkv_rs, out_rs],
            [out_rs, up_rs],
        )
    )
    clock.tick(None, [], [qkv_rs])
    grad_patches, sums_one = clock.tick(
        lambda t: qkv_back(t, grads, x, grad_residual, vecs, qkv_pieces, images, slots),
        [qkv_rs, out_rs, up_rs, down_rs],
    )
    eight_sums = jnp.stack(
        [
            sums_one[0],
            sums_one[1],
            sums_att[0],
            sums_att[2],
            sums_two[2],
            sums_two[0],
            sums_two[1],
            sums_two[3],
        ]
    )
    packed = jnp.concatenate(
        [
            eight_sums.reshape(8, ndev, own).transpose(1, 0, 2).reshape(ndev, 8 * own),
            sum_up.reshape(ndev, own_up),
        ],
        axis=1,
    )
    vec_rs = Chain(scatter_small_steps(lay, packed))
    late = [qkv_rs, vec_rs, out_rs, up_rs, down_rs]
    shape = (images, slots, width)
    block_out = None
    for i in range(images // IMG_BLOCK):
        block_out = clock.tick(
            lambda t: down_product(
                t, act, residual, vecs, keep_f, down_pieces, shape, i, i + 1, block_out
            ),
            late,
        )
    clock.drain(*late)
    mine = vec_rs.result
    vecs = [mine[own * i : own * (i + 1)] for i in range(8)]
    return (
        block_out.transpose(1, 0, 2),
        grad_patches.transpose(1, 0, 2),
        vecs[0],
        vecs[1],
        qkv_rs.result,
        vecs[2],
        vecs[3],
        out_rs.result,
        vecs[4],
        vecs[5],
        vecs[6],
        up_rs.result,
        mine[8 * own :],
        down_rs.result,
        vecs[7],
    )


def solution(mesh):
    both = P(AXES)
    mat = P(AXES, None)
    cube = P(AXES, None, None)
    in_specs = (
        cube, mat, both, both, both, mat, both, both, mat, both, both, both, mat, both, mat, both,
        cube,
    )
    out_specs = (
        cube, cube, both, both, mat, both, both, mat, both, both, both, mat, both, mat, both,
    )
    return jax.shard_map(
        functools.partial(local, Layout(mesh)),
        mesh=mesh,
        in_specs=in_specs,
        out_specs=out_specs,
        check_vma=False,
    )
```

```python
import functools

import jax
import jax.numpy as jnp
import numpy as np
from jax import lax
from jax.experimental import pallas as pl
from jax.experimental.pallas import tpu as pltpu
from jax.sharding import PartitionSpec as P

HEADS = 16
EPS = 1e-06
AXES = ("wide", "narrow")
BF = jnp.bfloat16
F32 = jnp.float32
NEG = -1e30
VMEM_LIMIT = 62 << 20
IMG_BLOCK = 8
LN1_GAIN, LN1_BIAS, BIAS_Q, BIAS_V, BIAS_OUT, LN2_GAIN, LN2_BIAS, BIAS_DOWN, BIAS_UP = range(9)
VECS = 16


class Layout:
    def __init__(self, mesh):
        self.wide = mesh.shape["wide"]
        self.narrow = mesh.shape["narrow"]
        self.count = self.wide * self.narrow
        self.chip_bits = (self.wide // 2).bit_length() - 1
        self.line_bits = self.narrow.bit_length() - 1

    def bit_of(self, core, level):
        return level if core == 0 else self.chip_bits - 1 - level

    def flip(self, core, piece):
        total = 0
        for level in range(self.chip_bits):
            if piece >> level & 1:
                total ^= 1 << self.bit_of(core, level)
        return total

    def swap_line(self, bit):
        return [(d, d ^ (1 << bit)) for d in range(self.count)]

    def swap_core(self):
        return [(d, d ^ self.narrow) for d in range(self.count)]

    def swap_chip(self, level):
        pairs = []
        for d in range(self.count):
            place, line = divmod(d, self.narrow)
            chip, core = divmod(place, 2)
            other = chip ^ (1 << self.bit_of(core, level))
            pairs.append((d, (other * 2 + core) * self.narrow + line))
        return pairs

    def shift_line(self, by):
        return [(d, d ^ by) for d in range(self.count)]

    def shift_chip(self, by):
        return [(d, d ^ (2 * self.narrow * by)) for d in range(self.count)]

    def swap_chip_bit(self, bit):
        return [(d, d ^ (2 * self.narrow << bit)) for d in range(self.count)]

    def table(self):
        place = lax.axis_index("wide")
        chip, core = place // 2, place % 2
        half = 1 << self.chip_bits
        even = np.array([self.flip(0, q) for q in range(half)], np.int32)
        odd = np.array([self.flip(1, q) for q in range(half)], np.int32)
        mine = jnp.where(core == 0, even, odd)
        other = jnp.where(core == 0, odd, even)
        return jnp.concatenate(
            [(chip ^ mine) * 2 + core, (chip ^ other) * 2 + (1 - core)]
        ).astype(jnp.int32)


def move(x, pairs):
    return lax.ppermute(x, AXES, pairs)


def gather_steps(lay, x, join=None):
    x = yield from gather_line_steps(lay, x, join)
    parts = [x]
    for level in range(lay.chip_bits):
        x = parts[0] if len(parts) == 1 else jnp.concatenate(parts, 0)
        if level < lay.chip_bits - 1:
            (got,) = yield [(x, lay.swap_chip(level))]
            parts = [x, got]
        else:
            got, other = yield [(x, lay.swap_chip(level)), (x, lay.swap_core())]
    (last,) = yield [(got, lay.swap_core())]
    return [x, got, other, last]


def vector_step(lay, v, join):
    (got,) = yield [(v[None], lay.swap_line(lay.line_bits - 1))]
    join.append((v[None], got))


def gather_line_steps(lay, x, join=None):
    line = lax.axis_index("narrow")
    x = x[None]
    for b in reversed(range(lay.line_bits)):
        (got,) = yield [(x, lay.swap_line(b))]
        if join:
            mine, theirs = join.pop()
            x, got = jnp.concatenate([x, mine], -1), jnp.concatenate([got, theirs], -1)
        bit = (line >> b) & 1
        a, c = x[:, None], got[:, None]
        both = jnp.where(bit == 0, jnp.concatenate([a, c], 1), jnp.concatenate([c, a], 1))
        x = both.reshape(-1, *x.shape[1:])
    return x.reshape(-1, x.shape[-1])


def total(terms, dtype=BF):
    out = terms[0].astype(F32)
    for t in terms[1:]:
        out += t.astype(F32)
    return out.astype(dtype)


def scatter_line_steps(lay, terms, dtype=BF):
    line = lax.axis_index("narrow")
    own, cols = terms[0].shape[0] // lay.narrow, terms[0].shape[1]
    terms = [t.reshape((2,) * lay.line_bits + (own, cols)) for t in terms]
    for b in range(lay.line_bits):
        bit, axis = (line >> b) & 1, lay.line_bits - 1 - b
        give = [lax.dynamic_index_in_dim(t, 1 - bit, axis, False) for t in terms]
        (got,) = yield [(total(give, dtype), lay.swap_line(b))]
        terms = [lax.dynamic_index_in_dim(t, bit, axis, False) for t in terms] + [got]
    return total(terms, F32)


def scatter_steps(lay, give, keep):
    (got,) = yield [(give, lay.swap_core())]
    terms = [keep[0], got]
    for level in reversed(range(lay.chip_bits)):
        size = terms[0].shape[0] // 2
        (got,) = yield [(total([t[size:] for t in terms]), lay.swap_chip(level))]
        terms = [t[:size] for t in terms] + [got]
    return (yield from scatter_line_steps(lay, [total(terms)]))


def swap_step(lay, give):
    (got,) = yield [(give, lay.swap_core())]
    return got


def scatter_rest(lay, low, high):
    terms, give = [low], high
    for level in reversed(range(lay.chip_bits)):
        if give is None:
            size = terms[0].shape[0] // 2
            give = total([t[size:] for t in terms])
            terms = [t[:size] for t in terms]
        (got,) = yield [(give, lay.swap_chip(level))]
        terms, give = terms + [got], None
    return (yield from scatter_line_steps(lay, [total(terms)]))


def direct(x, at, pairs):
    gives = [
        (lax.dynamic_index_in_dim(x, at ^ k, 0, False), pairs(k)) for k in range(1, x.shape[0])
    ]
    got = yield gives
    return total([lax.dynamic_index_in_dim(x, at, 0, False)] + list(got), F32)


def scatter_small_steps(lay, x):
    place, line = lax.axis_index("wide"), lax.axis_index("narrow")
    cols = x.shape[1]
    x = x.reshape(lay.wide // 2, -1, cols)
    x = yield from direct(x, place // 2, lay.shift_chip)
    x = x.reshape(2, lay.narrow, cols)
    x = yield from direct(x, place % 2, lambda k: lay.swap_core())
    return (yield from direct(x, line, lay.shift_line))


class Chain:
    def __init__(self, steps):
        self.steps = steps
        self.want = next(steps)
        self.flying = None
        self.result = None

    def take(self, got):
        self.flying = None
        try:
            self.want = self.steps.send(got)
        except StopIteration as end:
            self.want, self.result = None, end.value


class Clock:
    def __init__(self, tab):
        self.tab = tab
        self.chains = []

    def begin(self, *chains):
        for c in chains:
            if c.want is None or c.flying is not None:
                continue
            operands, self.tab = lax.optimization_barrier(([w[0] for w in c.want], self.tab))
            c.flying = [move(x, w[1]) for x, w in zip(operands, c.want)]

    def tick(self, compute=None, start=(), finish=None):
        self.begin(*start)
        out = compute(self.tab) if compute is not None else ()
        done = [c for c in (start if finish is None else finish) if c.flying is not None]
        self.tab, got, out = lax.optimization_barrier((self.tab, [c.flying for c in done], out))
        for c, g in zip(done, got):
            c.take(g)
        return out

    def drain(self, *chains):
        while any(c.want is not None for c in chains):
            self.tick(None, chains)


def dot_nn(a, b):
    return jnp.dot(a, b, preferred_element_type=F32)


def dot_nt(a, b):
    return lax.dot_general(a, b, (((1,), (1,)), ((), ())), preferred_element_type=F32)


def dot_tn(a, b):
    return lax.dot_general(a, b, (((0,), (0,)), ((), ())), preferred_element_type=F32)


def normalize(r):
    center = r - jnp.mean(r, axis=-1, keepdims=True)
    spread = jnp.mean(center * center, axis=-1, keepdims=True)
    rinv = lax.rsqrt(spread + EPS)
    return center * rinv, rinv


def norm_back(up, gain, n, rinv):
    u = up * gain
    return rinv * (
        u - jnp.mean(u, axis=-1, keepdims=True) - n * jnp.mean(u * n, axis=-1, keepdims=True)
    )


def col_sum(x):
    return jnp.sum(x, axis=0, keepdims=True)


def call(body, outs, grid, in_specs, out_specs, scratch, flops, nbytes, name, trans=0, aliases={}):
    return pl.pallas_call(
        body,
        out_shape=outs,
        grid_spec=pltpu.PrefetchScalarGridSpec(
            num_scalar_prefetch=1,
            grid=grid,
            in_specs=in_specs,
            out_specs=out_specs,
            scratch_shapes=scratch,
        ),
        compiler_params=pltpu.CompilerParams(vmem_limit_bytes=VMEM_LIMIT),
        cost_estimate=pl.CostEstimate(flops=flops, bytes_accessed=nbytes, transcendentals=trans),
        name=name,
        input_output_aliases=aliases,
    )


def full(shape):
    zeros = (0,) * len(shape)
    return pl.BlockSpec(shape, lambda *_: zeros)


def anywhere(count):
    return [pl.BlockSpec(memory_space=pl.ANY)] * count


def sds(shape, dtype):
    return jax.ShapeDtypeStruct(shape, dtype)


def fill_tile(tab, pieces, tile, size):
    per = pieces[0].shape[0] // size
    for a, piece in enumerate(pieces):
        for i in range(per):
            at = pl.multiple_of(tab[a * per + i] * size, size)
            tile[pl.ds(at, size), :] = piece[i * size : (i + 1) * size, :]


def load_copies(tab, pieces, store, sem, size, columns=slice(None)):
    per = pieces[0].shape[0] // size
    copies = []
    for a, piece in enumerate(pieces):
        for i in range(per):
            at = pl.multiple_of(tab[a * per + i] * size, size)
            copies.append(
                pltpu.make_async_copy(
                    piece.at[pl.ds(i * size, size), columns],
                    store.at[pl.ds(at, size)],
                    sem.at[a * per + i],
                )
            )
    return copies


def by_slot(y, o_ref, turn, slots):
    for b in range(IMG_BLOCK):
        turn[:, b, :] = y[slots * b : slots * (b + 1)]
    o_ref[...] = turn[...].astype(BF)


def row_chunk(rows):
    for size in (240, 200, 160, 80, 48, 16):
        if rows % size == 0:
            return size
    return rows


def qkv_product(tab, x, pieces):
    rows, width = x.shape
    tn = width // 2
    count = len(pieces)
    size = pieces[0].shape[0]
    chunk = row_chunk(rows)

    def body(tab_ref, x_ref, *rest):
        piece_refs, vec_refs = rest[:count], rest[count : 2 * count]
        n_ref, o_ref, v_ref, tile, cols = rest[2 * count :]
        j = pl.program_id(0)

        @pl.when(j == 0)
        def _():
            fill_tile(tab_ref, vec_refs, cols, width // tab.shape[0])
            v_ref[...] = cols[...].astype(F32).T[0:VECS]

            @pl.loop(0, rows // chunk)
            def _(i):
                at = pl.ds(pl.multiple_of(i * chunk, chunk), chunk)
                n, _unused = normalize(x_ref[at, :].astype(F32))
                n_ref[at, :] = (n * vec(v_ref, LN1_GAIN) + vec(v_ref, LN1_BIAS)).astype(BF)

        fill_tile(tab_ref, piece_refs, tile, width // tab.shape[0])
        part = vec(v_ref, BIAS_Q), jnp.zeros((1, width), F32), vec(v_ref, BIAS_V)
        bias = jnp.zeros((1, tn), F32)
        for at in range(6):
            lo = at % 2 * tn
            bias = jnp.where(j == at, part[at // 2][:, lo : lo + tn], bias)
        o_ref[...] = (dot_nn(n_ref[...], tile[...]) + bias).astype(BF)

    return call(
        body,
        (sds((rows, width), BF), sds((rows, 3 * width), BF), sds((VECS, width), F32)),
        (6,),
        [full((rows, width))]
        + [pl.BlockSpec((size, tn), lambda j, t: (0, j))] * count
        + [pl.BlockSpec((size, 128), lambda j, t: (0, 6 * tn // 128))] * count,
        (
            full((rows, width)),
            pl.BlockSpec((rows, tn), lambda j, t: (0, j)),
            full((VECS, width)),
        ),
        [pltpu.VMEM((width, tn), BF), pltpu.VMEM((width, 128), BF)],
        6 * rows * width * width,
        2 * (5 * rows * width + 3 * width * width),
        "qkv_product",
    )(tab, x, *pieces, *pieces)


def two_heads(x, lane):
    return jnp.concatenate([jnp.where(lane < 64, x, 0.0), jnp.where(lane < 64, 0.0, x)], 0).astype(
        BF
    )


def half_max(s, low):
    a = jnp.max(jnp.where(low, s, NEG), axis=-1, keepdims=True)
    b = jnp.max(jnp.where(low, NEG, s), axis=-1, keepdims=True)
    return jnp.where(low, a, b)


def half_sum(s, ones):
    high = s.astype(BF)
    rest = (s - high.astype(F32)).astype(BF)
    return dot_nn(high, ones) + dot_nn(rest, ones)


def softmax_pair(s, low, ones):
    e = jnp.exp(s - half_max(s, low))
    return e / half_sum(e, ones)


def head_ones():
    row = lax.broadcasted_iota(jnp.int32, (128, 128), 0) < 64
    col = lax.broadcasted_iota(jnp.int32, (128, 128), 1) < 64
    return jnp.where(row == col, 1.0, 0.0).astype(BF)


def attention(tab, qkv, key_bias, slots, first, last, before=()):
    rows, three = qkv.shape
    width = three // 3
    pairs = width // 128
    blk = IMG_BLOCK * slots
    pad = -(-slots // 8) * 8
    scale = float(64**-0.5)

    def body(tab_ref, q_ref, k_ref, v_ref, kb_ref, *rest):
        o_ref, qf, kf, vf, of, sf = rest[len(before) :]
        for ref, src in ((qf, q_ref), (kf, k_ref), (vf, v_ref)):
            ref[0:blk, :] = src[...].astype(F32)
            ref[blk : blk + 16, :] = jnp.zeros((16, 128), F32)
        lane = lax.broadcasted_iota(jnp.int32, (64, 128), 1)
        low = lax.broadcasted_iota(jnp.int32, (pad, 128), 1) < 64
        ones = head_ones()
        for b in range(IMG_BLOCK):
            at = slots * b
            kk = two_heads(kf[at : at + 64, :], lane)
            q = qf[at : at + pad, :].astype(BF)
            sf[pad * b : pad * (b + 1), :] = dot_nt(q, kk) * scale + kb_ref[b]
        low = lax.broadcasted_iota(jnp.int32, (pad * IMG_BLOCK, 128), 1) < 64
        p = softmax_pair(sf[...], low, ones)
        outs = []
        for b in range(IMG_BLOCK):
            at = slots * b
            vv = two_heads(vf[at : at + 64, :], lane)
            outs.append(dot_nn(p[pad * b : pad * (b + 1)].astype(BF), vv))
        for b in range(IMG_BLOCK):
            at = slots * b
            of[at : at + pad, :] = outs[b]
        o_ref[...] = of[0:blk, :].astype(BF)

    return call(
        body,
        sds((rows, width), BF),
        (last - first, rows // blk),
        [
            pl.BlockSpec((blk, 128), lambda h, i, t: (i, h + first)),
            pl.BlockSpec((blk, 128), lambda h, i, t: (i, h + first + pairs)),
            pl.BlockSpec((blk, 128), lambda h, i, t: (i, h + first + 2 * pairs)),
            pl.BlockSpec((IMG_BLOCK, 1, 128), lambda h, i, t: (i, 0, 0)),
        ]
        + anywhere(len(before)),
        pl.BlockSpec((blk, 128), lambda h, i, t: (i, h + first)),
        [pltpu.VMEM((blk + 16, 128), F32)] * 4 + [pltpu.VMEM((pad * IMG_BLOCK, 128), F32)],
        8 * rows * 128 * width * 2 * (last - first) // pairs,
        2 * 4 * rows * width * (last - first) // pairs,
        "attention",
        aliases={5: 0} if before else {},
    )(tab, qkv, qkv, qkv, key_bias, *before)


def attention_back(tab, qkv, key_bias, grad_mixed, slots, first, last, before=()):
    rows, three = qkv.shape
    width = three // 3
    pairs = width // 128
    blk = IMG_BLOCK * slots
    pad = -(-slots // 8) * 8
    tall = pad * IMG_BLOCK
    scale = float(64**-0.5)

    def body(tab_ref, q_ref, k_ref, v_ref, kb_ref, g_ref, *rest):
        o_ref, s_ref, qf, kf, vf, gf, dqf, dkf, dvf, sf, pf = rest[len(before) :]
        for ref, src in ((qf, q_ref), (kf, k_ref), (vf, v_ref), (gf, g_ref)):
            ref[0:blk, :] = src[...].astype(F32)
            ref[blk : blk + 16, :] = jnp.zeros((16, 128), F32)
        lane = lax.broadcasted_iota(jnp.int32, (64, 128), 1)
        low = lax.broadcasted_iota(jnp.int32, (pad, 128), 1) < 64
        real = lax.broadcasted_iota(jnp.int32, (pad, 128), 0) < slots
        ones = head_ones()
        kks, qs, gs = [], [], []
        for b in range(IMG_BLOCK):
            at = slots * b
            kks.append(two_heads(kf[at : at + 64, :], lane))
            vv = two_heads(vf[at : at + 64, :], lane)
            qs.append(jnp.where(real, qf[at : at + pad, :], 0.0).astype(BF))
            gs.append(jnp.where(real, gf[at : at + pad, :], 0.0).astype(BF))
            sf[pad * b : pad * (b + 1), :] = dot_nt(qs[b], kks[b]) * scale + kb_ref[b]
            pf[pad * b : pad * (b + 1), :] = dot_nt(gs[b], vv)
        p = softmax_pair(sf[...], lax.broadcasted_iota(jnp.int32, (tall, 128), 1) < 64, ones)
        dp = pf[...]
        ds = p * (dp - half_sum(p * dp, ones))
        res = []
        for b in range(IMG_BLOCK):
            d = ds[pad * b : pad * (b + 1)].astype(BF)
            w = p[pad * b : pad * (b + 1)].astype(BF)
            res.append((dot_nn(d, kks[b]), dot_tn(d, qs[b]), dot_tn(w, gs[b])))
        for b in range(IMG_BLOCK):
            at = slots * b
            dq, dk, dv = res[b]
            dqf[at : at + pad, :] = dq * scale
            dkf[at : at + pad, :] = jnp.where(low, dk[0:pad], dk[64 : 64 + pad]) * scale
            dvf[at : at + pad, :] = jnp.where(low, dv[0:pad], dv[64 : 64 + pad])

        @pl.when(pl.program_id(1) == 0)
        def _():
            s_ref[...] = jnp.zeros_like(s_ref)

        for at, ref in enumerate((dqf, dkf, dvf)):
            rounded = ref[0:blk, :].astype(BF)
            o_ref[at] = rounded
            if at != 1:
                s_ref[at : at + 1, :] += col_sum(rounded.astype(F32))

    def pair(skip):
        return pl.BlockSpec((blk, 128), lambda h, i, t: (i, h + first + skip))

    return call(
        body,
        (sds((3, rows, width), BF), sds((8, width), F32)),
        (last - first, rows // blk),
        [
            pair(0),
            pair(pairs),
            pair(2 * pairs),
            pl.BlockSpec((IMG_BLOCK, 1, 128), lambda h, i, t: (i, 0, 0)),
            pair(0),
        ]
        + anywhere(len(before)),
        (
            pl.BlockSpec((3, blk, 128), lambda h, i, t: (0, i, h + first)),
            pl.BlockSpec((8, 128), lambda h, i, t: (0, h + first)),
        ),
        [pltpu.VMEM((blk + 16, 128), F32)] * 7 + [pltpu.VMEM((tall, 128), F32)] * 2,
        20 * rows * 128 * width * 2 * (last - first) // pairs,
        2 * 7 * rows * width * (last - first) // pairs,
        "attention_back",
        aliases={6: 0, 7: 1} if before else {},
    )(tab, qkv, qkv, qkv, key_bias, grad_mixed, *before)


def vec(ref, at):
    return ref[at : at + 1, :]


def out_product(tab, mixed, x, vecs, pieces, slots):
    rows, width = mixed.shape
    blk = IMG_BLOCK * slots
    count = len(pieces)

    def body(tab_ref, m_ref, x_ref, v_ref, *rest):
        piece_refs, (r_ref, n_ref, store, sem) = rest[:count], rest[count:]

        @pl.when(pl.program_id(0) == 0)
        def _():
            copies = load_copies(tab_ref, piece_refs, store, sem, width // tab.shape[0])
            for c in copies:
                c.start()
            for c in copies:
                c.wait()

        r = x_ref[...].astype(F32) + dot_nn(m_ref[...], store[...]) + vec(v_ref, BIAS_OUT)
        r_ref[...] = r
        n, _unused = normalize(r)
        n_ref[...] = (n * vec(v_ref, LN2_GAIN) + vec(v_ref, LN2_BIAS)).astype(BF)

    spec = pl.BlockSpec((blk, width), lambda i, t: (i, 0))
    return call(
        body,
        (sds((rows, width), F32), sds((rows, width), BF)),
        (rows // blk,),
        [spec, spec, full((VECS, width))] + anywhere(count),
        (spec, spec),
        [pltpu.VMEM((width, width), BF), pltpu.SemaphoreType.DMA((tab.shape[0],))],
        2 * rows * width * width,
        10 * rows * width + 2 * width * width,
        "out_product",
    )(tab, mixed, x, vecs, *pieces)


def up_product(tab, n2, bias_up, pieces, first, last, before=()):
    rows, width = n2.shape
    hid = pieces[0].shape[1]
    count = len(pieces)
    groups = tab.shape[0]
    tn = hid // groups
    size = pieces[0].shape[0]

    def body(tab_ref, n_ref, c_ref, *rest):
        piece_refs, (a_ref, d_ref, tile) = rest[:count], rest[count + len(before) :]
        fill_tile(tab_ref, piece_refs, tile, width // groups)
        u = dot_nn(n_ref[...], tile[...]) + c_ref[...]
        phi = 0.5 + 0.5 * lax.erf(u * np.float32(0.5**0.5))
        a_ref[...] = (u * phi).astype(BF)
        slope = phi + u * jnp.exp(-0.5 * u * u) * np.float32((2 * np.pi) ** -0.5)
        d_ref[...] = slope.astype(BF)

    spec = pl.BlockSpec((rows, tn), lambda p, t: (0, p + first))
    return call(
        body,
        (sds((rows, hid), BF), sds((rows, hid), BF)),
        (last - first,),
        [full((rows, width)), pl.BlockSpec((1, tn), lambda p, t: (0, t[p + first]))]
        + [pl.BlockSpec((size, tn), lambda p, t: (0, t[p + first]))] * count
        + anywhere(len(before)),
        (spec, spec),
        [pltpu.VMEM((width, tn), BF)],
        2 * rows * width * hid + 30 * rows * hid,
        2 * (rows * width + 2 * rows * hid + width * hid),
        "up_product",
        2 * rows * hid,
        {3 + count: 0, 4 + count: 1} if before else {},
    )(tab, n2, bias_up, *pieces, *before)


def down_product(tab, act, residual, vecs, keep, pieces, shape, first, last, before=None):
    images, slots, width = shape
    rows, hid = act.shape
    blk = IMG_BLOCK * slots
    count = len(pieces)
    size = pieces[0].shape[0]

    def body(tab_ref, a_ref, r_ref, v_ref, k_ref, *rest):
        piece_refs, (o_ref, store, turn, sem) = rest[:count], rest[-4:]

        def dma(p):
            return pltpu.make_async_copy(
                piece_refs[p], store.at[pl.ds(p * size, size)], sem.at[p]
            )

        @pl.when(pl.program_id(0) == 0)
        def _():
            for p in range(count):
                dma(p).start()
            if last - first > 1:
                for p in range(count):
                    dma(p).wait()

        y = r_ref[...] + vec(v_ref, BIAS_DOWN)
        for p in range(count):
            if last - first == 1:
                dma(p).wait()
            part = slice(p * size, (p + 1) * size)
            y += dot_nn(a_ref[:, part], store[part, :])
        y = jnp.where(k_ref[...] > 0.0, y, 0.0)
        by_slot(y, o_ref, turn, slots)

    share = blk * (last - first)
    more = [] if before is None else [before]
    return call(
        body,
        sds((slots, images, width), BF),
        (last - first,),
        [
            pl.BlockSpec((blk, hid), lambda i, t: (i + first, 0)),
            pl.BlockSpec((blk, width), lambda i, t: (i + first, 0)),
            full((VECS, width)),
            pl.BlockSpec((blk, 1), lambda i, t: (i + first, 0)),
        ]
        + anywhere(count + len(more)),
        pl.BlockSpec((slots, IMG_BLOCK, width), lambda i, t: (0, i + first, 0)),
        [
            pltpu.VMEM((hid, width), BF),
            pltpu.VMEM((slots, IMG_BLOCK, width), F32),
            pltpu.SemaphoreType.DMA((count,)),
        ],
        2 * share * width * hid,
        2 * (share * hid + 3 * share * width + width * hid),
        "down_product",
        aliases={} if before is None else {5 + count: 0},
    )(tab, act, residual, vecs, keep, *pieces, *more)


def hidden_back(tab, top, slope, pieces):
    rows, width = top.shape
    hid = slope.shape[1]
    count = len(pieces)
    groups = tab.shape[0]
    tn = hid // groups
    per = groups // count

    def body(tab_ref, t_ref, d_ref, *rest):
        piece_refs, (o_ref, s_ref, store, sem) = rest[:count], rest[count:]
        p = pl.program_id(0)
        copies = [
            pltpu.make_async_copy(
                piece_refs[g // per].at[pl.ds(g % per * tn, tn)], store.at[g], sem.at[g]
            )
            for g in range(groups)
        ]

        @pl.when(p == 0)
        def _():
            for c in copies:
                c.start()

        pltpu.make_async_copy(store.at[p], store.at[p], sem.at[p]).wait()
        g = (dot_nt(t_ref[...], store[p]) * d_ref[...].astype(F32)).astype(BF)
        o_ref[...] = g
        s_ref[...] = col_sum(g.astype(F32))

    spec = pl.BlockSpec((rows, tn), lambda p, t: (0, p))
    return call(
        body,
        (sds((rows, hid), BF), sds((1, hid), F32)),
        (groups,),
        [full((rows, width)), spec] + anywhere(count),
        (
            pl.BlockSpec((rows, tn), lambda p, t: (0, t[p])),
            pl.BlockSpec((1, tn), lambda p, t: (0, t[p])),
        ),
        [pltpu.VMEM((groups, tn, width), BF), pltpu.SemaphoreType.DMA((groups,))],
        2 * rows * width * hid,
        2 * (rows * width + 2 * rows * hid + width * hid),
        "hidden_back",
    )(tab, top, slope, *pieces)


def up_back(tab, grad_hidden, residual, top, vecs, pieces, out_pieces, slots):
    rows, hid = grad_hidden.shape
    width = residual.shape[1]
    count = len(pieces)
    groups = tab.shape[0]
    blk = IMG_BLOCK * slots

    def body(tab_ref, h_ref, r_ref, t_ref, v_ref, *rest):
        piece_refs, out_refs = rest[:count], rest[count : 2 * count]
        gr_ref, gb_ref, gm_ref, s_ref, up_store, store, up_sem, sem = rest[2 * count :]

        @pl.when(pl.program_id(0) == 0)
        def _():
            ups = load_copies(tab_ref, piece_refs, up_store, up_sem, width // groups)
            outs = load_copies(tab_ref, out_refs, store, sem, width // groups)
            for c in ups + outs:
                c.start()
            s_ref[...] = jnp.zeros_like(s_ref)
            for c in ups + outs:
                c.wait()

        up = dot_nt(h_ref[...], up_store[...])
        n, rinv = normalize(r_ref[...])
        top_rows = t_ref[...].astype(F32)
        grad = top_rows + norm_back(up, vec(v_ref, LN2_GAIN), n, rinv)
        branch = grad.astype(BF)
        gr_ref[...] = grad
        gb_ref[...] = branch
        gm_ref[...] = dot_nt(branch, store[...]).astype(BF)
        s_ref[0:1, :] += col_sum(up * n)
        s_ref[1:2, :] += col_sum(up)
        s_ref[2:3, :] += col_sum(branch.astype(F32))
        s_ref[3:4, :] += col_sum(top_rows)

    spec = pl.BlockSpec((blk, width), lambda i, t: (i, 0))
    return call(
        body,
        (
            sds((rows, width), F32),
            sds((rows, width), BF),
            sds((rows, width), BF),
            sds((8, width), F32),
        ),
        (rows // blk,),
        [pl.BlockSpec((blk, hid), lambda i, t: (i, 0)), spec, spec, full((VECS, width))]
        + anywhere(2 * count),
        (spec, spec, spec, full((8, width))),
        [
            pltpu.VMEM((width, hid), BF),
            pltpu.VMEM((width, width), BF),
            pltpu.SemaphoreType.DMA((groups,)),
            pltpu.SemaphoreType.DMA((groups,)),
        ],
        2 * rows * width * (hid + width),
        2 * (rows * hid + 8 * rows * width + width * hid),
        "up_back",
    )(tab, grad_hidden, residual, top, vecs, *pieces, *out_pieces)


def qkv_back(tab, grads, x, grad_residual, vecs, pieces, images, slots):
    _three, rows, width = grads.shape
    blk = IMG_BLOCK * slots
    count = len(pieces)
    groups = tab.shape[0]

    def body(tab_ref, d_ref, x_ref, r_ref, v_ref, *rest):
        piece_refs, (o_ref, s_ref, store, turn, sem) = rest[:count], rest[count:]

        @pl.when(pl.program_id(0) == 0)
        def _():
            copies = load_copies(
                tab_ref, piece_refs, store, sem, width // groups, pl.ds(0, 3 * width)
            )
            for c in copies:
                c.start()
            s_ref[...] = jnp.zeros_like(s_ref)
            for c in copies:
                c.wait()

        up = dot_nt(d_ref[0], store[:, 0:width])
        up += dot_nt(d_ref[1], store[:, width : 2 * width])
        up += dot_nt(d_ref[2], store[:, 2 * width :])
        n, rinv = normalize(x_ref[...].astype(F32))
        y = r_ref[...] + norm_back(up, vec(v_ref, LN1_GAIN), n, rinv)
        s_ref[0:1, :] += col_sum(up * n)
        s_ref[1:2, :] += col_sum(up)
        by_slot(y, o_ref, turn, slots)

    spec = pl.BlockSpec((blk, width), lambda i, t: (i, 0))
    return call(
        body,
        (sds((slots, images, width), BF), sds((8, width), F32)),
        (rows // blk,),
        [pl.BlockSpec((3, blk, width), lambda i, t: (0, i, 0)), spec, spec, full((VECS, width))]
        + anywhere(count),
        (pl.BlockSpec((slots, IMG_BLOCK, width), lambda i, t: (0, i, 0)), full((8, width))),
        [
            pltpu.VMEM((width, 3 * width), BF),
            pltpu.VMEM((slots, IMG_BLOCK, width), F32),
            pltpu.SemaphoreType.DMA((groups,)),
        ],
        6 * rows * width * width,
        2 * (3 * rows * width + 4 * rows * width + 3 * width * width),
        "qkv_back",
    )(tab, grads, x, grad_residual, vecs, *pieces)


def weight_grad(order, x, g, pieces_of, name, got=None):
    parts, rows, width = g.shape
    count = order.shape[0]
    size = x.shape[1] // pieces_of
    tall = count * size
    tn = min(width, 1024)
    per = width // tn
    more = [] if got is None else [got]

    def body(tab_ref, *rest):
        x_refs, g_ref, (*o_refs, xs) = rest[:count], rest[count], rest[count + 1 + len(more) :]

        @pl.when(pl.program_id(0) == 0)
        def _():
            for p in range(count):
                xs[:, size * p : size * (p + 1)] = x_refs[p][...]

        y = dot_tn(xs[...], g_ref[0])
        if got is None:
            o_refs[0][...] = y.astype(BF)
        else:
            y += rest[count + 1][...].astype(F32)
            o_refs[0][...] = y[: tall // 2].astype(BF)
            o_refs[1][...] = y[tall // 2 :].astype(BF)

    def column(p):
        return lambda j, t: (0, t[p])

    def part(height):
        return pl.BlockSpec((height, tn), lambda j, t: (0, j))

    if got is None:
        outs, out_specs = sds((tall, parts * width), BF), part(tall)
    else:
        outs, out_specs = (sds((tall // 2, parts * width), BF),) * 2, (part(tall // 2),) * 2
    return call(
        body,
        outs,
        (parts * per,),
        [pl.BlockSpec((rows, size), column(p)) for p in range(count)]
        + [pl.BlockSpec((1, rows, tn), lambda j, t: (j // per, 0, j % per))]
        + [part(tall)] * len(more),
        out_specs,
        [pltpu.VMEM((rows, tall), BF)],
        2 * rows * tall * parts * width,
        2 * (rows * tall + parts * rows * width + tall * parts * width),
        name,
    )(order, *([x] * count), g, *more)


def down_grad(order, act, top, pieces_of, name):
    rows, hid = act.shape
    width = top.shape[1]
    count = order.shape[0]
    size = hid // pieces_of

    def body(tab_ref, a_ref, t_ref, o_ref):
        o_ref[...] = dot_tn(a_ref[...], t_ref[...]).astype(BF)

    return call(
        body,
        sds((count * size, width), BF),
        (count,),
        [pl.BlockSpec((rows, size), lambda p, t: (0, t[p])), full((rows, width))],
        pl.BlockSpec((size, width), lambda p, t: (p, 0)),
        [],
        2 * rows * count * size * width,
        2 * (rows * count * size + rows * width + count * size * width),
        name,
    )(order, act, top)


def kept_slots(keep_order, keep_count):
    slot_ids = lax.iota(jnp.int32, keep_order.shape[-1])
    listed = keep_order[:, :, None] == slot_ids[None, None, :]
    within = slot_ids[None, :] < keep_count[:, None]
    return jnp.any(jnp.logical_and(listed, within[:, :, None]), axis=1)


def local(lay, *args):
    (
        patches,
        keep_order,
        keep_count,
        ln1_gain,
        ln1_bias,
        w_qkv,
        bias_q,
        bias_v,
        w_out,
        bias_out,
        ln2_gain,
        ln2_bias,
        w_up,
        bias_up,
        w_down,
        bias_down,
        cotangent,
    ) = args
    images, slots, width = patches.shape
    rows = images * slots
    ndev = lay.count
    own = width // ndev
    own_up = bias_up.shape[0]
    hid = own_up * ndev

    tab = lay.table()
    groups = lay.wide
    half = groups // 2
    clock = Clock(tab)

    ups = own_up // own
    vectors = [ln1_gain, ln1_bias, bias_q, bias_v, bias_out, ln2_gain, ln2_bias, bias_down]
    columns = jnp.concatenate([jnp.stack(vectors), bias_up.reshape(ups, own)])
    columns = jnp.pad(columns.T, ((0, 0), (0, 128 - 8 - ups)))
    join = []
    qkv_chain = Chain(gather_steps(lay, w_qkv, join))
    vec_chain = Chain(vector_step(lay, columns, join))
    out_chain = Chain(gather_steps(lay, w_out))
    up_chain = Chain(gather_steps(lay, w_up))
    down_chain = Chain(gather_steps(lay, w_down))

    def masks(_tab):
        keep_mask = kept_slots(keep_order, keep_count)
        keep_rows = keep_mask.reshape(rows, 1)
        pad_keys = jnp.pad(
            jnp.where(keep_mask, 0.0, NEG), ((0, 0), (0, 64 - slots)), constant_values=NEG
        )
        key_bias = jnp.concatenate([pad_keys, pad_keys], 1).reshape(images, 1, 128)
        return keep_rows.astype(F32), key_bias

    def after(t, a):
        return lax.optimization_barrier((a, t))[0]

    keep_f, key_bias = clock.tick(masks, [qkv_chain, vec_chain], [vec_chain, qkv_chain])
    clock.tick(None, [qkv_chain])
    for _ in range(lay.chip_bits + lay.line_bits - 4):
        clock.tick(None, [qkv_chain])
    x = clock.tick(
        lambda t: after(t, patches).reshape(rows, width),
        [qkv_chain, out_chain, up_chain],
        [qkv_chain, out_chain],
    )
    top = clock.tick(
        lambda t: jnp.where(
            keep_f > 0, after(t, cotangent).reshape(rows, width), jnp.zeros((), BF)
        ),
        [qkv_chain, out_chain],
        [qkv_chain, out_chain, up_chain],
    )
    clock.tick(None, [qkv_chain, out_chain, up_chain], [qkv_chain, out_chain])
    clock.drain(qkv_chain)

    pairs = width // 128
    half_pairs = pairs // 2
    qkv_pieces = qkv_chain.result
    normed_one, qkv, vecs = clock.tick(
        lambda t: qkv_product(t, x, qkv_pieces), [out_chain], [out_chain, up_chain]
    )
    mixed = clock.tick(
        lambda t: attention(t, qkv, key_bias, slots, 0, half_pairs),
        [out_chain, up_chain, down_chain],
    )
    mixed = clock.tick(
        lambda t: attention(t, qkv, key_bias, slots, half_pairs, pairs, [mixed]),
        [out_chain, up_chain, down_chain],
        [out_chain, down_chain],
    )
    clock.drain(out_chain)
    out_pieces = out_chain.result
    residual, normed_two = clock.tick(
        lambda t: out_product(t, mixed, x, vecs, out_pieces, slots),
        [down_chain],
        [up_chain],
    )
    bias_rows = vecs[BIAS_UP : BIAS_UP + ups].reshape(ups, ndev, own)
    vec_up = bias_rows.transpose(1, 0, 2).reshape(1, hid)
    clock.drain(up_chain)
    up_pieces = up_chain.result
    part = clock.tick(
        lambda t: up_product(t, normed_two, vec_up, up_pieces, 0, half), [], [down_chain]
    )
    act, slope = clock.tick(
        lambda t: up_product(t, normed_two, vec_up, up_pieces, half, groups, part),
        [down_chain],
        [],
    )

    straight = jnp.arange(groups, dtype=jnp.int32)
    size = width // groups
    fits = size % 128 == 0

    def rows_of(t, part):
        if fits:
            return t[half * part : half * (part + 1)]
        return straight[part : part + 1] + 0 * t[:1]

    def placed(a):
        return a if fits else a.reshape(rows, groups, size)[:, tab].reshape(rows, width)

    many = groups if fits else 2

    give = clock.tick(
        lambda t: down_grad(straight[half:] + 0 * t[:half], act, top, groups, "down_grad_give"),
        [down_chain],
    )
    keep = []
    down_rs = Chain(scatter_steps(lay, give, keep))
    keep.append(
        clock.tick(
            lambda t: down_grad(straight[:half] + 0 * t[:half], act, top, groups, "down_grad_keep"),
            [down_rs, down_chain],
            [down_chain],
        )
    )
    clock.drain(down_chain)
    down_pieces = down_chain.result
    clock.tick(None, [], [down_rs])
    grad_hidden, sum_up = clock.tick(
        lambda t: hidden_back(t, top, slope, down_pieces), [down_rs], []
    )

    n2 = placed(normed_two)
    gh = grad_hidden[None]
    give = clock.tick(
        lambda t: weight_grad(rows_of(t, 1), n2, gh, many, "up_grad_give"), [], [down_rs]
    )
    up_swap = Chain(swap_step(lay, give))
    grad_residual, branch, grad_mixed, sums_two = clock.tick(
        lambda t: up_back(t, grad_hidden, residual, top, vecs, up_pieces, out_pieces, slots),
        [up_swap, down_rs],
    )
    mx = placed(mixed)
    give = clock.tick(
        lambda t: weight_grad(rows_of(t, 1), mx, branch[None], many, "out_grad_give"),
        [down_rs],
        [],
    )
    out_swap = Chain(swap_step(lay, give))
    halves = clock.tick(
        lambda t: weight_grad(rows_of(t, 0), n2, gh, many, "up_grad_keep", up_swap.result),
        [out_swap],
        [out_swap, down_rs],
    )
    up_rs = Chain(scatter_rest(lay, *halves))
    halves = clock.tick(
        lambda t: weight_grad(
            rows_of(t, 0), mx, branch[None], many, "out_grad_keep", out_swap.result
        ),
        [up_rs, down_rs],
        [],
    )
    out_rs = Chain(scatter_rest(lay, *halves))
    part = clock.tick(
        lambda t: attention_back(t, qkv, key_bias, grad_mixed, slots, 0, half_pairs),
        [],
        [up_rs, down_rs],
    )
    grads, sums_att = clock.tick(
        lambda t: attention_back(t, qkv, key_bias, grad_mixed, slots, half_pairs, pairs, part),
        [up_rs, out_rs],
    )
    n1 = placed(normed_one)
    give = clock.tick(
        lambda t: weight_grad(rows_of(t, 1), n1, grads, many, "qkv_grad_give"),
        [out_rs, up_rs],
        [out_rs],
    )
    keep = []
    qkv_rs = Chain(scatter_steps(lay, give, keep))
    keep.append(
        clock.tick(
            lambda t: weight_grad(rows_of(t, 0), n1, grads, many, "qkv_grad_keep"),
            [qkv_rs, out_rs],
            [out_rs, up_rs],
        )
    )
    clock.tick(None, [], [qkv_rs])
    grad_patches, sums_one = clock.tick(
        lambda t: qkv_back(t, grads, x, grad_residual, vecs, qkv_pieces, images, slots),
        [qkv_rs, out_rs, up_rs, down_rs],
    )
    eight_sums = jnp.stack(
        [
            sums_one[0],
            sums_one[1],
            sums_att[0],
            sums_att[2],
            sums_two[2],
            sums_two[0],
            sums_two[1],
            sums_two[3],
        ]
    )
    packed = jnp.concatenate(
        [
            eight_sums.reshape(8, ndev, own).transpose(1, 0, 2).reshape(ndev, 8 * own),
            sum_up.reshape(ndev, own_up),
        ],
        axis=1,
    )
    vec_rs = Chain(scatter_small_steps(lay, packed))
    late = [qkv_rs, vec_rs, out_rs, up_rs, down_rs]
    shape = (images, slots, width)
    block_out = None
    for i in range(images // IMG_BLOCK):
        block_out = clock.tick(
            lambda t: down_product(
                t, act, residual, vecs, keep_f, down_pieces, shape, i, i + 1, block_out
            ),
            late,
        )
    clock.drain(*late)
    mine = vec_rs.result
    vecs = [mine[own * i : own * (i + 1)] for i in range(8)]
    return (
        block_out.transpose(1, 0, 2),
        grad_patches.transpose(1, 0, 2),
        vecs[0],
        vecs[1],
        qkv_rs.result,
        vecs[2],
        vecs[3],
        out_rs.result,
        vecs[4],
        vecs[5],
        vecs[6],
        up_rs.result,
        mine[8 * own :],
        down_rs.result,
        vecs[7],
    )


def solution(mesh):
    both = P(AXES)
    mat = P(AXES, None)
    cube = P(AXES, None, None)
    in_specs = (
        cube, mat, both, both, both, mat, both, both, mat, both, both, both, mat, both, mat, both,
        cube,
    )
    out_specs = (
        cube, cube, both, both, mat, both, both, mat, both, both, both, mat, both, mat, both,
    )
    return jax.shard_map(
        functools.partial(local, Layout(mesh)),
        mesh=mesh,
        in_specs=in_specs,
        out_specs=out_specs,
        check_vma=False,
    )
```
